32 devices in a mesh: dp: 16 (over z, y, core), tensor: 2 (over x).
Axes of the slice: x: 2, y: 2, z: 4, core: 2. Of those that a mesh axis runs over, the one named last changes fastest.
Arguments:
- inputs: bfloat16 [16, 1024, 768], P('dp', 'tensor'), may hold values from -6 to 6
- lengths: int32 [16], P('dp'), may hold values from 256 to 1024, as said below
- w_qkv: bfloat16 [3, 768, 768], P(None, 'dp', 'tensor'), may hold values from -0.21875 to 0.21875
- b_qv: float32 [2, 768], P(None, 'tensor'), may hold values from -2 to 2
- w_out: bfloat16 [768, 768], P('tensor', 'dp'), may hold values from -1.75 to 1.75
- b_out: float32 [768], replicated, may hold values from -2 to 2
- ln1_gain: float32 [768], replicated, may hold values from 0.5 to 1.5
- ln1_bias: float32 [768], replicated, may hold values from -2 to 2
- w_in: bfloat16 [768, 3072], P('dp', 'tensor'), may hold values from -0.21875 to 0.21875
- b_in: float32 [3072], P('tensor'), may hold values from -2 to 2
- w_hid: bfloat16 [3072, 768], P('tensor', 'dp'), may hold values from -0.109375 to 0.109375
- b_hid: float32 [768], replicated, may hold values from -2 to 2
- ln2_gain: float32 [768], replicated, may hold values from 0.5 to 1.5
- ln2_bias: float32 [768], replicated, may hold values from -2 to 2
- mask_logits: float32 [12, 1024, 1024], P('tensor', 'dp'), may hold values from -6 to 6
- noise: float32 [12, 1024, 1024], P('tensor', 'dp'), may hold values from -6 to 6
- cotangent: float32 [16, 1024, 768], P('dp', 'tensor'), may hold values from -6 to 6
Outputs:
- outputs: bfloat16 [16, 1024, 768], P('dp', 'tensor')
- input_grad: float32 [16, 1024, 768], P('dp', 'tensor')
- grad_w_qkv: float32 [3, 768, 768], P(None, 'dp', 'tensor')
- grad_b_qv: float32 [2, 768], P(None, 'tensor')
- grad_w_out: float32 [768, 768], P('tensor', 'dp')
- grad_b_out: float32 [768], replicated
- grad_ln1_gain: float32 [768], replicated
- grad_ln1_bias: float32 [768], replicated
- grad_w_in: float32 [768, 3072], P('dp', 'tensor')
- grad_b_in: float32 [3072], P('tensor')
- grad_w_hid: float32 [3072, 768], P('tensor', 'dp')
- grad_b_hid: float32 [768], replicated
- grad_ln2_gain: float32 [768], replicated
- grad_ln2_bias: float32 [768], replicated
- grad_mask_logits: float32 [12, 1024, 1024], P('tensor', 'dp')
The draws below stay inside these ranges and needn't reach their ends.
Inputs may be any that keep to these rules, and one draw needn't show every extreme that they name: `lengths`: some sequence fills all 1024 slots and some has exactly 256 valid tokens.
All inputs are finite; a program needn't handle non-finite values.
Results may differ from the reference program's by a relative error of at most 0.014.
Values may be sent and summed in bfloat16 or wider, within the bound.
A program may use at most 192 MiB of HBM per device.

```python
import math
from functools import partial
import jax
import jax.numpy as jnp
from jax import lax

D = 768
HEADS = 12
HEAD_WIDTH = 64
FF = 3072
SLOT = 1024
SEQS = 16


def draw_lengths(key, part):
    first_key = jax.random.fold_in(key, 11)
    second_key = jax.random.fold_in(key, 23)
    third_key = jax.random.fold_in(key, 37)
    drawn = jax.random.randint(first_key, (SEQS,), SLOT // 4, SLOT + 1)
    longest = jax.random.randint(second_key, (), 0, SEQS)
    offset = jax.random.randint(third_key, (), 1, SEQS)
    shortest = (longest + offset) % SEQS
    drawn = drawn.at[longest].set(SLOT)
    drawn = drawn.at[shortest].set(SLOT // 4)
    return drawn.astype(jnp.int32)


def spiked(values, rng, source, target, parts, factor):
    def block_of(dim):
        return (jnp.arange(values.shape[dim]) // (values.shape[dim] // parts)).reshape((-1,) + (1,) * (values.ndim - 1 - dim))

    one_side = jax.random.permutation(rng, parts)[block_of(target)]
    far = (block_of(target) + parts // 2) % parts
    return jnp.where((block_of(source) == one_side) | (block_of(source) == far), factor * values, values)


def shard_levels(stream_key, shape, cuts, smallest, top_value):
    def one(dim, shards_of):
        steps = jax.random.uniform(jax.random.fold_in(jax.random.fold_in(stream_key, 6), dim), (shards_of,), jnp.float32, smallest / len(cuts), top_value / len(cuts))
        return jnp.repeat(jnp.exp(steps), shape[dim] // shards_of).reshape((-1,) + (1,) * (len(shape) - dim - 1))

    factor_of = one(*cuts[0])
    for cut in cuts[1:]:
        factor_of = factor_of * one(*cut)
    return factor_of


def gaussian(stream_key, shape, scale, reach, cuts=(), kind=jnp.bfloat16):
    values = scale * jax.random.normal(stream_key, shape, jnp.float32)
    if cuts:
        values = values * shard_levels(stream_key, shape, cuts, -0.22, 0.18)
    return jnp.clip(values, -reach, reach).astype(kind)


def heavy_noise(stream_key, shape, scale, most, split, heavy, kind=jnp.bfloat16):
    values = scale * jax.random.normal(stream_key, shape, jnp.float32)
    if split:
        values = values * shard_levels(stream_key, shape, split, -0.22, 0.18)
    return jnp.clip(spiked(values, jax.random.fold_in(stream_key, 3), *heavy), -most, most).astype(kind)


def setup_inputs(seed: int = 0) -> dict:
    seeds = jax.random.split(jax.random.key(seed), 18)
    return {
        "inputs": gaussian(seeds[0], (SEQS, SLOT, D), 1.0, 6.0, ((0, 16), (1, 2))),
        "lengths": draw_lengths(jax.random.fold_in(seeds[17], 71), 0),
        "w_qkv": gaussian(seeds[2], (3, D, HEADS * HEAD_WIDTH), D ** -0.5, 0.21875, ((1, 16), (2, 2))),
        "b_qv": gaussian(seeds[3], (2, HEADS * HEAD_WIDTH), 0.3, 2.0, ((1, 2),), jnp.float32),
        "w_out": gaussian(seeds[4], (HEADS * HEAD_WIDTH, D), (HEADS * HEAD_WIDTH // 64) ** -0.5, 1.75, ((0, 2), (1, 16))),
        "b_out": gaussian(seeds[5], (D,), 0.3, 2.0, (), jnp.float32),
        "ln1_gain": jnp.clip(1.0 + 0.1 * jax.random.normal(seeds[6], (D,), jnp.float32), 0.5, 1.5),
        "ln1_bias": gaussian(seeds[7], (D,), 0.3, 2.0, (), jnp.float32),
        "w_in": gaussian(seeds[8], (D, FF), D ** -0.5, 0.21875, ((0, 16), (1, 2))),
        "b_in": gaussian(seeds[9], (FF,), 0.3, 2.0, ((0, 2),), jnp.float32),
        "w_hid": gaussian(seeds[10], (FF, D), FF ** -0.5, 0.109375, ((0, 2), (1, 16))),
        "b_hid": gaussian(seeds[11], (D,), 0.3, 2.0, (), jnp.float32),
        "ln2_gain": jnp.clip(1.0 + 0.1 * jax.random.normal(seeds[12], (D,), jnp.float32), 0.5, 1.5),
        "ln2_bias": gaussian(seeds[13], (D,), 0.3, 2.0, (), jnp.float32),
        "mask_logits": gaussian(seeds[14], (HEADS, SLOT, SLOT), 1.5, 6.0, ((0, 2), (1, 16)), jnp.float32),
        "noise": gaussian(seeds[15], (HEADS, SLOT, SLOT), 1.0, 6.0, ((0, 2), (1, 16)), jnp.float32),
        "cotangent": heavy_noise(seeds[16], (SEQS, SLOT, D), 1.0, 6.0, ((0, 16), (1, 2)), (0, 2, 16, 2.0), jnp.float32),
    }


HIGH_PRECISION = lax.Precision.HIGHEST
NEG = -1e+30
EPS = 1e-12

@jax.custom_vjp
def low(v):
    return lax.optimization_barrier(v.astype(jnp.bfloat16)).astype(jnp.float32)

@jax.custom_vjp
def low_back(v):
    return v

def low_keep(v):
    return (low(v), None)

def low_pass(kept, grad):
    return (grad,)

def back_keep(v):
    return (v, None)

def back_low(kept, grad):
    return (low(grad),)
low.defvjp(low_keep, low_pass)
low_back.defvjp(back_keep, back_low)

def matmul(left, right):
    return jnp.dot(left, right, precision=HIGH_PRECISION)

def layer_norm(value_rows, scale_vec, shift_vec):
    centre = value_rows - lax.optimization_barrier(jnp.mean(value_rows, axis=-1, keepdims=True))
    spread = lax.optimization_barrier(jnp.mean(centre * centre, axis=-1, keepdims=True))
    return centre * lax.rsqrt(spread + EPS) * scale_vec + shift_vec

def head_scores(key_valid, operands):
    query_rows, key_rows, value_rows, logarithm_mask = operands
    score_matrix = jnp.einsum('noy,nvy->nov', query_rows, key_rows, precision=HIGH_PRECISION) * HEAD_WIDTH ** (-0.5) + logarithm_mask[None]
    score_matrix = low_back(jnp.where(key_valid[:, None, :], score_matrix, NEG))
    attention_probabilities = low(jax.nn.softmax(score_matrix, axis=-1))
    return jnp.einsum('jof,jfl->jol', attention_probabilities, value_rows, precision=HIGH_PRECISION)

def forward(params, block_x, block_len, noise):
    w_qkv, b_qv, w_out, b_out, ln1_gain, ln1_bias, w_in, b_in, w_hid, b_hid, ln2_gain, ln2_bias, mask_logits = params
    group, slot_len, width = block_x.shape
    flat_rows = block_x.reshape(group * slot_len, width)
    query_rows = low(low_back(matmul(flat_rows, w_qkv[0]) + b_qv[0]))
    key_rows = low(low_back(matmul(flat_rows, w_qkv[1])))
    value_rows = low(low_back(matmul(flat_rows, w_qkv[2]) + b_qv[1]))
    logarithm_mask = low(jax.nn.log_sigmoid(mask_logits + noise))

    def split_heads(matrix):
        return matrix.reshape(group, slot_len, HEADS, HEAD_WIDTH).transpose(2, 0, 1, 3)
    key_valid = jnp.arange(slot_len, dtype=jnp.int32)[None, :] < block_len[:, None]
    heads_out = lax.map(jax.checkpoint(partial(head_scores, key_valid)), (split_heads(query_rows), split_heads(key_rows), split_heads(value_rows), logarithm_mask))
    attn = low(low_back(heads_out.transpose(1, 2, 0, 3).reshape(group * slot_len, HEADS * HEAD_WIDTH)))
    branch_att = low_back(matmul(attn, w_out))
    first_sum = flat_rows + branch_att + b_out
    hidden_one = layer_norm(first_sum, ln1_gain, ln1_bias)
    pre_act = low_back(matmul(low(hidden_one), w_in) + b_in)
    activated = low(jax.nn.gelu(pre_act, approximate=False))
    branch_ffn = low_back(matmul(activated, w_hid))
    second_sum = hidden_one + branch_ffn + b_hid
    return layer_norm(second_sum, ln2_gain, ln2_bias).reshape(group, slot_len, width)

def reference(inputs, lengths, w_qkv, b_qv, w_out, b_out, ln1_gain, ln1_bias, w_in, b_in, w_hid, b_hid, ln2_gain, ln2_bias, mask_logits, noise, cotangent):
    params = tuple((item.astype(jnp.float32) for item in (w_qkv, b_qv, w_out, b_out, ln1_gain, ln1_bias, w_in, b_in, w_hid, b_hid, ln2_gain, ln2_bias, mask_logits)))
    noise_f = noise.astype(jnp.float32)
    seq_total, slot_len, width = inputs.shape
    group = math.gcd(seq_total, 4)
    blocks = seq_total // group
    block_inputs = inputs.astype(jnp.float32).reshape(blocks, group, slot_len, width)
    block_lengths = lengths.reshape(blocks, group).astype(jnp.int32)
    block_cot = cotangent.astype(jnp.float32).reshape(blocks, group, slot_len, width)
    zeros = tuple((jnp.zeros_like(item) for item in params))

    def step(totals, operands):
        block_x, block_len, block_c = operands

        def run_block(*pieces):
            return forward(pieces[:-1], pieces[-1], block_len, noise_f)
        block_y, pull = jax.vjp(run_block, *params, block_x)
        valid = (jnp.arange(slot_len, dtype=jnp.int32)[None, :] < block_len[:, None]).astype(block_c.dtype)
        grads = pull(block_c * valid[:, :, None])
        totals = tuple((acc + grad for acc, grad in zip(totals, grads[:-1])))
        return (totals, (block_y.astype(jnp.bfloat16), grads[-1]))
    totals, (block_out, block_grad) = lax.scan(step, zeros, (block_inputs, block_lengths, block_cot))
    outputs = block_out.reshape(seq_total, slot_len, width)
    input_grad = block_grad.reshape(seq_total, slot_len, width)
    return (outputs, input_grad, totals[0], totals[1], totals[2], totals[3], totals[4], totals[5], totals[6], totals[7], totals[8], totals[9], totals[10], totals[11], totals[12])
```

```python
import functools

import jax
import jax.numpy as jnp
from jax import lax
from jax.experimental import pallas as pl
from jax.experimental.pallas import tpu as pltpu
from jax.sharding import PartitionSpec as P

MESH = pl.DeviceIdType.MESH
BF, F32 = jnp.bfloat16, jnp.float32
ANY = pl.BlockSpec(memory_space=pl.ANY)
VM = pl.BlockSpec(memory_space=pltpu.VMEM)


class Place:
    def __init__(self, deep):
        self.Z, self.Y, self.C = deep // 4, 2, 2
        i = lax.axis_index("dp")
        self.t = lax.axis_index("tensor")
        self.c = lax.rem(i, 2)
        self.y = lax.rem(i // 2, 2)
        self.z = i // 4

    def dev(self, z=None, y=None, c=None, t=None):
        z = self.z if z is None else z
        y = self.y if y is None else y
        c = self.c if c is None else c
        t = self.t if t is None else t
        return ((z * self.Y + y) * self.C + c, t)

    def along_z(self, d):
        return self.dev(z=lax.rem(self.z + d, self.Z))

    def source_z(self, d):
        return lax.rem(self.z - d + self.Z, self.Z)

    @property
    def over_y(self):
        return self.dev(y=1 - self.y)

    @property
    def over_c(self):
        return self.dev(c=1 - self.c)

    @property
    def over_t(self):
        return self.dev(t=1 - self.t)

    def greet(self):
        bar = pltpu.get_barrier_semaphore()
        peers = [self.along_z(d) for d in range(1, self.Z)] + [self.over_y, self.over_c, self.over_t]
        for p in peers:
            pl.semaphore_signal(bar, inc=1, device_id=p, device_id_type=MESH)
        pl.semaphore_wait(bar, len(peers))


def rcopy(src, dst, ssem, rsem, dev):
    return pltpu.make_async_remote_copy(src_ref=src, dst_ref=dst, send_sem=ssem, recv_sem=rsem, device_id=dev, device_id_type=MESH)


def dot(a, b):
    return jnp.dot(a, b, preferred_element_type=F32)


def dot_t(a, b):
    return lax.dot_general(a, b, (((1,), (1,)), ((), ())), preferred_element_type=F32)


def dot_0(a, b):
    return lax.dot_general(a, b, (((0,), (0,)), ((), ())), preferred_element_type=F32)


def fwd_kernel(deep, x_sh, mask_sh, qkv_sh, out_sh, in_sh, hid_sh, bin_sh, bias, bqv,
               attn_o, q_o, k_o, v_o, lse_o, x_o, mask_o, qkv_o, out_o, in_o, hid_o, bin_o,
               x_v, w_v, m_v, q_v, k_v, v_v, a_v, lse_v,
               loc, xs, xr, qz_s, qz_r, q1_s, q1_r, mz_s, mz_r, m1_s, m1_r, wz_s, wz_r, w1_s, w1_r, as_, ar):
    me = Place(deep)
    Z = me.Z
    y, c, z, t = me.y, me.c, me.z, me.t
    half = x_sh.shape[0]
    seq, width = x_v.shape
    pairs = q_v.shape[0]
    heads = 2 * pairs
    shards = (out_sh, in_sh, hid_sh)
    wholes = (out_o, in_o, hid_o)

    def cols(k):
        n = shards[k].shape[1]
        return pl.ds(pl.multiple_of(t * n, 128), n)

    rows_own = pl.ds(pl.multiple_of(t * half, 128), half)
    rows_other = pl.ds(pl.multiple_of((1 - t) * half, 128), half)

    locals_ = [
        pltpu.make_async_copy(qkv_sh, w_v.at[z, y, c], loc.at[0]),
        pltpu.make_async_copy(x_sh, x_v.at[rows_own], loc.at[1]),
        pltpu.make_async_copy(mask_sh, m_v.at[:, z, y, c], loc.at[2]),
        pltpu.make_async_copy(bin_sh, bin_o.at[t], loc.at[3]),
    ] + [pltpu.make_async_copy(shards[k], wholes[k].at[z, y, c, :, cols(k)], loc.at[4 + k]) for k in range(3)]
    for cp in locals_:
        cp.start()

    me.greet()

    def x_copy():
        return rcopy(x_sh, x_v.at[rows_own], xs.at[0], xr.at[0], me.over_t)

    def b_copy():
        return rcopy(bin_sh, bin_o.at[t], xs.at[1], xr.at[1], me.over_t)

    def qkv_z(d):
        return rcopy(qkv_sh, w_v.at[z, y, c], qz_s.at[d - 1], qz_r.at[d - 1], me.along_z(d))

    def qkv_y():
        return rcopy(w_v.at[:, y, c], w_v.at[:, y, c], q1_s.at[0], q1_r.at[0], me.over_y)

    def qkv_c():
        return rcopy(w_v.at[:, :, c], w_v.at[:, :, c], q1_s.at[1], q1_r.at[1], me.over_c)

    def mask_z(h, d):
        return rcopy(mask_sh.at[h], m_v.at[h, z, y, c], mz_s.at[h, d - 1], mz_r.at[h, d - 1], me.along_z(d))

    def mask_y(h):
        return rcopy(m_v.at[h, :, y, c], m_v.at[h, :, y, c], m1_s.at[h, 0], m1_r.at[h, 0], me.over_y)

    def mask_c(h):
        return rcopy(m_v.at[h, :, :, c], m_v.at[h, :, :, c], m1_s.at[h, 1], m1_r.at[h, 1], me.over_c)

    def w_z(k, d):
        return rcopy(shards[k], wholes[k].at[z, y, c, :, cols(k)], wz_s.at[k, d - 1], wz_r.at[k, d - 1], me.along_z(d))

    def w_y(k):
        part = wholes[k].at[:, y, c, :, cols(k)]
        return rcopy(part, part, w1_s.at[k, 0], w1_r.at[k, 0], me.over_y)

    def w_x(k):
        part = wholes[k].at[:, :, c, :, cols(k)]
        return rcopy(part, part, w1_s.at[k, 1], w1_r.at[k, 1], me.over_t)

    def w_c(k):
        part = wholes[k].at[:, :, c]
        return rcopy(part, part, w1_s.at[k, 2], w1_r.at[k, 2], me.over_c)

    def a_copy(p):
        n = 128
        at = pl.ds(pl.multiple_of(t * (pairs * n) + p * n, 128), n)
        return rcopy(a_v.at[p, rows_other], attn_o.at[:, at], as_.at[p], ar.at[p], me.over_t)

    def a_local(p):
        n = 128
        at = pl.ds(pl.multiple_of(t * (pairs * n) + p * n, 128), n)
        return pltpu.make_async_copy(a_v.at[p, rows_own], attn_o.at[:, at], loc.at[7 + p])

    zs = range(1, Z)

    def start_z(make, *k):
        for d in zs:
            make(*k, d).start()

    def wait_z(make, *k):
        for d in zs:
            make(*k, d).wait_recv()

    x_copy().start()
    b_copy().start()
    start_z(qkv_z)
    start_z(mask_z, 0)
    start_z(mask_z, 1)
    start_z(w_z, 2)
    for cp in locals_:
        cp.wait()
    wait_z(qkv_z)
    qkv_y().start()
    wait_z(mask_z, 0)
    mask_y(0).start()
    qkv_y().wait_recv()
    qkv_c().start()
    x_copy().wait_recv()
    qkv_c().wait_recv()

    step = half // 2

    def project(r, carry):
        rows = pl.ds(pl.multiple_of(r * step, step), step)
        xb = x_v[rows, :]
        for j, dst in enumerate((q_v, k_v, v_v)):
            w = w_v[:, :, :, j].reshape(width, pairs * 128)
            acc = dot(xb, w)
            if j == 0:
                acc = acc + bqv[0:1, :]
            elif j == 2:
                acc = acc + bqv[1:2, :]
            out = acc.astype(BF)
            if j == 0:
                out = out * jnp.asarray(0.125, BF)
            for p in range(pairs):
                dst[p, rows, :] = out[:, p * 128:(p + 1) * 128]
        return carry

    lax.fori_loop(0, seq // step, project, 0)
    outs = [
        pltpu.make_async_copy(q_v, q_o, loc.at[0]),
        pltpu.make_async_copy(k_v, k_o, loc.at[1]),
        pltpu.make_async_copy(v_v, v_o, loc.at[2]),
        pltpu.make_async_copy(x_v, x_o, loc.at[3]),
        pltpu.make_async_copy(w_v, qkv_o, loc.at[4]),
    ]
    for cp in outs:
        cp.start()

    blk = seq // Z

    def attend(p, u):
        h = 2 * p + u
        sl = slice(64 * u, 64 * u + 64)

        def rows_of(b, carry):
            rows = pl.ds(pl.multiple_of(b * blk, blk), blk)
            s = dot_t(q_v[p, rows, sl], k_v[p, :, sl])
            s = s + m_v[h, b].reshape(blk, seq).astype(F32) + bias[...]
            top = jnp.max(s, axis=-1, keepdims=True)
            e = jnp.exp(s - top)
            total = jnp.sum(e, axis=-1, keepdims=True)
            o = dot(e.astype(BF), v_v[p, :, sl])
            a_v[p, rows, sl] = (o / total).astype(BF)
            lse_v[p, rows, u:u + 1] = top + jnp.log(total)
            return carry

        lax.fori_loop(0, Z, rows_of, 0)

    def mask_save(h):
        return pltpu.make_async_copy(m_v.at[h], mask_o.at[h], loc.at[10 + h])

    order = (2, 1, 0)

    def pair_step(p, carry):
        a, b = 2 * p, 2 * p + 1
        wait_z(mask_z, b)
        mask_y(b).start()

        @pl.when(p < pairs - 1)
        def _():
            start_z(mask_z, a + 2)

        mask_y(a).wait_recv()
        mask_c(a).start()
        for n, k in enumerate(order):
            @pl.when(p == n)
            def _():
                wait_z(w_z, k)
                w_y(k).start()

        @pl.when(p < pairs - 1)
        def _():
            start_z(mask_z, a + 3)

        mask_c(a).wait_recv()
        mask_save(a).start()
        attend(p, 0)
        mask_y(b).wait_recv()
        mask_c(b).start()
        for n, k in enumerate(order[1:]):
            @pl.when(p == n)
            def _():
                start_z(w_z, k)

        @pl.when(p < pairs - 1)
        def _():
            wait_z(mask_z, a + 2)
            mask_y(a + 2).start()

        mask_c(b).wait_recv()
        mask_save(b).start()
        attend(p, 1)
        for n, k in enumerate(order):
            @pl.when(p == n)
            def _():
                w_y(k).wait_recv()
                w_x(k).start()
                if n > 0:
                    w_x(order[n - 1]).wait_recv()
                    w_c(order[n - 1]).start()

        a_copy(p).start()
        a_local(p).start()
        return carry

    lax.fori_loop(0, pairs, pair_step, 0)
    lse_out = pltpu.make_async_copy(lse_v, lse_o, loc.at[5])
    lse_out.start()
    w_x(order[-1]).wait_recv()
    w_c(order[-1]).start()
    for cp in outs + [lse_out]:
        cp.wait()
    for p in range(pairs):
        a_local(p).wait()
        a_copy(p).wait()
    b_copy().wait()
    x_copy().wait_send()
    for d in zs:
        qkv_z(d).wait_send()
    qkv_y().wait_send()
    qkv_c().wait_send()
    for h in range(heads):
        for d in zs:
            mask_z(h, d).wait_send()
        mask_y(h).wait_send()
        mask_c(h).wait_send()
        mask_save(h).wait()
    for k in range(3):
        for d in zs:
            w_z(k, d).wait_send()
        w_y(k).wait_send()
        w_x(k).wait_send()
        w_c(k).wait()


def forward(deep, x, mask, qkv, w_out_t, w_in, w_hid_t, b_in, bias, b_qv):
    half, width = x.shape
    seq = 2 * half
    heads, blk, _ = mask.shape
    pairs = heads // 2
    Z, Y, C = deep // 4, 2, 2
    n_out, n_in = w_out_t.shape[1], w_in.shape[1]
    r = w_in.shape[0]
    sd = jax.ShapeDtypeStruct
    dma = pltpu.SemaphoreType.DMA
    out_shape = (
        sd((half, 2 * pairs * 128), BF),
        sd((pairs, seq, 128), BF), sd((pairs, seq, 128), BF), sd((pairs, seq, 128), BF),
        sd((pairs, seq, 128), F32),
        sd((seq, width), BF),
        sd((heads, Z, Y, C, blk, seq), BF),
        sd((Z, Y, C) + qkv.shape, BF),
        sd((Z, Y, C, r, 2 * n_out), BF), sd((Z, Y, C, r, 2 * n_in), BF), sd((Z, Y, C, r, 2 * n_in), BF),
        sd((2,) + b_in.shape, F32),
    )
    return pl.pallas_call(
        functools.partial(fwd_kernel, deep),
        out_shape=out_shape,
        in_specs=[ANY] * 7 + [VM, VM],
        out_specs=[ANY] * len(out_shape),
        scratch_shapes=[
            pltpu.VMEM((seq, width), BF),
            pltpu.VMEM((Z, Y, C) + qkv.shape, BF),
            pltpu.VMEM((heads, Z, Y, C, blk, seq), BF),
            pltpu.VMEM((pairs, seq, 128), BF), pltpu.VMEM((pairs, seq, 128), BF), pltpu.VMEM((pairs, seq, 128), BF),
            pltpu.VMEM((pairs, seq, 128), BF),
            pltpu.VMEM((pairs, seq, 128), F32),
            dma((16,)), dma((2,)), dma((2,)),
            dma((Z - 1,)), dma((Z - 1,)), dma((2,)), dma((2,)),
            dma((heads, Z - 1)), dma((heads, Z - 1)), dma((heads, 2)), dma((heads, 2)),
            dma((3, Z - 1)), dma((3, Z - 1)), dma((3, 3)), dma((3, 3)),
            dma((pairs,)), dma((pairs,)),
        ],
        compiler_params=pltpu.CompilerParams(collective_id=1, has_side_effects=True, vmem_limit_bytes=58 << 20),
        name="forward_attention",
    )(x, mask, qkv, w_out_t, w_in, w_hid_t, b_in, bias, b_qv)


def bwd_kernel(deep, dat, q_h, k_h, v_h, mask_h, lse_h, x_h, qkv_h, hid_h, in_h, out_h, dz1_h, sg_h, small_h, bias,
               dx_o, gqkv_o, ghid_o, gin_o, gout_o, gmask_o, small_o,
               q_v, k_v, v_v, do_v, lse_v, m_v, p_v, dq_v, dk_v, dv_v, acck, accv,
               lc_m, ly_m, lz_m, gm_v,
               own_w, lc_hid, lx_hid, ly_hid, lz_hid, lc_in, lx_in, ly_in, lz_in, lc_out, lx_out, ly_out, lz_out, fin_hid, fin_in, fin_out,
               p_q, lc_q, ly_q, lz_q, fin_q,
               x_v, w_v, sx_v, lx_x, dx_v, dz_v,
               s_v, sc_v, sy_v, sz_v, sx2_v,
               loc, msem, ds_, dr, wl, w1s, w1r, wzs, wzr, m1s, m1r, mzs, mzr, q1s, q1r, qzs, qzr, xs, xr, s1s, s1r, szs, szr):
    me = Place(deep)
    Z, y, c, z, t = me.Z, me.y, me.c, me.z, me.t
    pairs, seq, _ = q_v.shape
    heads = 2 * pairs
    half = seq // 2
    width = x_v.shape[1]
    zs = range(1, Z)
    rows_own = pl.ds(pl.multiple_of(t * half, 128), half)
    rows_other = pl.ds(pl.multiple_of((1 - t) * half, 128), half)
    parts = (hid_h, in_h, out_h)
    lcs, lxs, lys, lzs, fins = (lc_hid, lc_in, lc_out), (lx_hid, lx_in, lx_out), (ly_hid, ly_in, ly_out), (lz_hid, lz_in, lz_out), (fin_hid, fin_in, fin_out)
    w_outs = (ghid_o, gin_o, gout_o)

    def cols(k, who):
        n = lxs[k].shape[-1]
        return pl.ds(pl.multiple_of(who * n, 128), n)

    def dat_cols(p, who):
        return pl.ds(pl.multiple_of(who * (pairs * 128) + p * 128, 128), 128)

    def dat_local(p):
        return pltpu.make_async_copy(dat.at[:, dat_cols(p, t)], do_v.at[p, rows_own], loc.at[p])

    def dat_copy(p):
        return rcopy(dat.at[:, dat_cols(p, 1 - t)], do_v.at[p, rows_own], ds_.at[p], dr.at[p], me.over_t)

    loads = [pltpu.make_async_copy(a, b, loc.at[3 + n]) for n, (a, b) in enumerate((
        (q_h, q_v), (k_h, k_v), (v_h, v_v), (lse_h, lse_v), (x_h, x_v), (qkv_h, w_v), (dz1_h, dz_v), (small_h, s_v.at[pl.ds(0, small_h.shape[0])])))]

    def m_load(h, slot):
        return pltpu.make_async_copy(mask_h.at[h], m_v.at[slot], msem.at[slot])

    def sg_load(h):
        return pltpu.make_async_copy(sg_h.at[h], gm_v.at[h], loc.at[11 + h])

    def gm_save(h):
        return pltpu.make_async_copy(gm_v.at[h], gmask_o.at[h], loc.at[17 + h])

    def own_at(k):
        n = lcs[k].shape[-1]
        return own_w.at[:, :, :, pl.ds(0, n)]

    def own_load(k):
        return pltpu.make_async_copy(parts[k].at[:, :, c], own_at(k), wl.at[k])

    def w_c(k):
        return rcopy(parts[k].at[:, :, 1 - c], lcs[k], w1s.at[k, 0], w1r.at[k, 0], me.over_c)

    def w_x(k):
        return rcopy(lcs[k].at[:, :, :, cols(k, 1 - t)], lxs[k], w1s.at[k, 1], w1r.at[k, 1], me.over_t)

    def w_y(k):
        return rcopy(lxs[k].at[:, 1 - y], lys[k], w1s.at[k, 2], w1r.at[k, 2], me.over_y)

    def w_z(k, d):
        return rcopy(lys[k].at[lax.rem(z + d, Z)], lzs[k].at[d - 1], wzs.at[k, d - 1], wzr.at[k, d - 1], me.along_z(d))

    def m_c(h, slot):
        return rcopy(p_v.at[slot, :, :, 1 - c], lc_m.at[h], m1s.at[h, 0], m1r.at[h, 0], me.over_c)

    def m_y(h):
        return rcopy(lc_m.at[h, :, 1 - y], ly_m.at[h], m1s.at[h, 1], m1r.at[h, 1], me.over_y)

    def m_z(h, d):
        return rcopy(ly_m.at[h, lax.rem(z + d, Z)], lz_m.at[h, d - 1], mzs.at[h, d - 1], mzr.at[h, d - 1], me.along_z(d))

    def q_c():
        return rcopy(p_q.at[:, :, 1 - c], lc_q, q1s.at[0], q1r.at[0], me.over_c)

    def q_y():
        return rcopy(lc_q.at[:, 1 - y], ly_q, q1s.at[1], q1r.at[1], me.over_y)

    def q_z(d):
        return rcopy(ly_q.at[lax.rem(z + d, Z)], lz_q.at[d - 1], qzs.at[d - 1], qzr.at[d - 1], me.along_z(d))

    def x_copy():
        return rcopy(sx_v, lx_x, xs, xr, me.over_t)

    def s_c():
        return rcopy(s_v, sc_v, s1s.at[0], s1r.at[0], me.over_c)

    def s_y():
        return rcopy(sc_v, sy_v, s1s.at[1], s1r.at[1], me.over_y)

    def s_z(d):
        return rcopy(sy_v, sz_v.at[z], szs.at[d - 1], szr.at[d - 1], me.along_z(d))

    def s_z_in(d):
        return rcopy(sy_v, sz_v.at[me.source_z(d)], szs.at[d - 1], szr.at[d - 1], me.along_z(d))

    def s_x():
        return rcopy(s_v, sx2_v, s1s.at[2], s1r.at[2], me.over_t)

    for p in range(pairs):
        dat_local(p).start()
    for cp in loads:
        cp.start()
    own_load(0).start()
    m_load(0, 0).start()
    me.greet()
    for p in range(pairs):
        dat_copy(p).start()
    for k in range(3):
        w_c(k).start()
    for h in range(heads):
        sg_load(h).start()

    def add_own(k):
        own_load(k).wait()
        w_c(k).wait_recv()
        n = lcs[k].shape[-1]

        def one(i, carry):
            for j in range(me.Y):
                lcs[k][i, j] = lcs[k][i, j] + own_w[i, j, :, 0:n]
            return carry

        lax.fori_loop(0, Z, one, 0)

    for k in range(3):
        add_own(k)
        if k < 2:
            own_load(k + 1).start()
        w_x(k).start()
    for cp in loads:
        cp.wait()

    blk = seq // Z
    shape4 = p_v.shape[2:]

    def attend(p, u, slot):
        sl = slice(64 * u, 64 * u + 64)
        acck[...] = jnp.zeros_like(acck)
        accv[...] = jnp.zeros_like(accv)

        def rows_of(b, carry):
            rows = pl.ds(pl.multiple_of(b * blk, blk), blk)
            qb, dob = q_v[p, rows, sl], do_v[p, rows, sl]
            kk, vv = k_v[p, :, sl], v_v[p, :, sl]
            s = dot_t(qb, kk) + m_v[u, b].reshape(blk, seq).astype(F32) + bias[...]
            pr = jnp.exp(s - lse_v[p, rows, u:u + 1])
            dp = dot_t(dob, vv)
            tt = pr * dp
            delta = jnp.sum(tt, axis=-1, keepdims=True)
            dsb = (tt - pr * delta).astype(BF)
            p_v[slot, b] = dsb.reshape(shape4)
            dq_v[p, rows, sl] = (dot(dsb, kk) * 0.125).astype(BF)
            acck[...] += dot_0(dsb, qb)
            accv[...] += dot_0(pr.astype(BF), dob)
            return carry

        lax.fori_loop(0, Z, rows_of, 0)
        dk_v[p, :, sl] = acck[...].astype(BF)
        dv_v[p, :, sl] = accv[...].astype(BF)

    def m_add_c(h, slot):
        m_c(h, slot).wait_recv()

        def one(i, carry):
            for j in range(me.Y):
                lc_m[h, i, j] = lc_m[h, i, j] + p_v[slot, i, j, c]
            return carry

        lax.fori_loop(0, Z, one, 0)
        m_y(h).start()

    def m_add_y(h):
        m_y(h).wait_recv()

        def one(i, carry):
            ly_m[h, i] = ly_m[h, i] + lc_m[h, i, y]
            return carry

        lax.fori_loop(0, Z, one, 0)
        for d in zs:
            m_z(h, d).start()

    def m_end(h):
        total = ly_m[h, z].astype(F32)
        for d in zs:
            m_z(h, d).wait_recv()
            total = total + lz_m[h, d - 1].astype(F32)
        sg_load(h).wait()
        gm_v[h] = total * gm_v[h]
        gm_save(h).start()

    def head_step(p, u):
        h = 2 * p + u
        m_load(h, u).wait()
        if u == 0:
            m_load(h + 1, 1).start()
        else:
            @pl.when(p < pairs - 1)
            def _():
                m_load(h + 1, 0).start()

        @pl.when(p > 0)
        def _():
            m_c(h - 2, u).wait_send()

        attend(p, u, u)
        m_c(h, u).start()
        if u == 1:
            m_add_c(h - 1, 0)
        else:
            @pl.when(p > 0)
            def _():
                m_add_c(h - 1, 1)

        @pl.when(h >= 2)
        def _():
            m_add_y(h - 2)

    def pair_step(p, carry):
        dat_local(p).wait()
        dat_copy(p).wait_recv()
        head_step(p, 0)
        head_step(p, 1)
        return carry

    lax.fori_loop(0, pairs, pair_step, 0)

    def w_add_x(k):
        w_x(k).wait_recv()

        def one(i, carry):
            for j in range(me.Y):
                lxs[k][i, j] = lxs[k][i, j] + lcs[k][i, j, :, cols(k, t)]
            return carry

        lax.fori_loop(0, Z, one, 0)
        w_y(k).start()

    def w_add_y(k):
        w_y(k).wait_recv()

        def one(i, carry):
            lys[k][i] = lys[k][i] + lxs[k][i, y]
            return carry

        lax.fori_loop(0, Z, one, 0)
        for d in zs:
            w_z(k, d).start()

    def w_end(k):
        total = lys[k][z].astype(F32)
        for d in zs:
            w_z(k, d).wait_recv()
            total = total + lzs[k][d - 1].astype(F32)
        fins[k][...] = total
        pltpu.make_async_copy(fins[k], w_outs[k], wl.at[3 + k]).start()

    m_add_c(heads - 1, 1)
    w_add_x(0)

    step = half // 2

    def d_cat(ref, rows):
        return jnp.concatenate([ref[p, rows, :] for p in range(pairs)], axis=1)

    def weight(j):
        return w_v[:, :, :, j].reshape(width, pairs * 128)

    def terms(rows):
        acc = dot_t(d_cat(dq_v, rows), weight(0))
        acc = acc + dot_t(d_cat(dk_v, rows), weight(1))
        return acc + dot_t(d_cat(dv_v, rows), weight(2))

    def theirs(r, carry):
        at = pl.ds(pl.multiple_of(r * step, step), step)
        rows = pl.ds(pl.multiple_of((1 - t) * half + r * step, step), step)
        sx_v[at, :] = terms(rows).astype(BF)
        return carry

    lax.fori_loop(0, 2, theirs, 0)
    x_copy().start()

    for j, ref in enumerate((dq_v, dk_v, dv_v)):
        g = dot_0(x_v[...], d_cat(ref, slice(None)))
        p_q[:, :, :, j] = g.astype(BF).reshape(p_q.shape[:3] + p_q.shape[4:])
    q_c().start()
    base = small_h.shape[0]
    for n, ref in enumerate((dq_v, dv_v)):
        for p in range(pairs):
            at = base + n * pairs + p
            s_v[at:at + 1, :] = jnp.sum(ref[p].astype(F32), axis=0, keepdims=True)
    for at in range(base + 2 * pairs, s_v.shape[0]):
        s_v[at:at + 1, :] = jnp.zeros((1, 128), F32)
    s_c().start()

    def mine(r, carry):
        at = pl.ds(pl.multiple_of(r * step, step), step)
        rows = pl.ds(pl.multiple_of(t * half + r * step, step), step)
        dx_v[at, :] = terms(rows) + dz_v[at, :]
        return carry

    lax.fori_loop(0, 2, mine, 0)
    q_c().wait_recv()
    for i in range(Z):
        lc_q[i] = lc_q[i] + p_q[i, :, c]
    q_y().start()
    s_c().wait_recv()
    sc_v[...] = sc_v[...] + s_v[...]
    s_y().start()
    m_add_y(heads - 2)
    w_add_x(1)
    m_end(0)
    m_end(1)
    w_add_x(2)
    m_end(2)
    m_add_y(heads - 1)
    m_end(3)
    w_add_y(0)
    m_end(4)
    q_y().wait_recv()
    for i in range(Z):
        ly_q[i] = ly_q[i] + lc_q[i, y]
    for d in zs:
        q_z(d).start()
    s_y().wait_recv()
    sy_v[...] = sy_v[...] + sc_v[...]
    sz_v[z] = sy_v[...]
    for d in zs:
        s_z(d).start()
    m_end(5)
    w_add_y(1)
    w_end(0)
    w_add_y(2)
    x_copy().wait_recv()
    dx_v[...] = dx_v[...] + lx_x[...].astype(F32)
    dx_save = pltpu.make_async_copy(dx_v, dx_o, loc.at[23])
    dx_save.start()
    total = ly_q[z].astype(F32)
    for d in zs:
        q_z(d).wait_recv()
        total = total + lz_q[d - 1].astype(F32)
    fin_q[...] = total
    q_save = pltpu.make_async_copy(fin_q, gqkv_o, loc.at[24])
    q_save.start()
    for d in zs:
        s_z_in(d).wait_recv()
    s_c().wait_send()
    total = sz_v[0]
    for i in range(1, Z):
        total = total + sz_v[i]
    s_v[...] = total
    s_x().start()
    w_end(1)
    w_end(2)
    s_x().wait_recv()
    low = sx2_v[...] + s_v[...]
    row = lax.broadcasted_iota(jnp.int32, low.shape, 0)
    sy_done = s_y()
    sy_done.wait_send()
    sc_v[...] = jnp.where(row < base, low, s_v[...])
    s_save = pltpu.make_async_copy(sc_v, small_o, loc.at[25])
    s_save.start()

    for p in range(pairs):
        dat_copy(p).wait_send()
    for k in range(3):
        w_c(k).wait_send()
        w_x(k).wait_send()
        w_y(k).wait_send()
        for d in zs:
            w_z(k, d).wait_send()
        pltpu.make_async_copy(fins[k], w_outs[k], wl.at[3 + k]).wait()
    for h in range(heads):
        if h >= heads - 2:
            m_c(h, h % 2).wait_send()
        m_y(h).wait_send()
        for d in zs:
            m_z(h, d).wait_send()
        gm_save(h).wait()
    q_c().wait_send()
    q_y().wait_send()
    for d in zs:
        q_z(d).wait_send()
        s_z(d).wait_send()
    x_copy().wait_send()
    s_x().wait_send()
    dx_save.wait()
    q_save.wait()
    s_save.wait()


def backward(deep, dat, q, k, v, mask, lse, x, qkv, g_hid, g_in, g_out, dz1, sg, small, bias):
    pairs, seq, _ = q.shape
    half, width = dz1.shape
    heads, Z, Y, C, blk, _ = mask.shape
    r, n2 = g_in.shape[3], g_in.shape[4]
    n2o = g_out.shape[4]
    n, no = n2 // 2, n2o // 2
    base = small.shape[0]
    rows_s = base + 8
    sd = jax.ShapeDtypeStruct
    dma = pltpu.SemaphoreType.DMA
    vm = pltpu.VMEM
    out_shape = (
        sd((half, width), F32), sd(qkv.shape[3:], F32), sd((r, n), F32), sd((r, n), F32), sd((r, no), F32),
        sd((heads, blk, seq), F32), sd((rows_s, 128), F32),
    )
    pair = vm((pairs, seq, 128), BF)

    def chain(m):
        return [vm((Z, Y, r, 2 * m), BF), vm((Z, Y, r, m), BF), vm((Z, r, m), BF), vm((Z - 1, r, m), BF)]

    three, rq, nq = qkv.shape[3:]
    return pl.pallas_call(
        functools.partial(bwd_kernel, deep),
        out_shape=out_shape,
        in_specs=[ANY] * 14 + [VM],
        out_specs=[ANY] * len(out_shape),
        scratch_shapes=[
            pair, pair, pair, pair, vm((pairs, seq, 128), F32), vm((2, Z, Y, C, blk, seq), BF), vm((2, Z, Y, C, blk, seq), BF),
            pair, pair, pair, vm((seq, 64), F32), vm((seq, 64), F32),
            vm((heads, Z, Y, blk, seq), BF), vm((heads, Z, blk, seq), BF), vm((heads, Z - 1, blk, seq), BF), vm((heads, blk, seq), F32),
            vm((Z, Y, r, n2), BF), *chain(n), *chain(n), *chain(no), vm((r, n), F32), vm((r, n), F32), vm((r, no), F32),
            vm((Z, Y, C, three, rq, nq), BF), vm((Z, Y, three, rq, nq), BF), vm((Z, three, rq, nq), BF), vm((Z - 1, three, rq, nq), BF), vm((three, rq, nq), F32),
            vm((seq, width), BF), vm((Z, Y, C, three, rq, nq), BF), vm((half, width), BF), vm((half, width), BF), vm((half, width), F32), vm((half, width), F32),
            vm((rows_s, 128), F32), vm((rows_s, 128), F32), vm((rows_s, 128), F32), vm((Z, rows_s, 128), F32), vm((rows_s, 128), F32),
            dma((26,)), dma((2,)), dma((pairs,)), dma((pairs,)),
            dma((6,)), dma((3, 3)), dma((3, 3)), dma((3, Z - 1)), dma((3, Z - 1)),
            dma((heads, 2)), dma((heads, 2)), dma((heads, Z - 1)), dma((heads, Z - 1)),
            dma((2,)), dma((2,)), dma((Z - 1,)), dma((Z - 1,)), dma, dma,
            dma((3,)), dma((3,)), dma((Z - 1,)), dma((Z - 1,)),
        ],
        compiler_params=pltpu.CompilerParams(collective_id=2, has_side_effects=True, vmem_limit_bytes=62 << 20),
        name="backward_attention",
    )(dat, q, k, v, mask, lse, x, qkv, g_hid, g_in, g_out, dz1, sg, small, bias)


NEG = -1e30
EPS = 1e-12


def layer_norm(value_rows, scale_vec, shift_vec):
    centre = value_rows - jnp.mean(value_rows, axis=-1, keepdims=True)
    spread = jnp.mean(centre * centre, axis=-1, keepdims=True)
    return centre * lax.rsqrt(spread + EPS) * scale_vec + shift_vec


def gelu_exact(value_rows):
    return jax.nn.gelu(value_rows, approximate=False)


def matmul(left, right):
    return jnp.dot(left, right, preferred_element_type=jnp.float32)


def times_transposed(left, right):
    return lax.dot_general(
        left, right, (((1,), (1,)), ((), ())), preferred_element_type=jnp.float32
    )


def over_rows(left, right):
    return lax.dot_general(
        left, right, (((0,), (0,)), ((), ())), preferred_element_type=jnp.float32
    )


def plain_body(
    inputs,
    lengths,
    w_qkv,
    b_qv,
    w_out,
    b_out,
    ln1_gain,
    ln1_bias,
    w_in,
    b_in,
    w_hid,
    b_hid,
    ln2_gain,
    ln2_bias,
    mask_logits,
    noise,
    cotangent,
):
    seq_count, half_rows, width = inputs.shape
    slot_len = half_rows * lax.axis_size("tensor")
    tensor_rank = lax.axis_index("tensor")
    head_count = mask_logits.shape[0]
    head_dim = w_qkv.shape[2] // head_count
    scale = head_dim ** (-0.5)
    token_count = seq_count * slot_len
    mixed_logits = mask_logits + noise
    local_mask = jax.nn.log_sigmoid(mixed_logits).astype(jnp.bfloat16)
    full_qkv, full_out, full_in, full_hid, full_mask = (
        lax.all_gather(w_qkv, "dp", axis=1, tiled=True),
        lax.all_gather(w_out, "dp", axis=1, tiled=True),
        lax.all_gather(w_in, "dp", axis=0, tiled=True),
        lax.all_gather(w_hid, "dp", axis=1, tiled=True),
        lax.all_gather(local_mask, "dp", axis=1, tiled=True),
    )
    key_valid = jnp.arange(slot_len, dtype=jnp.int32)[None, :] < lengths[:, None]
    own_rows = tensor_rank * half_rows + jnp.arange(half_rows, dtype=jnp.int32)
    row_valid = (own_rows[None, :] < lengths[:, None]).astype(jnp.float32)
    gathered = lax.all_gather(inputs, "tensor", axis=1, tiled=True)
    flat_rows = gathered.reshape(token_count, width)
    query_rows = (matmul(flat_rows, full_qkv[0]) + b_qv[0]).astype(jnp.bfloat16)
    key_rows = matmul(flat_rows, full_qkv[1]).astype(jnp.bfloat16)
    value_rows = (matmul(flat_rows, full_qkv[2]) + b_qv[1]).astype(jnp.bfloat16)

    def split_heads(matrix):
        return matrix.reshape(seq_count, slot_len, head_count, head_dim).transpose(0, 2, 1, 3)

    def join_heads(stacked):
        return stacked.transpose(0, 2, 1, 3).reshape(token_count, head_count * head_dim)

    def masked_scores(query_h, keys_h, mask_h, valid_keys):
        score_matrix = (
            jnp.einsum("qd,kd->qk", query_h, keys_h, preferred_element_type=jnp.float32) * scale
        )
        score_matrix = score_matrix + mask_h.astype(jnp.float32)
        return jnp.where(valid_keys[None, :], score_matrix, NEG)

    def attend_sequence(operands):
        query_s, keys_s, values_s, valid_keys = operands

        def attend_head(head_ops):
            query_h, keys_h, values_h, mask_h = head_ops
            score_matrix = masked_scores(query_h, keys_h, mask_h, valid_keys)
            top_score = jnp.max(score_matrix, axis=-1, keepdims=True)
            expo = jnp.exp(score_matrix - top_score)
            row_total = jnp.sum(expo, axis=-1, keepdims=True)
            attention_probabilities = (expo / row_total).astype(jnp.bfloat16)
            result = jnp.einsum(
                "qk,kd->qd", attention_probabilities, values_h, preferred_element_type=jnp.float32
            )
            return (result.astype(jnp.bfloat16), (top_score + jnp.log(row_total))[:, 0])

        return lax.map(attend_head, (query_s, keys_s, values_s, full_mask))

    head_out, log_total = lax.map(
        attend_sequence,
        (split_heads(query_rows), split_heads(key_rows), split_heads(value_rows), key_valid),
    )
    attn = join_heads(head_out)
    attn_terms = matmul(attn, full_out).reshape(seq_count, slot_len, width)
    attn_part = lax.psum_scatter(attn_terms, "tensor", scatter_dimension=1, tiled=True)
    first_sum = inputs.astype(jnp.float32) + attn_part + b_out
    hidden_one = layer_norm(first_sum, ln1_gain, ln1_bias)
    hidden_rows = lax.all_gather(
        hidden_one.astype(jnp.bfloat16), "tensor", axis=1, tiled=True
    ).reshape(token_count, width)
    pre_act = matmul(hidden_rows, full_in) + b_in
    activated = gelu_exact(pre_act).astype(jnp.bfloat16)
    ffn_terms = matmul(activated, full_hid).reshape(seq_count, slot_len, width)
    ffn_part = lax.psum_scatter(ffn_terms, "tensor", scatter_dimension=1, tiled=True)
    second_sum = hidden_one + ffn_part + b_hid
    outputs = layer_norm(second_sum, ln2_gain, ln2_bias).astype(jnp.bfloat16)
    back_qkv, back_out, back_in, back_hid, back_mask = (
        lax.all_gather(w_qkv, "dp", axis=1, tiled=True),
        lax.all_gather(w_out, "dp", axis=1, tiled=True),
        lax.all_gather(w_in, "dp", axis=0, tiled=True),
        lax.all_gather(w_hid, "dp", axis=1, tiled=True),
        lax.all_gather(local_mask, "dp", axis=1, tiled=True),
    )
    grad_output = cotangent * row_valid[:, :, None]
    _, pull_second = jax.vjp(layer_norm, second_sum, ln2_gain, ln2_bias)
    grad_second, ln2_gain_part, ln2_bias_part = pull_second(grad_output)
    b_hid_part = jnp.sum(grad_second, axis=(0, 1))
    second_rows = lax.all_gather(
        grad_second.astype(jnp.bfloat16), "tensor", axis=1, tiled=True
    ).reshape(token_count, width)
    w_hid_grad = over_rows(activated, second_rows)
    grad_act = times_transposed(second_rows, back_hid)
    _, pull_gelu = jax.vjp(gelu_exact, pre_act)
    grad_pre = pull_gelu(grad_act)[0].astype(jnp.bfloat16)
    b_in_part = jnp.sum(grad_pre.astype(jnp.float32), axis=0)
    w_in_grad = over_rows(hidden_rows, grad_pre)
    hidden_terms = times_transposed(grad_pre, back_in).reshape(seq_count, slot_len, width)
    grad_hidden = grad_second + lax.psum_scatter(
        hidden_terms, "tensor", scatter_dimension=1, tiled=True
    )
    _, pull_first = jax.vjp(layer_norm, first_sum, ln1_gain, ln1_bias)
    grad_first, ln1_gain_part, ln1_bias_part = pull_first(grad_hidden)
    b_out_part = jnp.sum(grad_first, axis=(0, 1))
    first_rows = lax.all_gather(
        grad_first.astype(jnp.bfloat16), "tensor", axis=1, tiled=True
    ).reshape(token_count, width)
    w_out_grad = over_rows(attn, first_rows)
    grad_attn = times_transposed(first_rows, back_out).astype(jnp.bfloat16)

    def sequence_back(mask_acc, operands):
        query_s, keys_s, values_s, grad_s, total_s, valid_keys = operands

        def head_back(head_ops):
            query_h, keys_h, values_h, mask_h, grad_h, total_h = head_ops
            score_matrix = masked_scores(query_h, keys_h, mask_h, valid_keys)
            attention_probabilities = jnp.exp(score_matrix - total_h[:, None])
            grad_probs = jnp.einsum(
                "qd,kd->qk", grad_h, values_h, preferred_element_type=jnp.float32
            )
            centre = jnp.sum(attention_probabilities * grad_probs, axis=-1, keepdims=True)
            grad_scores = (attention_probabilities * (grad_probs - centre)).astype(jnp.bfloat16)
            grad_q = (
                jnp.einsum("qk,kd->qd", grad_scores, keys_h, preferred_element_type=jnp.float32)
                * scale
            ).astype(jnp.bfloat16)
            grad_k = (
                jnp.einsum("qk,qd->kd", grad_scores, query_h, preferred_element_type=jnp.float32)
                * scale
            ).astype(jnp.bfloat16)
            grad_v = jnp.einsum(
                "qk,qd->kd",
                attention_probabilities.astype(jnp.bfloat16),
                grad_h,
                preferred_element_type=jnp.float32,
            ).astype(jnp.bfloat16)
            return (grad_q, grad_k, grad_v, grad_scores)

        grad_q, grad_k, grad_v, grad_sc = lax.map(
            head_back, (query_s, keys_s, values_s, back_mask, grad_s, total_s)
        )
        return (mask_acc + grad_sc.astype(jnp.float32), (grad_q, grad_k, grad_v))

    mask_zero = jnp.zeros(back_mask.shape, jnp.float32)
    mask_grad, (heads_q, heads_k, heads_v) = lax.scan(
        sequence_back,
        mask_zero,
        (
            split_heads(query_rows),
            split_heads(key_rows),
            split_heads(value_rows),
            split_heads(grad_attn),
            log_total,
            key_valid,
        ),
    )
    query_grad = join_heads(heads_q)
    keys_grad = join_heads(heads_k)
    values_grad = join_heads(heads_v)
    b_qv_part = jnp.stack(
        [
            jnp.sum(query_grad.astype(jnp.float32), axis=0),
            jnp.sum(values_grad.astype(jnp.float32), axis=0),
        ]
    )
    w_qkv_grad = jnp.stack(
        [
            over_rows(flat_rows, query_grad),
            over_rows(flat_rows, keys_grad),
            over_rows(flat_rows, values_grad),
        ]
    )
    input_terms = (
        times_transposed(query_grad, back_qkv[0])
        + times_transposed(keys_grad, back_qkv[1])
        + times_transposed(values_grad, back_qkv[2])
    ).reshape(seq_count, slot_len, width)
    input_grad = grad_first + lax.psum_scatter(
        input_terms.astype(jnp.bfloat16), "tensor", scatter_dimension=1, tiled=True
    ).astype(jnp.float32)
    qkv_total, out_total, in_total, hid_total, mask_total = (
        lax.psum_scatter(w_qkv_grad, "dp", scatter_dimension=1, tiled=True),
        lax.psum_scatter(w_out_grad, "dp", scatter_dimension=1, tiled=True),
        lax.psum_scatter(w_in_grad, "dp", scatter_dimension=0, tiled=True),
        lax.psum_scatter(w_hid_grad, "dp", scatter_dimension=1, tiled=True),
        lax.psum_scatter(mask_grad, "dp", scatter_dimension=1, tiled=True),
    )
    mask_logit_grad = mask_total * jax.nn.sigmoid(-mixed_logits)
    ln1_gain_total, ln1_bias_total, ln2_gain_total, ln2_bias_total, b_out_total, b_hid_total = (
        lax.psum(
            (ln1_gain_part, ln1_bias_part, ln2_gain_part, ln2_bias_part, b_out_part, b_hid_part),
            ("dp", "tensor"),
        )
    )
    b_qv_total, b_in_total = lax.psum((b_qv_part, b_in_part), "dp")
    return (
        outputs,
        input_grad,
        qkv_total,
        b_qv_total,
        out_total,
        b_out_total,
        ln1_gain_total,
        ln1_bias_total,
        in_total,
        b_in_total,
        hid_total,
        b_hid_total,
        ln2_gain_total,
        ln2_bias_total,
        mask_logit_grad,
    )


def norm_stats(rows):
    centre = rows - jnp.mean(rows, axis=-1, keepdims=True)
    scale = lax.rsqrt(jnp.mean(centre * centre, axis=-1, keepdims=True) + EPS)
    return centre * scale, scale


def norm_back(e, hat, scale):
    return (e - jnp.mean(e, axis=-1, keepdims=True) - hat * jnp.mean(e * hat, axis=-1, keepdims=True)) * scale


def body(
    inputs, lengths, w_qkv, b_qv, w_out, b_out, ln1_gain, ln1_bias, w_in, b_in, w_hid, b_hid,
    ln2_gain, ln2_bias, mask_logits, noise, cotangent,
):
    deep = lax.axis_size("dp")
    x = inputs[0]
    half, width = x.shape
    seq = 2 * half
    t = lax.axis_index("tensor")
    length = lengths[0]
    mixed = mask_logits + noise
    mask = jax.nn.log_sigmoid(mixed).astype(BF)
    gate = jax.nn.sigmoid(-mixed)
    bias = jnp.where(jnp.arange(seq, dtype=jnp.int32) < length, 0.0, NEG).astype(F32)[None]
    attn, q, k, v, lse, x_all, mask_all, qkv_all, out_all, in_all, hid_all, bin_all = forward(
        deep, x, mask, w_qkv, w_out.T, w_in, w_hid.T, b_in[None], bias, b_qv)
    w_out_t = out_all.reshape(width, -1)
    w_in_all = in_all.reshape(width, -1)
    w_hid_t = hid_all.reshape(width, -1)

    z1 = x.astype(F32) + dot_t(attn, w_out_t) + b_out
    hat1, scale1 = norm_stats(z1)
    h1 = hat1 * ln1_gain + ln1_bias
    h1b = h1.astype(BF)
    pre = dot(h1b, w_in_all) + bin_all.reshape(-1)
    act = gelu_exact(pre).astype(BF)
    z2 = h1 + dot_t(act, w_hid_t) + b_hid
    hat2, scale2 = norm_stats(z2)
    outputs = (hat2 * ln2_gain + ln2_bias).astype(BF)

    rows = t * half + jnp.arange(half, dtype=jnp.int32)
    dy = cotangent[0] * (rows < length).astype(F32)[:, None]
    dz2 = norm_back(dy * ln2_gain, hat2, scale2)
    dz2b = dz2.astype(BF)
    g_hid = dot_0(dz2b, act).astype(BF)
    _, pull = jax.vjp(gelu_exact, pre)
    dpre = pull(dot(dz2b, w_hid_t))[0].astype(BF)
    g_in = dot_0(h1b, dpre).astype(BF)
    dh1 = dz2 + dot_t(dpre, w_in_all)
    dz1 = norm_back(dh1 * ln1_gain, hat1, scale1)
    dz1b = dz1.astype(BF)
    g_out = dot_0(dz1b, attn).astype(BF)
    dattn = dot(dz1b, w_out_t).astype(BF)

    sums = [
        jnp.sum(dh1 * hat1, axis=0), jnp.sum(dh1, axis=0), jnp.sum(dy * hat2, axis=0), jnp.sum(dy, axis=0),
        jnp.sum(dz1, axis=0), jnp.sum(dz2, axis=0), jnp.sum(dpre.astype(F32), axis=0),
    ]
    flat = jnp.concatenate(sums).reshape(-1, 128)
    filled = flat.shape[0]
    small = jnp.pad(flat, ((0, -filled % 8), (0, 0)))

    dx, gqkv, ghid, gin, gout, gmask, total = backward(
        deep, dattn, q, k, v, mask_all, lse, x_all, qkv_all,
        g_hid.reshape(hid_all.shape), g_in.reshape(in_all.shape), g_out.reshape(out_all.shape), dz1, gate, small, bias)
    vec = total[:6 * width // 128].reshape(6, width)
    g_bin = lax.dynamic_slice_in_dim(total[6 * width // 128:filled].reshape(-1), t * b_in.shape[0], b_in.shape[0])
    g_bqv = total[small.shape[0]:small.shape[0] + 2 * b_qv.shape[1] // 128].reshape(b_qv.shape)
    return (
        outputs[None], dx[None], gqkv, g_bqv, gout.T, vec[4], vec[0], vec[1], gin, g_bin, ghid.T, vec[5],
        vec[2], vec[3], gmask,
    )


def solution(mesh):
    placed = (
        P("dp", "tensor", None),
        P("dp"),
        P(None, "dp", "tensor"),
        P(None, "tensor"),
        P("tensor", "dp"),
        P(),
        P(),
        P(),
        P("dp", "tensor"),
        P("tensor"),
        P("tensor", "dp"),
        P(),
        P(),
        P(),
        P("tensor", "dp", None),
        P("tensor", "dp", None),
        P("dp", "tensor", None),
    )

    def run(*args):
        w_rows, m_rows = args[8].shape[0], args[14].shape[1]
        tiled = w_rows % 16 == 0 and m_rows % 16 == 0 and args[0].shape[0] == 1
        return (body if tiled else plain_body)(*args)

    return jax.shard_map(
        run,
        mesh=mesh,
        in_specs=placed,
        out_specs=(
            P("dp", "tensor", None),
            P("dp", "tensor", None),
            P(None, "dp", "tensor"),
            P(None, "tensor"),
            P("tensor", "dp"),
            P(),
            P(),
            P(),
            P("dp", "tensor"),
            P("tensor"),
            P("tensor", "dp"),
            P(),
            P(),
            P(),
            P("tensor", "dp", None),
        ),
        check_vma=False,
    )
```

```python
import functools

import jax
import jax.numpy as jnp
from jax import lax
from jax.experimental import pallas as pl
from jax.experimental.pallas import tpu as pltpu
from jax.sharding import PartitionSpec as P

MESH = pl.DeviceIdType.MESH
BF, F32 = jnp.bfloat16, jnp.float32
ANY = pl.BlockSpec(memory_space=pl.ANY)
VM = pl.BlockSpec(memory_space=pltpu.VMEM)


class Place:
    def __init__(self, deep):
        self.Z, self.Y, self.C = deep // 4, 2, 2
        i = lax.axis_index("dp")
        self.t = lax.axis_index("tensor")
        self.c = lax.rem(i, 2)
        self.y = lax.rem(i // 2, 2)
        self.z = i // 4
        far = self.z // 2
        self.outer = 1 - lax.rem(self.z + far, 2)
        self.z_near = self.z + 1 - 2 * lax.rem(self.z, 2)
        self.z_far_inner = 2 - far
        self.z_far_outer = 3 - 3 * far

    def dev(self, z=None, y=None, c=None, t=None):
        z = self.z if z is None else z
        y = self.y if y is None else y
        c = self.c if c is None else c
        t = self.t if t is None else t
        return ((z * self.Y + y) * self.C + c, t)

    def along_z(self, d):
        return self.dev(z=lax.rem(self.z + d, self.Z))

    def source_z(self, d):
        return lax.rem(self.z - d + self.Z, self.Z)

    @property
    def over_y(self):
        return self.dev(y=1 - self.y)

    @property
    def over_c(self):
        return self.dev(c=1 - self.c)

    @property
    def over_t(self):
        return self.dev(t=1 - self.t)

    def greet(self):
        bar = pltpu.get_barrier_semaphore()
        peers = [self.along_z(d) for d in range(1, self.Z)] + [self.over_y, self.over_c, self.over_t]
        for p in peers:
            pl.semaphore_signal(bar, inc=1, device_id=p, device_id_type=MESH)
        pl.semaphore_wait(bar, len(peers))


def rcopy(src, dst, ssem, rsem, dev):
    return pltpu.make_async_remote_copy(src_ref=src, dst_ref=dst, send_sem=ssem, recv_sem=rsem, device_id=dev, device_id_type=MESH)


def dot(a, b):
    return jnp.dot(a, b, preferred_element_type=F32)


def dot_t(a, b):
    return lax.dot_general(a, b, (((1,), (1,)), ((), ())), preferred_element_type=F32)


def dot_0(a, b):
    return lax.dot_general(a, b, (((0,), (0,)), ((), ())), preferred_element_type=F32)


class Pass:
    def __init__(self, me, own, view, pair, sems, early=False, wide=False):
        self.me, self.own, self.view, self.pair, self.early, self.wide = me, own, view, pair, early, wide
        self.zs, self.zr, self.fs, self.ys, self.yr, self.xs, self.xr, self.cs, self.cr = sems

    def held(self, z):
        me = self.me
        return self.view(z, slice(None) if self.early else me.y, me.t)

    def source(self):
        return self.held(self.me.z) if self.early else self.own

    def near(self):
        me = self.me
        return rcopy(self.source(), self.held(me.z), self.zs.at[0], self.zr.at[0], me.dev(z=me.z_near))

    def far(self):
        me = self.me
        return rcopy(self.source(), self.held(me.z), self.zs.at[1], self.zr.at[1 + me.outer], me.dev(z=me.z_far_inner))

    def onward(self, n):
        me = self.me
        place = self.held(me.z_far_inner if n == 0 else me.z_far_outer)
        return rcopy(place, place, self.fs.at[n], self.zr.at[1 + n], me.dev(z=me.z_near))

    def z_start(self):
        self.near().start()
        self.far().start()

    def relay(self):
        @pl.when(self.me.outer == 0)
        def _():
            for n in range(2):
                self.onward(n).wait_recv()
                self.onward(n).start()

    def z_wait(self):
        @pl.when(self.me.outer == 1)
        def _():
            for n in range(2):
                self.onward(n).wait_recv()

        self.near().wait_recv()

    def y_copy(self):
        me = self.me
        place = self.view(me.z if self.early else slice(None), me.y, me.t)
        return rcopy(self.own if self.early else place, place, self.ys, self.yr, me.over_y)

    def x_copy(self):
        me = self.me
        place = self.view(slice(None), slice(None), me.t)
        return rcopy(place, place, self.xs, self.xr, me.over_t)

    def c_copy(self):
        return rcopy(self.pair(), self.pair(), self.cs, self.cr, self.me.over_c)

    def finish(self):
        self.near().wait_send()
        self.far().wait_send()

        @pl.when(self.me.outer == 0)
        def _():
            for n in range(2):
                self.onward(n).wait_send()

        self.y_copy().wait_send()
        if self.wide:
            self.x_copy().wait_send()
        self.c_copy().wait_send()


def pass_sems(*lead):
    dma = pltpu.SemaphoreType.DMA
    return [dma(lead + (2,)), dma(lead + (3,)), dma(lead + (2,))] + [dma(lead or (1,))] * 6


def fwd_kernel(deep, x_sh, mask_sh, qkv_sh, out_sh, in_sh, hid_sh, bin_sh, bias, bqv,
               attn_o, q_o, k_o, v_o, lse_o, x_o, mask_o, qkv_o, out_o, in_o, hid_o, bin_o,
               x_v, w_v, m_v, q_v, k_v, v_v, a_v, lse_v,
               loc, xs, xr, as_, ar, *sems):
    me = Place(deep)
    Z = me.Z
    y, c, z, t = me.y, me.c, me.z, me.t
    half = x_sh.shape[0]
    seq, width = x_v.shape
    pairs = q_v.shape[0]
    heads = 2 * pairs
    q_sems, m_sems, w_sems = sems[0:9], sems[9:18], sems[18:27]

    def cols(n):
        return pl.ds(pl.multiple_of(t * n, 128), n)

    rows_own = pl.ds(pl.multiple_of(t * half, 128), half)
    rows_other = pl.ds(pl.multiple_of((1 - t) * half, 128), half)

    P_Q = Pass(me, qkv_sh, lambda zs, ys, ts: w_v.at[zs, ys, c], lambda: w_v.at[:, :, c],
               list(q_sems[:3]) + [s.at[0] for s in q_sems[3:]])

    def M(h):
        return Pass(me, mask_sh.at[h], lambda zs, ys, ts: m_v.at[h, zs, ys, c], lambda: m_v.at[h, :, :, c],
                    [s.at[h] for s in m_sems])

    def W(k, shard, whole, early):
        n = shard.shape[1]

        def view(zs, ys, ts):
            return whole.at[zs, ys, c, :, pl.ds(pl.multiple_of(ts * n, 128), n)]

        return Pass(me, shard, view, lambda: whole.at[:, :, c], [s.at[k] for s in w_sems], early, True)

    WO, WI, WH = W(0, out_sh, out_o, False), W(1, in_sh, in_o, True), W(2, hid_sh, hid_o, False)

    locals_ = [
        pltpu.make_async_copy(qkv_sh, w_v.at[z, y, c], loc.at[0]),
        pltpu.make_async_copy(x_sh, x_v.at[rows_own], loc.at[1]),
        pltpu.make_async_copy(mask_sh, m_v.at[:, z, y, c], loc.at[2]),
        pltpu.make_async_copy(bin_sh, bin_o.at[t], loc.at[3]),
    ] + [pltpu.make_async_copy(w.own, w.view(z, y, t), loc.at[4 + k]) for k, w in enumerate((WO, WI, WH))]
    for cp in locals_:
        cp.start()
    me.greet()

    def x_copy():
        return rcopy(x_sh, x_v.at[rows_own], xs.at[0], xr.at[0], me.over_t)

    def b_copy():
        return rcopy(bin_sh, bin_o.at[t], xs.at[1], xr.at[1], me.over_t)

    def a_cols(p):
        return pl.ds(pl.multiple_of(t * (pairs * 128) + p * 128, 128), 128)

    def a_copy(p):
        return rcopy(a_v.at[p, rows_other], attn_o.at[:, a_cols(p)], as_.at[p], ar.at[p], me.over_t)

    def a_local(p):
        return pltpu.make_async_copy(a_v.at[p, rows_own], attn_o.at[:, a_cols(p)], loc.at[7 + p])

    def mask_save(h):
        return pltpu.make_async_copy(m_v.at[h], mask_o.at[h], loc.at[10 + h])

    P_Q.z_start()
    WI.y_copy().start()
    x_copy().start()
    b_copy().start()
    M(0).z_start()
    for cp in locals_:
        cp.wait()
    P_Q.relay()
    P_Q.z_wait()
    P_Q.y_copy().start()
    WH.z_start()
    M(0).relay()
    M(0).z_wait()
    M(0).y_copy().start()
    WI.y_copy().wait_recv()
    WI.z_start()
    WH.relay()
    WH.z_wait()
    WH.y_copy().start()
    M(1).z_start()
    P_Q.y_copy().wait_recv()
    P_Q.c_copy().start()
    x_copy().wait_recv()
    P_Q.c_copy().wait_recv()

    step = half // 2

    def project(r, carry):
        rows = pl.ds(pl.multiple_of(r * step, step), step)
        xb = x_v[rows, :]
        for j, dst in enumerate((q_v, k_v, v_v)):
            w = w_v[:, :, :, j].reshape(width, pairs * 128)
            acc = dot(xb, w)
            if j == 0:
                acc = acc + bqv[0:1, :]
            elif j == 2:
                acc = acc + bqv[1:2, :]
            out = acc.astype(BF)
            if j == 0:
                out = out * jnp.asarray(0.125, BF)
            for p in range(pairs):
                dst[p, rows, :] = out[:, p * 128:(p + 1) * 128]
        return carry

    lax.fori_loop(0, seq // step, project, 0)
    outs = [
        pltpu.make_async_copy(q_v, q_o, loc.at[0]),
        pltpu.make_async_copy(k_v, k_o, loc.at[1]),
        pltpu.make_async_copy(v_v, v_o, loc.at[2]),
        pltpu.make_async_copy(x_v, x_o, loc.at[3]),
        pltpu.make_async_copy(w_v, qkv_o, loc.at[4]),
    ]
    for cp in outs:
        cp.start()
    blk = seq // Z

    def attend(p, u):
        h = 2 * p + u
        sl = slice(64 * u, 64 * u + 64)

        def rows_of(b, carry):
            rows = pl.ds(pl.multiple_of(b * blk, blk), blk)
            s = dot_t(q_v[p, rows, sl], k_v[p, :, sl])
            s = s + m_v[h, b].reshape(blk, seq).astype(F32) + bias[...]
            top = jnp.max(s, axis=-1, keepdims=True)
            e = jnp.exp(s - top)
            total = jnp.sum(e, axis=-1, keepdims=True)
            o = dot(e.astype(BF), v_v[p, :, sl])
            a_v[p, rows, sl] = (o / total).astype(BF)
            lse_v[p, rows, u:u + 1] = top + jnp.log(total)
            return carry

        lax.fori_loop(0, Z, rows_of, 0)

    def with_0():
        M(1).relay()
        M(1).z_wait()
        M(1).y_copy().start()
        M(2).z_start()

    def with_1():
        M(3).z_start()

    def with_2():
        pass

    def with_3():
        WI.x_copy().wait_recv()
        WI.c_copy().start()

    def with_4():
        WH.x_copy().wait_recv()
        WH.c_copy().start()

    def with_5():
        WO.y_copy().wait_recv()
        WO.x_copy().start()

    def ahead_0():
        pass

    def ahead_1():
        WI.relay()
        WI.z_wait()
        WI.x_copy().start()
        WH.y_copy().wait_recv()
        WH.x_copy().start()
        M(2).relay()
        M(2).z_wait()
        M(2).y_copy().start()

    def ahead_2():
        M(3).relay()
        M(3).z_wait()
        M(3).y_copy().start()
        M(4).z_start()
        WO.z_start()

    def ahead_3():
        M(4).relay()
        M(4).z_wait()
        M(4).y_copy().start()
        M(5).z_start()

    def ahead_4():
        WO.relay()
        WO.z_wait()
        WO.y_copy().start()
        M(5).relay()
        M(5).z_wait()
        M(5).y_copy().start()

    def ahead_5():
        pass

    ahead = (ahead_0, ahead_1, ahead_2, ahead_3, ahead_4, ahead_5)
    beside = (with_0, with_1, with_2, with_3, with_4, with_5)

    def pair_step(p, carry):
        for u in range(2):
            h = 2 * p + u
            for n in range(pairs):
                pl.when(p == n)(ahead[2 * n + u])
            M(h).y_copy().wait_recv()
            M(h).c_copy().start()
            for n in range(pairs):
                pl.when(p == n)(beside[2 * n + u])
            M(h).c_copy().wait_recv()
            mask_save(h).start()
            attend(p, u)
        a_copy(p).start()
        a_local(p).start()
        return carry

    lax.fori_loop(0, pairs, pair_step, 0)
    lse_out = pltpu.make_async_copy(lse_v, lse_o, loc.at[5])
    lse_out.start()
    WO.x_copy().wait_recv()
    WO.c_copy().start()
    for cp in outs + [lse_out]:
        cp.wait()
    for p in range(pairs):
        a_local(p).wait()
        a_copy(p).wait()
    b_copy().wait()
    x_copy().wait_send()
    P_Q.finish()
    for h in range(heads):
        M(h).finish()
        mask_save(h).wait()
    for w in (WO, WI, WH):
        w.finish()
        w.c_copy().wait_recv()


def forward(deep, x, mask, qkv, w_out_t, w_in, w_hid_t, b_in, bias, b_qv):
    half, width = x.shape
    seq = 2 * half
    heads, blk, _ = mask.shape
    pairs = heads // 2
    Z, Y, C = deep // 4, 2, 2
    n_out, n_in = w_out_t.shape[1], w_in.shape[1]
    r = w_in.shape[0]
    sd = jax.ShapeDtypeStruct
    dma = pltpu.SemaphoreType.DMA
    out_shape = (
        sd((half, 2 * pairs * 128), BF),
        sd((pairs, seq, 128), BF), sd((pairs, seq, 128), BF), sd((pairs, seq, 128), BF),
        sd((pairs, seq, 128), F32),
        sd((seq, width), BF),
        sd((heads, Z, Y, C, blk, seq), BF),
        sd((Z, Y, C) + qkv.shape, BF),
        sd((Z, Y, C, r, 2 * n_out), BF), sd((Z, Y, C, r, 2 * n_in), BF), sd((Z, Y, C, r, 2 * n_in), BF),
        sd((2,) + b_in.shape, F32),
    )
    return pl.pallas_call(
        functools.partial(fwd_kernel, deep),
        out_shape=out_shape,
        in_specs=[ANY] * 7 + [VM, VM],
        out_specs=[ANY] * len(out_shape),
        scratch_shapes=[
            pltpu.VMEM((seq, width), BF),
            pltpu.VMEM((Z, Y, C) + qkv.shape, BF),
            pltpu.VMEM((heads, Z, Y, C, blk, seq), BF),
            pltpu.VMEM((pairs, seq, 128), BF), pltpu.VMEM((pairs, seq, 128), BF), pltpu.VMEM((pairs, seq, 128), BF),
            pltpu.VMEM((pairs, seq, 128), BF),
            pltpu.VMEM((pairs, seq, 128), F32),
            dma((16,)), dma((2,)), dma((2,)), dma((pairs,)), dma((pairs,)),
            *pass_sems(), *pass_sems(heads), *pass_sems(3),
        ],
        compiler_params=pltpu.CompilerParams(collective_id=1, has_side_effects=True, vmem_limit_bytes=58 << 20),
        name="forward_attention",
    )(x, mask, qkv, w_out_t, w_in, w_hid_t, b_in, bias, b_qv)


class Fold:
    def __init__(self, me, near_part, far_part, lc, bufs, sems, final, lx=None, early=False, cols=None):
        self.me, self.own, self.away, self.lc = me, near_part, far_part, lc
        self.ly, self.lz, self.lr = bufs
        self.s, self.r = sems
        self.final, self.lx, self.early, self.cols = final, lx, early, cols

    def base(self):
        return self.lc if self.lx is None else self.lx

    def c_copy(self):
        return rcopy(self.away, self.lc, self.s(0), self.r(0), self.me.over_c)

    def c_add(self):
        self.c_copy().wait_recv()

        def one(i, carry):
            for j in range(self.me.Y):
                self.lc[i, j] = self.lc[i, j] + self.own(i, j)
            return carry

        lax.fori_loop(0, self.me.Z, one, 0)

    def x_copy(self):
        me = self.me
        return rcopy(self.lc.at[:, :, :, self.cols(1 - me.t)], self.lx, self.s(1), self.r(1), me.over_t)

    def x_add(self):
        self.x_copy().wait_recv()
        at = self.cols(self.me.t)

        def one(i, carry):
            for j in range(self.me.Y):
                self.lx[i, j] = self.lx[i, j] + self.lc[i, j, :, at]
            return carry

        lax.fori_loop(0, self.me.Z, one, 0)

    def y_copy(self):
        me = self.me
        src = self.base().at[me.z, 1 - me.y] if self.early else self.base().at[:, 1 - me.y]
        return rcopy(src, self.ly, self.s(2), self.r(2), me.over_y)

    def y_add(self):
        self.y_copy().wait_recv()
        base, y = self.base(), self.me.y

        def one(i, carry):
            self.ly[i] = self.ly[i] + base[i, y]
            return carry

        lax.fori_loop(0, self.me.Z, one, 0)

    def along(self):
        return self.base() if self.early else self.ly

    def near(self):
        me = self.me
        return rcopy(self.along().at[me.z_near], self.lz.at[0], self.s(3), self.r(3), me.dev(z=me.z_near))

    def through(self, n):
        me = self.me
        place = self.along().at[me.z_far_inner if n == 0 else me.z_far_outer]
        return rcopy(place, self.lr.at[n], self.s(4 + n), self.r(4 + n), me.dev(z=me.z_near))

    def onward(self, n):
        me = self.me
        z = me.z_far_inner if n == 0 else me.z_far_outer
        return rcopy(self.along().at[z], self.lz.at[1], self.s(6 + n), self.r(6), me.dev(z=z))

    def z_start(self):
        @pl.when(self.me.outer == 1)
        def _():
            for n in range(2):
                self.through(n).start()

        self.near().start()

    def relay(self):
        me = self.me

        @pl.when(me.outer == 0)
        def _():
            for n in range(2):
                self.through(n).wait_recv()
                z = me.z_far_inner if n == 0 else me.z_far_outer
                self.along()[z] = self.along()[z] + self.lr[n]
                self.onward(n).start()

    def z_sum(self):
        self.near().wait_recv()
        self.onward(0).wait_recv()
        total = self.along()[self.me.z].astype(F32) + self.lz[0].astype(F32)
        return total + self.lz[1].astype(F32)

    def z_end(self):
        self.final(self.z_sum())

    def early_z_end(self):
        self.base()[self.me.z] = self.z_sum().astype(BF)
        self.y_copy().start()

    def early_y_end(self):
        self.y_copy().wait_recv()
        self.final(self.base()[self.me.z, self.me.y].astype(F32) + self.ly[...].astype(F32))

    def finish(self, skip_c=False):
        if not skip_c:
            self.c_copy().wait_send()
        if self.lx is not None:
            self.x_copy().wait_send()
        self.y_copy().wait_send()
        self.near().wait_send()

        @pl.when(self.me.outer == 1)
        def _():
            for n in range(2):
                self.through(n).wait_send()

        @pl.when(self.me.outer == 0)
        def _():
            for n in range(2):
                self.onward(n).wait_send()


def bwd_kernel(deep, dat, q_h, k_h, v_h, mask_h, lse_h, x_h, qkv_h, hid_h, in_h, out_h, dz1_h, sg_h, small_h, bias,
               dx_o, gqkv_o, ghid_o, gin_o, gout_o, gmask_o, small_o,
               q_v, k_v, v_v, do_v, lse_v, m_v, p_v, dq_v, dk_v, dv_v, acck, accv,
               lc_m, ly_m, lz_m, lr_m, gm_v,
               own_w, lc_hid, lx_hid, ly_hid, lz_hid, lr_hid, lc_in, lx_in, ly_in, lz_in, lr_in, lc_out, lx_out, ly_out, lz_out, lr_out,
               fin_hid, fin_in, fin_out,
               p_q, lc_q, ly_q, lz_q, lr_q, fin_q,
               x_v, w_v, sx_v, lx_x, dx_v, dz_v,
               s_v, sc_v, sy_v, sz_v, sx2_v,
               loc, msem, ds_, dr, wl, w_s, w_r, m_s, m_r, q_s, q_r, xs, xr, s1s, s1r, szs, szr):
    me = Place(deep)
    Z, y, c, z, t = me.Z, me.y, me.c, me.z, me.t
    pairs, seq, _ = q_v.shape
    heads = 2 * pairs
    half = seq // 2
    width = x_v.shape[1]
    zs = range(1, Z)
    rows_own = pl.ds(pl.multiple_of(t * half, 128), half)

    def dat_cols(p, who):
        return pl.ds(pl.multiple_of(who * (pairs * 128) + p * 128, 128), 128)

    def dat_local(p):
        return pltpu.make_async_copy(dat.at[:, dat_cols(p, t)], do_v.at[p, rows_own], loc.at[p])

    def dat_copy(p):
        return rcopy(dat.at[:, dat_cols(p, 1 - t)], do_v.at[p, rows_own], ds_.at[p], dr.at[p], me.over_t)

    loads = [pltpu.make_async_copy(a, b, loc.at[3 + n]) for n, (a, b) in enumerate((
        (q_h, q_v), (k_h, k_v), (v_h, v_v), (lse_h, lse_v), (x_h, x_v), (qkv_h, w_v), (dz1_h, dz_v), (small_h, s_v.at[pl.ds(0, small_h.shape[0])])))]

    def m_load(h, slot):
        return pltpu.make_async_copy(mask_h.at[h], m_v.at[slot], msem.at[slot])

    def sg_load(h):
        return pltpu.make_async_copy(sg_h.at[h], gm_v.at[h], loc.at[11 + h])

    def gm_save(h):
        return pltpu.make_async_copy(gm_v.at[h], gmask_o.at[h], loc.at[17 + h])

    def M(h, slot=None):
        def own(i, j):
            return p_v[slot, i, j, c]

        def final(total):
            sg_load(h).wait()
            gm_v[h] = total * gm_v[h]
            gm_save(h).start()

        away = None if slot is None else p_v.at[slot, :, :, 1 - c]
        return Fold(me, own, p_v.at[0, :, :, 1 - c] if away is None else away, lc_m.at[h],
                    (ly_m.at[h], lz_m.at[h], lr_m.at[h]), (lambda n: m_s.at[h, n], lambda n: m_r.at[h, n]), final)

    def W(k, part, lc, lx, ly, lz, lr, fin, out, early):
        n = lx.shape[-1]

        def own(i, j):
            return own_w[i, j, :, 0:2 * n]

        def final(total):
            fin[...] = total
            pltpu.make_async_copy(fin, out, wl.at[3 + k]).start()

        fold = Fold(me, own, part.at[:, :, 1 - c], lc, (ly, lz, lr), (lambda i: w_s.at[k, i], lambda i: w_r.at[k, i]), final,
                    lx, early, lambda who: pl.ds(pl.multiple_of(who * n, 128), n))
        fold.own_load = lambda: pltpu.make_async_copy(part.at[:, :, c], own_w.at[:, :, :, pl.ds(0, 2 * n)], wl.at[k])
        fold.saved = lambda: pltpu.make_async_copy(fin, out, wl.at[3 + k])
        return fold

    WH = W(0, hid_h, lc_hid, lx_hid, ly_hid, lz_hid, lr_hid, fin_hid, ghid_o, False)
    WI = W(1, in_h, lc_in, lx_in, ly_in, lz_in, lr_in, fin_in, gin_o, True)
    WO = W(2, out_h, lc_out, lx_out, ly_out, lz_out, lr_out, fin_out, gout_o, False)

    def q_final(total):
        fin_q[...] = total
        pltpu.make_async_copy(fin_q, gqkv_o, loc.at[24]).start()

    Q = Fold(me, lambda i, j: p_q[i, j, c], p_q.at[:, :, 1 - c], lc_q, (ly_q, lz_q, lr_q),
             (lambda n: q_s.at[n], lambda n: q_r.at[n]), q_final)

    def x_copy():
        return rcopy(sx_v, lx_x, xs, xr, me.over_t)

    def s_c():
        return rcopy(s_v, sc_v, s1s.at[0], s1r.at[0], me.over_c)

    def s_y():
        return rcopy(sc_v, sy_v, s1s.at[1], s1r.at[1], me.over_y)

    def s_z(d):
        return rcopy(sy_v, sz_v.at[z], szs.at[d - 1], szr.at[d - 1], me.along_z(d))

    def s_z_in(d):
        return rcopy(sy_v, sz_v.at[me.source_z(d)], szs.at[d - 1], szr.at[d - 1], me.along_z(d))

    def s_x():
        return rcopy(s_v, sx2_v, s1s.at[2], s1r.at[2], me.over_t)

    m_load(0, 0).start()
    for cp in loads[:4]:
        cp.start()
    for p in range(pairs):
        dat_local(p).start()
    WH.own_load().start()
    for cp in loads[4:]:
        cp.start()
    me.greet()
    for p in range(pairs):
        dat_copy(p).start()
    for w in (WH, WI, WO):
        w.c_copy().start()
    for h in range(heads):
        sg_load(h).start()
    for cp in loads:
        cp.wait()

    blk = seq // Z
    shape4 = p_v.shape[2:]

    def attend(p, u, slot):
        sl = slice(64 * u, 64 * u + 64)
        acck[...] = jnp.zeros_like(acck)
        accv[...] = jnp.zeros_like(accv)

        def rows_of(n, carry):
            b = lax.rem(t * (Z // 2) + n, Z)
            if u == 0:
                @pl.when(n == Z // 2)
                def _():
                    dat_copy(p).wait_recv()

            rows = pl.ds(pl.multiple_of(b * blk, blk), blk)
            qb, dob = q_v[p, rows, sl], do_v[p, rows, sl]
            kk, vv = k_v[p, :, sl], v_v[p, :, sl]
            s = dot_t(qb, kk) + m_v[u, b].reshape(blk, seq).astype(F32) + bias[...]
            pr = jnp.exp(s - lse_v[p, rows, u:u + 1])
            dp = dot_t(dob, vv)
            tt = pr * dp
            delta = jnp.sum(tt, axis=-1, keepdims=True)
            dsb = (tt - pr * delta).astype(BF)
            p_v[slot, b] = dsb.reshape(shape4)
            dq_v[p, rows, sl] = (dot(dsb, kk) * 0.125).astype(BF)
            acck[...] += dot_0(dsb, qb)
            accv[...] += dot_0(pr.astype(BF), dob)
            return carry

        lax.fori_loop(0, Z, rows_of, 0)
        dk_v[p, :, sl] = acck[...].astype(BF)
        dv_v[p, :, sl] = accv[...].astype(BF)

    def after_0():
        WH.own_load().wait()
        WH.c_add()
        WI.own_load().start()
        WH.x_copy().start()
        M(0, 0).c_add()
        M(0).y_copy().start()

    def after_1():
        WI.own_load().wait()
        WI.c_add()
        WO.own_load().start()
        WI.x_copy().start()
        M(1, 1).c_add()
        M(1).y_copy().start()

    def after_2():
        WO.own_load().wait()
        WO.c_add()
        WO.x_copy().start()
        M(2, 0).c_add()
        M(2).y_copy().start()
        M(0).y_add()
        M(0).z_start()

    def after_3():
        M(3, 1).c_add()
        M(3).y_copy().start()
        WH.x_add()
        WH.y_copy().start()
        M(0).relay()

    def after_4():
        M(1).y_add()
        M(1).z_start()
        M(4, 0).c_add()
        M(4).y_copy().start()

    def after_5():
        M(1).relay()
        M(2).y_add()
        M(2).z_start()
        M(5, 1).c_add()
        M(5).y_copy().start()

    after = (after_0, after_1, after_2, after_3, after_4, after_5)

    def pair_step(p, carry):
        dat_local(p).wait()
        for u in range(2):
            h = 2 * p + u
            m_load(h, u).wait()
            if u == 0:
                m_load(h + 1, 1).start()
            else:
                @pl.when(p < pairs - 1)
                def _():
                    m_load(h + 1, 0).start()

            @pl.when(p > 0)
            def _():
                M(h - 2, u).c_copy().wait_send()

            attend(p, u, u)
            M(h, u).c_copy().start()
            for n in range(pairs):
                pl.when(p == n)(after[2 * n + u])
        return carry

    lax.fori_loop(0, pairs, pair_step, 0)

    step = half // 2

    def d_cat(ref, rows):
        return jnp.concatenate([ref[p, rows, :] for p in range(pairs)], axis=1)

    def weight(j):
        return w_v[:, :, :, j].reshape(width, pairs * 128)

    def terms(rows):
        acc = dot_t(d_cat(dq_v, rows), weight(0))
        acc = acc + dot_t(d_cat(dk_v, rows), weight(1))
        return acc + dot_t(d_cat(dv_v, rows), weight(2))

    def theirs(r, carry):
        at = pl.ds(pl.multiple_of(r * step, step), step)
        rows = pl.ds(pl.multiple_of((1 - t) * half + r * step, step), step)
        sx_v[at, :] = terms(rows).astype(BF)
        return carry

    lax.fori_loop(0, 2, theirs, 0)
    x_copy().start()

    for j, ref in enumerate((dq_v, dk_v, dv_v)):
        g = dot_0(x_v[...], d_cat(ref, slice(None)))
        p_q[:, :, :, j] = g.astype(BF).reshape(p_q.shape[:3] + p_q.shape[4:])
    Q.c_copy().start()
    M(2).relay()
    base = small_h.shape[0]
    for n, ref in enumerate((dq_v, dv_v)):
        for p in range(pairs):
            at = base + n * pairs + p
            s_v[at:at + 1, :] = jnp.sum(ref[p].astype(F32), axis=0, keepdims=True)
    for at in range(base + 2 * pairs, s_v.shape[0]):
        s_v[at:at + 1, :] = jnp.zeros((1, 128), F32)
    s_c().start()
    Q.c_add()
    Q.y_copy().start()

    def mine(r, carry):
        at = pl.ds(pl.multiple_of(r * step, step), step)
        rows = pl.ds(pl.multiple_of(t * half + r * step, step), step)
        dx_v[at, :] = terms(rows) + dz_v[at, :]
        return carry

    lax.fori_loop(0, 2, mine, 0)
    s_c().wait_recv()
    sc_v[...] = sc_v[...] + s_v[...]
    s_y().start()
    M(3).y_add()
    M(3).z_start()
    WI.x_add()
    WI.z_start()
    M(0).z_end()
    WO.x_add()
    WO.y_copy().start()
    M(3).relay()
    WI.relay()
    WH.y_add()
    WH.z_start()
    M(1).z_end()
    M(2).z_end()
    M(4).y_add()
    M(4).z_start()
    WH.relay()
    WI.early_z_end()
    M(3).z_end()
    M(4).relay()
    M(5).y_add()
    M(5).z_start()
    s_y().wait_recv()
    sy_v[...] = sy_v[...] + sc_v[...]
    sz_v[z] = sy_v[...]
    for d in zs:
        s_z(d).start()
    Q.y_add()
    Q.z_start()
    WH.z_end()
    M(5).relay()
    WO.y_add()
    WO.z_start()
    Q.relay()
    M(4).z_end()
    x_copy().wait_recv()
    dx_v[...] = dx_v[...] + lx_x[...].astype(F32)
    dx_save = pltpu.make_async_copy(dx_v, dx_o, loc.at[23])
    dx_save.start()
    WO.relay()
    for d in zs:
        s_z_in(d).wait_recv()
    s_c().wait_send()
    total = sz_v[0]
    for i in range(1, Z):
        total = total + sz_v[i]
    s_v[...] = total
    s_x().start()
    M(5).z_end()
    WI.early_y_end()
    Q.z_end()
    WO.z_end()
    s_x().wait_recv()
    low = sx2_v[...] + s_v[...]
    row = lax.broadcasted_iota(jnp.int32, low.shape, 0)
    s_y().wait_send()
    sc_v[...] = jnp.where(row < base, low, s_v[...])
    s_save = pltpu.make_async_copy(sc_v, small_o, loc.at[25])
    s_save.start()

    for p in range(pairs):
        dat_copy(p).wait_send()
    for w in (WH, WI, WO):
        w.finish()
        w.saved().wait()
    for h in range(heads):
        M(h).finish(h < heads - 2)
        gm_save(h).wait()
    Q.finish()
    for d in zs:
        s_z(d).wait_send()
    x_copy().wait_send()
    s_x().wait_send()
    dx_save.wait()
    pltpu.make_async_copy(fin_q, gqkv_o, loc.at[24]).wait()
    s_save.wait()


def backward(deep, dat, q, k, v, mask, lse, x, qkv, g_hid, g_in, g_out, dz1, sg, small, bias):
    pairs, seq, _ = q.shape
    half, width = dz1.shape
    heads, Z, Y, C, blk, _ = mask.shape
    r, n2 = g_in.shape[3], g_in.shape[4]
    n2o = g_out.shape[4]
    n, no = n2 // 2, n2o // 2
    base = small.shape[0]
    rows_s = base + 8
    sd = jax.ShapeDtypeStruct
    dma = pltpu.SemaphoreType.DMA
    vm = pltpu.VMEM
    out_shape = (
        sd((half, width), F32), sd(qkv.shape[3:], F32), sd((r, n), F32), sd((r, n), F32), sd((r, no), F32),
        sd((heads, blk, seq), F32), sd((rows_s, 128), F32),
    )
    pair = vm((pairs, seq, 128), BF)

    def chain(m, early):
        last = (Y, r, m) if early else (r, m)
        return [vm((Z, Y, r, 2 * m), BF), vm((Z, Y, r, m), BF), vm((r, m) if early else (Z, r, m), BF), vm((2,) + last, BF), vm((2,) + last, BF)]

    three, rq, nq = qkv.shape[3:]
    return pl.pallas_call(
        functools.partial(bwd_kernel, deep),
        out_shape=out_shape,
        in_specs=[ANY] * 14 + [VM],
        out_specs=[ANY] * len(out_shape),
        scratch_shapes=[
            pair, pair, pair, pair, vm((pairs, seq, 128), F32), vm((2, Z, Y, C, blk, seq), BF), vm((2, Z, Y, C, blk, seq), BF),
            pair, pair, pair, vm((seq, 64), F32), vm((seq, 64), F32),
            vm((heads, Z, Y, blk, seq), BF), vm((heads, Z, blk, seq), BF), vm((heads, 2, blk, seq), BF), vm((heads, 2, blk, seq), BF),
            vm((heads, blk, seq), F32),
            vm((Z, Y, r, n2), BF), *chain(n, False), *chain(n, True), *chain(no, False), vm((r, n), F32), vm((r, n), F32), vm((r, no), F32),
            vm((Z, Y, C, three, rq, nq), BF), vm((Z, Y, three, rq, nq), BF), vm((Z, three, rq, nq), BF),
            vm((2, three, rq, nq), BF), vm((2, three, rq, nq), BF), vm((three, rq, nq), F32),
            vm((seq, width), BF), vm((Z, Y, C, three, rq, nq), BF), vm((half, width), BF), vm((half, width), BF), vm((half, width), F32), vm((half, width), F32),
            vm((rows_s, 128), F32), vm((rows_s, 128), F32), vm((rows_s, 128), F32), vm((Z, rows_s, 128), F32), vm((rows_s, 128), F32),
            dma((26,)), dma((2,)), dma((pairs,)), dma((pairs,)),
            dma((6,)), dma((3, 8)), dma((3, 7)), dma((heads, 8)), dma((heads, 7)), dma((8,)), dma((7,)), dma, dma,
            dma((3,)), dma((3,)), dma((Z - 1,)), dma((Z - 1,)),
        ],
        compiler_params=pltpu.CompilerParams(collective_id=2, has_side_effects=True, vmem_limit_bytes=62 << 20),
        name="backward_attention",
    )(dat, q, k, v, mask, lse, x, qkv, g_hid, g_in, g_out, dz1, sg, small, bias)


NEG = -1e30
EPS = 1e-12


def layer_norm(value_rows, scale_vec, shift_vec):
    centre = value_rows - jnp.mean(value_rows, axis=-1, keepdims=True)
    spread = jnp.mean(centre * centre, axis=-1, keepdims=True)
    return centre * lax.rsqrt(spread + EPS) * scale_vec + shift_vec


def gelu_exact(value_rows):
    return jax.nn.gelu(value_rows, approximate=False)


def matmul(left, right):
    return jnp.dot(left, right, preferred_element_type=jnp.float32)


def times_transposed(left, right):
    return lax.dot_general(
        left, right, (((1,), (1,)), ((), ())), preferred_element_type=jnp.float32
    )


def over_rows(left, right):
    return lax.dot_general(
        left, right, (((0,), (0,)), ((), ())), preferred_element_type=jnp.float32
    )


def plain_body(
    inputs,
    lengths,
    w_qkv,
    b_qv,
    w_out,
    b_out,
    ln1_gain,
    ln1_bias,
    w_in,
    b_in,
    w_hid,
    b_hid,
    ln2_gain,
    ln2_bias,
    mask_logits,
    noise,
    cotangent,
):
    seq_count, half_rows, width = inputs.shape
    slot_len = half_rows * lax.axis_size("tensor")
    tensor_rank = lax.axis_index("tensor")
    head_count = mask_logits.shape[0]
    head_dim = w_qkv.shape[2] // head_count
    scale = head_dim ** (-0.5)
    token_count = seq_count * slot_len
    mixed_logits = mask_logits + noise
    local_mask = jax.nn.log_sigmoid(mixed_logits).astype(jnp.bfloat16)
    full_qkv, full_out, full_in, full_hid, full_mask = (
        lax.all_gather(w_qkv, "dp", axis=1, tiled=True),
        lax.all_gather(w_out, "dp", axis=1, tiled=True),
        lax.all_gather(w_in, "dp", axis=0, tiled=True),
        lax.all_gather(w_hid, "dp", axis=1, tiled=True),
        lax.all_gather(local_mask, "dp", axis=1, tiled=True),
    )
    key_valid = jnp.arange(slot_len, dtype=jnp.int32)[None, :] < lengths[:, None]
    own_rows = tensor_rank * half_rows + jnp.arange(half_rows, dtype=jnp.int32)
    row_valid = (own_rows[None, :] < lengths[:, None]).astype(jnp.float32)
    gathered = lax.all_gather(inputs, "tensor", axis=1, tiled=True)
    flat_rows = gathered.reshape(token_count, width)
    query_rows = (matmul(flat_rows, full_qkv[0]) + b_qv[0]).astype(jnp.bfloat16)
    key_rows = matmul(flat_rows, full_qkv[1]).astype(jnp.bfloat16)
    value_rows = (matmul(flat_rows, full_qkv[2]) + b_qv[1]).astype(jnp.bfloat16)

    def split_heads(matrix):
        return matrix.reshape(seq_count, slot_len, head_count, head_dim).transpose(0, 2, 1, 3)

    def join_heads(stacked):
        return stacked.transpose(0, 2, 1, 3).reshape(token_count, head_count * head_dim)

    def masked_scores(query_h, keys_h, mask_h, valid_keys):
        score_matrix = (
            jnp.einsum("qd,kd->qk", query_h, keys_h, preferred_element_type=jnp.float32) * scale
        )
        score_matrix = score_matrix + mask_h.astype(jnp.float32)
        return jnp.where(valid_keys[None, :], score_matrix, NEG)

    def attend_sequence(operands):
        query_s, keys_s, values_s, valid_keys = operands

        def attend_head(head_ops):
            query_h, keys_h, values_h, mask_h = head_ops
            score_matrix = masked_scores(query_h, keys_h, mask_h, valid_keys)
            top_score = jnp.max(score_matrix, axis=-1, keepdims=True)
            expo = jnp.exp(score_matrix - top_score)
            row_total = jnp.sum(expo, axis=-1, keepdims=True)
            attention_probabilities = (expo / row_total).astype(jnp.bfloat16)
            result = jnp.einsum(
                "qk,kd->qd", attention_probabilities, values_h, preferred_element_type=jnp.float32
            )
            return (result.astype(jnp.bfloat16), (top_score + jnp.log(row_total))[:, 0])

        return lax.map(attend_head, (query_s, keys_s, values_s, full_mask))

    head_out, log_total = lax.map(
        attend_sequence,
        (split_heads(query_rows), split_heads(key_rows), split_heads(value_rows), key_valid),
    )
    attn = join_heads(head_out)
    attn_terms = matmul(attn, full_out).reshape(seq_count, slot_len, width)
    attn_part = lax.psum_scatter(attn_terms, "tensor", scatter_dimension=1, tiled=True)
    first_sum = inputs.astype(jnp.float32) + attn_part + b_out
    hidden_one = layer_norm(first_sum, ln1_gain, ln1_bias)
    hidden_rows = lax.all_gather(
        hidden_one.astype(jnp.bfloat16), "tensor", axis=1, tiled=True
    ).reshape(token_count, width)
    pre_act = matmul(hidden_rows, full_in) + b_in
    activated = gelu_exact(pre_act).astype(jnp.bfloat16)
    ffn_terms = matmul(activated, full_hid).reshape(seq_count, slot_len, width)
    ffn_part = lax.psum_scatter(ffn_terms, "tensor", scatter_dimension=1, tiled=True)
    second_sum = hidden_one + ffn_part + b_hid
    outputs = layer_norm(second_sum, ln2_gain, ln2_bias).astype(jnp.bfloat16)
    back_qkv, back_out, back_in, back_hid, back_mask = (
        lax.all_gather(w_qkv, "dp", axis=1, tiled=True),
        lax.all_gather(w_out, "dp", axis=1, tiled=True),
        lax.all_gather(w_in, "dp", axis=0, tiled=True),
        lax.all_gather(w_hid, "dp", axis=1, tiled=True),
        lax.all_gather(local_mask, "dp", axis=1, tiled=True),
    )
    grad_output = cotangent * row_valid[:, :, None]
    _, pull_second = jax.vjp(layer_norm, second_sum, ln2_gain, ln2_bias)
    grad_second, ln2_gain_part, ln2_bias_part = pull_second(grad_output)
    b_hid_part = jnp.sum(grad_second, axis=(0, 1))
    second_rows = lax.all_gather(
        grad_second.astype(jnp.bfloat16), "tensor", axis=1, tiled=True
    ).reshape(token_count, width)
    w_hid_grad = over_rows(activated, second_rows)
    grad_act = times_transposed(second_rows, back_hid)
    _, pull_gelu = jax.vjp(gelu_exact, pre_act)
    grad_pre = pull_gelu(grad_act)[0].astype(jnp.bfloat16)
    b_in_part = jnp.sum(grad_pre.astype(jnp.float32), axis=0)
    w_in_grad = over_rows(hidden_rows, grad_pre)
    hidden_terms = times_transposed(grad_pre, back_in).reshape(seq_count, slot_len, width)
    grad_hidden = grad_second + lax.psum_scatter(
        hidden_terms, "tensor", scatter_dimension=1, tiled=True
    )
    _, pull_first = jax.vjp(layer_norm, first_sum, ln1_gain, ln1_bias)
    grad_first, ln1_gain_part, ln1_bias_part = pull_first(grad_hidden)
    b_out_part = jnp.sum(grad_first, axis=(0, 1))
    first_rows = lax.all_gather(
        grad_first.astype(jnp.bfloat16), "tensor", axis=1, tiled=True
    ).reshape(token_count, width)
    w_out_grad = over_rows(attn, first_rows)
    grad_attn = times_transposed(first_rows, back_out).astype(jnp.bfloat16)

    def sequence_back(mask_acc, operands):
        query_s, keys_s, values_s, grad_s, total_s, valid_keys = operands

        def head_back(head_ops):
            query_h, keys_h, values_h, mask_h, grad_h, total_h = head_ops
            score_matrix = masked_scores(query_h, keys_h, mask_h, valid_keys)
            attention_probabilities = jnp.exp(score_matrix - total_h[:, None])
            grad_probs = jnp.einsum(
                "qd,kd->qk", grad_h, values_h, preferred_element_type=jnp.float32
            )
            centre = jnp.sum(attention_probabilities * grad_probs, axis=-1, keepdims=True)
            grad_scores = (attention_probabilities * (grad_probs - centre)).astype(jnp.bfloat16)
            grad_q = (
                jnp.einsum("qk,kd->qd", grad_scores, keys_h, preferred_element_type=jnp.float32)
                * scale
            ).astype(jnp.bfloat16)
            grad_k = (
                jnp.einsum("qk,qd->kd", grad_scores, query_h, preferred_element_type=jnp.float32)
                * scale
            ).astype(jnp.bfloat16)
            grad_v = jnp.einsum(
                "qk,qd->kd",
                attention_probabilities.astype(jnp.bfloat16),
                grad_h,
                preferred_element_type=jnp.float32,
            ).astype(jnp.bfloat16)
            return (grad_q, grad_k, grad_v, grad_scores)

        grad_q, grad_k, grad_v, grad_sc = lax.map(
            head_back, (query_s, keys_s, values_s, back_mask, grad_s, total_s)
        )
        return (mask_acc + grad_sc.astype(jnp.float32), (grad_q, grad_k, grad_v))

    mask_zero = jnp.zeros(back_mask.shape, jnp.float32)
    mask_grad, (heads_q, heads_k, heads_v) = lax.scan(
        sequence_back,
        mask_zero,
        (
            split_heads(query_rows),
            split_heads(key_rows),
            split_heads(value_rows),
            split_heads(grad_attn),
            log_total,
            key_valid,
        ),
    )
    query_grad = join_heads(heads_q)
    keys_grad = join_heads(heads_k)
    values_grad = join_heads(heads_v)
    b_qv_part = jnp.stack(
        [
            jnp.sum(query_grad.astype(jnp.float32), axis=0),
            jnp.sum(values_grad.astype(jnp.float32), axis=0),
        ]
    )
    w_qkv_grad = jnp.stack(
        [
            over_rows(flat_rows, query_grad),
            over_rows(flat_rows, keys_grad),
            over_rows(flat_rows, values_grad),
        ]
    )
    input_terms = (
        times_transposed(query_grad, back_qkv[0])
        + times_transposed(keys_grad, back_qkv[1])
        + times_transposed(values_grad, back_qkv[2])
    ).reshape(seq_count, slot_len, width)
    input_grad = grad_first + lax.psum_scatter(
        input_terms.astype(jnp.bfloat16), "tensor", scatter_dimension=1, tiled=True
    ).astype(jnp.float32)
    qkv_total, out_total, in_total, hid_total, mask_total = (
        lax.psum_scatter(w_qkv_grad, "dp", scatter_dimension=1, tiled=True),
        lax.psum_scatter(w_out_grad, "dp", scatter_dimension=1, tiled=True),
        lax.psum_scatter(w_in_grad, "dp", scatter_dimension=0, tiled=True),
        lax.psum_scatter(w_hid_grad, "dp", scatter_dimension=1, tiled=True),
        lax.psum_scatter(mask_grad, "dp", scatter_dimension=1, tiled=True),
    )
    mask_logit_grad = mask_total * jax.nn.sigmoid(-mixed_logits)
    ln1_gain_total, ln1_bias_total, ln2_gain_total, ln2_bias_total, b_out_total, b_hid_total = (
        lax.psum(
            (ln1_gain_part, ln1_bias_part, ln2_gain_part, ln2_bias_part, b_out_part, b_hid_part),
            ("dp", "tensor"),
        )
    )
    b_qv_total, b_in_total = lax.psum((b_qv_part, b_in_part), "dp")
    return (
        outputs,
        input_grad,
        qkv_total,
        b_qv_total,
        out_total,
        b_out_total,
        ln1_gain_total,
        ln1_bias_total,
        in_total,
        b_in_total,
        hid_total,
        b_hid_total,
        ln2_gain_total,
        ln2_bias_total,
        mask_logit_grad,
    )


def norm_stats(rows):
    centre = rows - jnp.mean(rows, axis=-1, keepdims=True)
    scale = lax.rsqrt(jnp.mean(centre * centre, axis=-1, keepdims=True) + EPS)
    return centre * scale, scale


def norm_back(e, hat, scale):
    return (e - jnp.mean(e, axis=-1, keepdims=True) - hat * jnp.mean(e * hat, axis=-1, keepdims=True)) * scale


def body(
    inputs, lengths, w_qkv, b_qv, w_out, b_out, ln1_gain, ln1_bias, w_in, b_in, w_hid, b_hid,
    ln2_gain, ln2_bias, mask_logits, noise, cotangent,
):
    deep = lax.axis_size("dp")
    x = inputs[0]
    half, width = x.shape
    seq = 2 * half
    t = lax.axis_index("tensor")
    length = lengths[0]
    mixed = mask_logits + noise
    mask = jax.nn.log_sigmoid(mixed).astype(BF)
    gate = jax.nn.sigmoid(-mixed)
    bias = jnp.where(jnp.arange(seq, dtype=jnp.int32) < length, 0.0, NEG).astype(F32)[None]
    attn, q, k, v, lse, x_all, mask_all, qkv_all, out_all, in_all, hid_all, bin_all = forward(
        deep, x, mask, w_qkv, w_out.T, w_in, w_hid.T, b_in[None], bias, b_qv)
    w_out_t = out_all.reshape(width, -1)
    w_in_all = in_all.reshape(width, -1)
    w_hid_t = hid_all.reshape(width, -1)

    z1 = x.astype(F32) + dot_t(attn, w_out_t) + b_out
    hat1, scale1 = norm_stats(z1)
    h1 = hat1 * ln1_gain + ln1_bias
    h1b = h1.astype(BF)
    pre = dot(h1b, w_in_all) + bin_all.reshape(-1)
    act = gelu_exact(pre).astype(BF)
    z2 = h1 + dot_t(act, w_hid_t) + b_hid
    hat2, scale2 = norm_stats(z2)
    outputs = (hat2 * ln2_gain + ln2_bias).astype(BF)

    rows = t * half + jnp.arange(half, dtype=jnp.int32)
    dy = cotangent[0] * (rows < length).astype(F32)[:, None]
    dz2 = norm_back(dy * ln2_gain, hat2, scale2)
    dz2b = dz2.astype(BF)
    g_hid = dot_0(dz2b, act).astype(BF)
    _, pull = jax.vjp(gelu_exact, pre)
    dpre = pull(dot(dz2b, w_hid_t))[0].astype(BF)
    g_in = dot_0(h1b, dpre).astype(BF)
    dh1 = dz2 + dot_t(dpre, w_in_all)
    dz1 = norm_back(dh1 * ln1_gain, hat1, scale1)
    dz1b = dz1.astype(BF)
    g_out = dot_0(dz1b, attn).astype(BF)
    dattn = dot(dz1b, w_out_t).astype(BF)

    sums = [
        jnp.sum(dh1 * hat1, axis=0), jnp.sum(dh1, axis=0), jnp.sum(dy * hat2, axis=0), jnp.sum(dy, axis=0),
        jnp.sum(dz1, axis=0), jnp.sum(dz2, axis=0), jnp.sum(dpre.astype(F32), axis=0),
    ]
    flat = jnp.concatenate(sums).reshape(-1, 128)
    filled = flat.shape[0]
    small = jnp.pad(flat, ((0, -filled % 8), (0, 0)))

    dx, gqkv, ghid, gin, gout, gmask, total = backward(
        deep, dattn, q, k, v, mask_all, lse, x_all, qkv_all,
        g_hid.reshape(hid_all.shape), g_in.reshape(in_all.shape), g_out.reshape(out_all.shape), dz1, gate, small, bias)
    vec = total[:6 * width // 128].reshape(6, width)
    g_bin = lax.dynamic_slice_in_dim(total[6 * width // 128:filled].reshape(-1), t * b_in.shape[0], b_in.shape[0])
    g_bqv = total[small.shape[0]:small.shape[0] + 2 * b_qv.shape[1] // 128].reshape(b_qv.shape)
    return (
        outputs[None], dx[None], gqkv, g_bqv, gout.T, vec[4], vec[0], vec[1], gin, g_bin, ghid.T, vec[5],
        vec[2], vec[3], gmask,
    )


def solution(mesh):
    placed = (
        P("dp", "tensor", None),
        P("dp"),
        P(None, "dp", "tensor"),
        P(None, "tensor"),
        P("tensor", "dp"),
        P(),
        P(),
        P(),
        P("dp", "tensor"),
        P("tensor"),
        P("tensor", "dp"),
        P(),
        P(),
        P(),
        P("tensor", "dp", None),
        P("tensor", "dp", None),
        P("dp", "tensor", None),
    )

    def run(*args):
        w_rows, m_rows = args[8].shape[0], args[14].shape[1]
        tiled = w_rows % 16 == 0 and m_rows % 16 == 0 and args[0].shape[0] == 1 and mesh.shape["dp"] == 16
        return (body if tiled else plain_body)(*args)

    return jax.shard_map(
        run,
        mesh=mesh,
        in_specs=placed,
        out_specs=(
            P("dp", "tensor", None),
            P("dp", "tensor", None),
            P(None, "dp", "tensor"),
            P(None, "tensor"),
            P("tensor", "dp"),
            P(),
            P(),
            P(),
            P("dp", "tensor"),
            P("tensor"),
            P("tensor", "dp"),
            P(),
            P(),
            P(),
            P("tensor", "dp", None),
        ),
        check_vma=False,
    )
```

```python
import functools

import jax
import jax.numpy as jnp
from jax import lax
from jax.experimental import pallas as pl
from jax.experimental.pallas import tpu as pltpu
from jax.sharding import PartitionSpec as P

MESH = pl.DeviceIdType.MESH
BF, F32 = jnp.bfloat16, jnp.float32
ANY = pl.BlockSpec(memory_space=pl.ANY)
VM = pl.BlockSpec(memory_space=pltpu.VMEM)


class Place:
    def __init__(self, deep):
        self.Z, self.Y, self.C = deep // 4, 2, 2
        i = lax.axis_index("dp")
        self.t = lax.axis_index("tensor")
        self.c = lax.rem(i, 2)
        self.y = lax.rem(i // 2, 2)
        self.z = i // 4
        far = self.z // 2
        self.outer = 1 - lax.rem(self.z + far, 2)
        self.z_near = self.z + 1 - 2 * lax.rem(self.z, 2)
        self.z_far_inner = 2 - far
        self.z_far_outer = 3 - 3 * far

    def dev(self, z=None, y=None, c=None, t=None):
        z = self.z if z is None else z
        y = self.y if y is None else y
        c = self.c if c is None else c
        t = self.t if t is None else t
        return ((z * self.Y + y) * self.C + c, t)

    def along_z(self, d):
        return self.dev(z=lax.rem(self.z + d, self.Z))

    def source_z(self, d):
        return lax.rem(self.z - d + self.Z, self.Z)

    @property
    def over_y(self):
        return self.dev(y=1 - self.y)

    @property
    def over_c(self):
        return self.dev(c=1 - self.c)

    @property
    def over_t(self):
        return self.dev(t=1 - self.t)

    def greet(self):
        bar = pltpu.get_barrier_semaphore()
        peers = [self.along_z(d) for d in range(1, self.Z)] + [self.over_y, self.over_c, self.over_t]
        for p in peers:
            pl.semaphore_signal(bar, inc=1, device_id=p, device_id_type=MESH)
        pl.semaphore_wait(bar, len(peers))


def rcopy(src, dst, ssem, rsem, dev):
    return pltpu.make_async_remote_copy(src_ref=src, dst_ref=dst, send_sem=ssem, recv_sem=rsem, device_id=dev, device_id_type=MESH)


def dot(a, b):
    return jnp.dot(a, b, preferred_element_type=F32)


def dot_t(a, b):
    return lax.dot_general(a, b, (((1,), (1,)), ((), ())), preferred_element_type=F32)


def dot_0(a, b):
    return lax.dot_general(a, b, (((0,), (0,)), ((), ())), preferred_element_type=F32)


def norm_stats(rows):
    centre = rows - jnp.mean(rows, axis=-1, keepdims=True)
    scale = lax.rsqrt(jnp.mean(centre * centre, axis=-1, keepdims=True) + EPS)
    return centre * scale, scale


def norm_back(e, hat, scale):
    return (e - jnp.mean(e, axis=-1, keepdims=True) - hat * jnp.mean(e * hat, axis=-1, keepdims=True)) * scale


def middle_math(attn, x, wo, wi, wh, b_out, b_in, b_hid, g1, c1, g2, c2, cot, length, first,
                out, dz1, gout, dat, small, hat1_v, s1_v, h1b_v, ht_v, act_v, dg_v, z_v, hat2_v, zt_v,
                put_hid, put_in, ready, turned):
    half, width = hat1_v.shape
    wide = act_v.shape[1]
    rb, step = half // 2, 512

    def by_rows(body):
        def one(r, carry):
            body(pl.ds(pl.multiple_of(r * rb, rb), rb), r)
            return carry

        lax.fori_loop(0, half // rb, one, 0)

    def by_cols(body):
        def one(j, carry):
            body(pl.ds(pl.multiple_of(j * step, step), step), j)
            return carry

        lax.fori_loop(0, wide // step, one, 0)

    def put(n, vec, add):
        for i in range(width // 128):
            at = n * (width // 128) + i
            piece = vec[:, i * 128:(i + 1) * 128]
            small[at:at + 1, :] = small[at:at + 1, :] + piece if add else piece

    small[...] = jnp.zeros_like(small)

    def first_norm(rows, r):
        z1 = x(rows).astype(F32) + dot_t(attn[rows, :], wo()) + b_out[...]
        hat, scale = norm_stats(z1)
        hat1_v[rows, :] = hat
        s1_v[rows, 0:1] = scale
        h1 = hat * g1[...] + c1[...]
        h1b_v[rows, :] = h1.astype(BF)
        z_v[rows, :] = h1 + b_hid[...]

    by_rows(first_norm)

    def up(cols, j):
        pre = dot(h1b_v[...], wi(cols)) + b_in(j)
        phi = jnp.exp(pre * pre * -0.5) * 0.3989422804014327
        cdf = 0.5 + 0.5 * lax.erf(pre * 0.7071067811865476)
        act = (pre * cdf).astype(BF)
        act_v[:, cols] = act
        dg_v[:, cols] = cdf + pre * phi
        z_v[...] += dot_t(act, wh(cols))

    by_cols(up)

    def second_norm(rows, r):
        hat, scale = norm_stats(z_v[rows, :])
        out[rows, :] = (hat * g2[...] + c2[...]).astype(BF)
        at = first + r * rb + lax.broadcasted_iota(jnp.int32, (rb, width), 0)
        dy = jnp.where(at < length, cot[rows, :], 0.0)
        put(2, jnp.sum(dy * hat, axis=0, keepdims=True), True)
        put(3, jnp.sum(dy, axis=0, keepdims=True), True)
        dz2 = norm_back(dy * g2[...], hat, scale)
        put(5, jnp.sum(dz2, axis=0, keepdims=True), True)
        z_v[rows, :] = dz2
        hat2_v[rows, :] = dz2.astype(BF)

    by_rows(second_norm)
    turned()
    zt_v[...] = hat2_v[...].T
    ht_v[...] = h1b_v[...].T
    ready()

    def down(cols, j):
        put_hid(j, dot(zt_v[...], act_v[:, cols]).astype(BF))
        dpre = (dot(hat2_v[...], wh(cols)) * dg_v[:, cols]).astype(BF)
        sums = jnp.sum(dpre.astype(F32), axis=0, keepdims=True)
        for i in range(step // 128):
            small[pl.ds(6 * (width // 128) + j * (step // 128) + i, 1), :] = sums[:, i * 128:(i + 1) * 128]
        put_in(j, dot(ht_v[...], dpre).astype(BF))
        z_v[...] += dot_t(dpre, wi(cols))

    by_cols(down)

    def first_back(rows, r):
        dh1, hat = z_v[rows, :], hat1_v[rows, :]
        put(0, jnp.sum(dh1 * hat, axis=0, keepdims=True), True)
        put(1, jnp.sum(dh1, axis=0, keepdims=True), True)
        d = norm_back(dh1 * g1[...], hat, s1_v[rows, 0:1])
        put(4, jnp.sum(d, axis=0, keepdims=True), True)
        dz1[rows, :] = d
        db = d.astype(BF)
        hat2_v[rows, :] = db
        dat[rows, :] = dot(db, wo()).astype(BF)

    by_rows(first_back)
    zt_v[...] = hat2_v[...].T
    gout[...] = dot(zt_v[...], attn[...]).astype(BF)


class Pass:
    def __init__(self, me, own, view, pair, sems, early=False, wide=False):
        self.me, self.own, self.view, self.pair, self.early, self.wide = me, own, view, pair, early, wide
        self.zs, self.zr, self.fs, self.ys, self.yr, self.xs, self.xr, self.cs, self.cr = sems

    def held(self, z):
        me = self.me
        return self.view(z, slice(None) if self.early else me.y, me.t)

    def source(self):
        return self.held(self.me.z) if self.early else self.own

    def near(self):
        me = self.me
        return rcopy(self.source(), self.held(me.z), self.zs.at[0], self.zr.at[0], me.dev(z=me.z_near))

    def far(self):
        me = self.me
        return rcopy(self.source(), self.held(me.z), self.zs.at[1], self.zr.at[1 + me.outer], me.dev(z=me.z_far_inner))

    def onward(self, n):
        me = self.me
        place = self.held(me.z_far_inner if n == 0 else me.z_far_outer)
        return rcopy(place, place, self.fs.at[n], self.zr.at[1 + n], me.dev(z=me.z_near))

    def z_start(self):
        self.near().start()
        self.far().start()

    def relay(self):
        @pl.when(self.me.outer == 0)
        def _():
            for n in range(2):
                self.onward(n).wait_recv()
                self.onward(n).start()

    def z_wait(self):
        @pl.when(self.me.outer == 1)
        def _():
            for n in range(2):
                self.onward(n).wait_recv()

        self.near().wait_recv()

    def y_copy(self):
        me = self.me
        place = self.view(me.z if self.early else slice(None), me.y, me.t)
        return rcopy(self.own if self.early else place, place, self.ys, self.yr, me.over_y)

    def x_copy(self):
        me = self.me
        place = self.view(slice(None), slice(None), me.t)
        return rcopy(place, place, self.xs, self.xr, me.over_t)

    def c_copy(self):
        return rcopy(self.pair(), self.pair(), self.cs, self.cr, self.me.over_c)

    def finish(self):
        self.near().wait_send()
        self.far().wait_send()

        @pl.when(self.me.outer == 0)
        def _():
            for n in range(2):
                self.onward(n).wait_send()

        self.y_copy().wait_send()
        if self.wide:
            self.x_copy().wait_send()
        self.c_copy().wait_send()


def pass_sems(*lead):
    dma = pltpu.SemaphoreType.DMA
    return [dma(lead + (2,)), dma(lead + (3,)), dma(lead + (2,))] + [dma(lead or (1,))] * 6


def fwd_kernel(deep, x_sh, ml_sh, nz_sh, qkv_sh, out_sh, in_sh, hid_sh, bin_sh, cot_h, bqv, length, *rest):
    fwd_steps(deep, x_sh, ml_sh, nz_sh, qkv_sh, out_sh, in_sh, hid_sh, bin_sh, cot_h, bqv, length, rest[:6], *rest[6:])


def fwd_steps(deep, x_sh, ml_sh, nz_sh, qkv_sh, out_sh, in_sh, hid_sh, bin_sh, cot_h, bqv, length, vec_h,
               q_o, k_o, v_o, lse_o, x_o, mask_o, qkv_o, gate_o, outs_o, dz1_o, ghid_o, gin_o, gout_o, dat_o, small_o,
               x_v, w_v, m_v, q_v, k_v, v_v, a_v, lse_v, out_w, in_w, hid_w, bin_v, attn_v, bias,
               hat1_v, s1_v, h1b_v, ht_v, act_v, dg_v, z_v, hat2_v, zt_v, outs_v, dz1_v, gout_v, dat_v, cot_v, small_v, vec_v,
               loc, gs, xs, xr, as_, ar, *sems):
    me = Place(deep)
    Z = me.Z
    y, c, z, t = me.y, me.c, me.z, me.t
    half = x_sh.shape[0]
    seq, width = x_v.shape
    pairs = q_v.shape[0]
    heads = 2 * pairs
    q_sems, m_sems, w_sems = sems[0:9], sems[9:18], sems[18:27]

    def cols(n):
        return pl.ds(pl.multiple_of(t * n, 128), n)

    rows_own = pl.ds(pl.multiple_of(t * half, 128), half)
    rows_other = pl.ds(pl.multiple_of((1 - t) * half, 128), half)

    P_Q = Pass(me, qkv_sh, lambda zs, ys, ts: w_v.at[zs, ys, c], lambda: w_v.at[:, :, c],
               list(q_sems[:3]) + [s.at[0] for s in q_sems[3:]])

    def M(h):
        return Pass(me, m_v.at[h, z, y, c], lambda zs, ys, ts: m_v.at[h, zs, ys, c], lambda: m_v.at[h, :, :, c],
                    [s.at[h] for s in m_sems])

    def W(k, shard, whole, early):
        n = shard.shape[1]

        def view(zs, ys, ts):
            return whole.at[zs, ys, c, :, pl.ds(pl.multiple_of(ts * n, 128), n)]

        return Pass(me, shard, view, lambda: whole.at[:, :, c], [s.at[k] for s in w_sems], early, True)

    WO, WI, WH = W(0, out_sh, out_w, False), W(1, in_sh, in_w, True), W(2, hid_sh, hid_w, False)

    locals_ = [
        pltpu.make_async_copy(qkv_sh, w_v.at[z, y, c], loc.at[17]),
        pltpu.make_async_copy(x_sh, x_v.at[rows_own], loc.at[16]),
        pltpu.make_async_copy(bin_sh, bin_v.at[t, 0], loc.at[3]),
    ] + [pltpu.make_async_copy(w.own, w.view(z, y, t), loc.at[4 + k]) for k, w in enumerate((WO, WI, WH))]
    raw = ml_sh.shape
    mixed = [pltpu.make_async_copy(a, dg_v.at[pl.ds(0, raw[0]), pl.ds(n * raw[1], raw[1])], loc.at[n])
             for a, n in ((ml_sh, 0), (nz_sh, 1))]
    late = [pltpu.make_async_copy(cot_h, cot_v, loc.at[2])] + [
        pltpu.make_async_copy(a, vec_v.at[n], loc.at[18 + n]) for n, a in enumerate(vec_h)]
    b_out, b_hid, g1, c1, g2, c2 = (vec_v.at[pl.ds(n, 1)] for n in range(6))
    for cp in mixed + locals_ + late:
        cp.start()
    me.greet()

    def x_copy():
        return rcopy(x_sh, x_v.at[rows_own], xs.at[0], xr.at[0], me.over_t)

    def b_copy():
        return rcopy(bin_sh, bin_v.at[t, 0], xs.at[1], xr.at[1], me.over_t)

    def a_cols(p):
        return pl.ds(pl.multiple_of(t * (pairs * 128) + p * 128, 128), 128)

    def a_copy(p):
        return rcopy(a_v.at[p, rows_other], attn_v.at[:, a_cols(p)], as_.at[p], ar.at[p], me.over_t)

    def a_local(p):
        return pltpu.make_async_copy(a_v.at[p, rows_own], attn_v.at[:, a_cols(p)], loc.at[7 + p])

    def mask_save(h):
        return pltpu.make_async_copy(m_v.at[h], mask_o.at[h], loc.at[10 + h])

    P_Q.z_start()
    WI.y_copy().start()
    x_copy().start()
    b_copy().start()
    for cp in mixed:
        cp.wait()
    per = raw[0] // heads

    def mask_of(h):
        rows = pl.ds(pl.multiple_of(h * per, per), per)
        v = dg_v[rows, 0:raw[1]] + dg_v[rows, raw[1]:2 * raw[1]]
        m_v[h, z, y, c] = (jnp.minimum(v, 0.0) - jnp.log1p(jnp.exp(-jnp.abs(v)))).astype(BF)
        dg_v[rows, 2 * raw[1]:3 * raw[1]] = jax.nn.sigmoid(-v)

    mask_of(0)
    M(0).z_start()
    for h in range(1, heads):
        mask_of(h)
    gate_save = pltpu.make_async_copy(dg_v.at[pl.ds(0, raw[0]), pl.ds(2 * raw[1], raw[1])], gate_o, loc.at[0])
    gate_save.start()
    key = lax.broadcasted_iota(jnp.int32, bias.shape, 1)
    bias[...] = jnp.where(key < length[0], 0.0, NEG)
    for cp in locals_:
        cp.wait()
    P_Q.relay()
    P_Q.z_wait()
    P_Q.y_copy().start()
    WH.z_start()
    M(0).relay()
    M(0).z_wait()
    M(0).y_copy().start()
    WI.y_copy().wait_recv()
    WI.z_start()
    WH.relay()
    WH.z_wait()
    WH.y_copy().start()
    M(1).z_start()
    P_Q.y_copy().wait_recv()
    P_Q.c_copy().start()
    x_copy().wait_recv()
    P_Q.c_copy().wait_recv()

    step = half // 2

    def project(r, carry):
        rows = pl.ds(pl.multiple_of(r * step, step), step)
        xb = x_v[rows, :]
        for j, dst in enumerate((q_v, k_v, v_v)):
            w = w_v[:, :, :, j].reshape(width, pairs * 128)
            acc = dot(xb, w)
            if j == 0:
                acc = acc + bqv[0:1, :]
            elif j == 2:
                acc = acc + bqv[1:2, :]
            out = acc.astype(BF)
            if j == 0:
                out = out * jnp.asarray(0.125, BF)
            for p in range(pairs):
                dst[p, rows, :] = out[:, p * 128:(p + 1) * 128]
        return carry

    lax.fori_loop(0, seq // step, project, 0)
    outs = [
        pltpu.make_async_copy(q_v, q_o, loc.at[6]),
        pltpu.make_async_copy(k_v, k_o, loc.at[1]),
        pltpu.make_async_copy(v_v, v_o, loc.at[2]),
        pltpu.make_async_copy(x_v, x_o, loc.at[3]),
        pltpu.make_async_copy(w_v, qkv_o, loc.at[4]),
    ]
    for cp in outs:
        cp.start()
    blk = seq // Z

    def attend(p, u):
        h = 2 * p + u
        sl = slice(64 * u, 64 * u + 64)

        def rows_of(b, carry):
            rows = pl.ds(pl.multiple_of(b * blk, blk), blk)
            s = dot_t(q_v[p, rows, sl], k_v[p, :, sl])
            s = s + m_v[h, b].reshape(blk, seq).astype(F32) + bias[...]
            top = jnp.max(s, axis=-1, keepdims=True)
            e = jnp.exp(s - top)
            total = jnp.sum(e, axis=-1, keepdims=True)
            o = dot(e.astype(BF), v_v[p, :, sl])
            a_v[p, rows, sl] = (o / total).astype(BF)
            lse_v[p, rows, u:u + 1] = top + jnp.log(total)
            return carry

        lax.fori_loop(0, Z, rows_of, 0)

    def with_0():
        M(1).relay()
        M(1).z_wait()
        M(1).y_copy().start()
        M(2).z_start()

    def with_1():
        M(3).z_start()

    def with_2():
        pass

    def with_3():
        WI.x_copy().wait_recv()
        WI.c_copy().start()

    def with_4():
        WH.x_copy().wait_recv()
        WH.c_copy().start()

    def with_5():
        WO.y_copy().wait_recv()
        WO.x_copy().start()

    def ahead_0():
        pass

    def ahead_1():
        WI.relay()
        WI.z_wait()
        WI.x_copy().start()
        WH.y_copy().wait_recv()
        WH.x_copy().start()
        M(2).relay()
        M(2).z_wait()
        M(2).y_copy().start()

    def ahead_2():
        M(3).relay()
        M(3).z_wait()
        M(3).y_copy().start()
        M(4).z_start()
        WO.z_start()

    def ahead_3():
        M(4).relay()
        M(4).z_wait()
        M(4).y_copy().start()
        M(5).z_start()

    def ahead_4():
        WO.relay()
        WO.z_wait()
        WO.y_copy().start()
        M(5).relay()
        M(5).z_wait()
        M(5).y_copy().start()

    def ahead_5():
        pass

    ahead = (ahead_0, ahead_1, ahead_2, ahead_3, ahead_4, ahead_5)
    beside = (with_0, with_1, with_2, with_3, with_4, with_5)

    def pair_step(p, carry):
        for u in range(2):
            h = 2 * p + u
            for n in range(pairs):
                pl.when(p == n)(ahead[2 * n + u])
            M(h).y_copy().wait_recv()
            M(h).c_copy().start()
            for n in range(pairs):
                pl.when(p == n)(beside[2 * n + u])
            M(h).c_copy().wait_recv()
            mask_save(h).start()
            attend(p, u)
        a_copy(p).start()
        a_local(p).start()
        return carry

    lax.fori_loop(0, pairs, pair_step, 0)
    lse_out = pltpu.make_async_copy(lse_v, lse_o, loc.at[5])
    lse_out.start()
    WO.x_copy().wait_recv()
    WO.c_copy().start()
    for p in range(pairs):
        a_local(p).wait()
        a_copy(p).wait()
    b_copy().wait()
    for cp in late:
        cp.wait()
    for w in (WI, WH, WO):
        w.c_copy().wait_recv()

    quarter = m_v.shape[1:5]
    deep_w = width // (quarter[0 + 1] * quarter[2] * quarter[3])
    step = seq // 2
    flat = width

    def whole(ref, at):
        return ref[:, :, :, :, at].reshape(flat, -1)

    def slab(j, n):
        return m_v.at[j, pl.ds(0, deep_w), :, :, :, pl.ds(n * step, step)]

    def save(j, n):
        out = (ghid_o, gin_o)[n]
        return pltpu.make_async_copy(slab(j, n), out.at[:, :, :, :, pl.ds(pl.multiple_of(j * step, 128), step)], gs.at[j, n])

    def put(n):
        def one(j, value):
            m_v[j, 0:deep_w, :, :, :, n * step:(n + 1) * step] = value.reshape((deep_w,) + quarter[1:] + (step,))
            save(j, n).start()

        return one

    def ready():
        for h in range(heads):
            M(h).finish()
            mask_save(h).wait()

    outs_save = pltpu.make_async_copy(outs_v, outs_o, loc.at[0])
    per_t = bin_v.shape[2] // step

    def bin_of(j):
        return bin_v[j // per_t, :, pl.ds(pl.multiple_of(lax.rem(j, per_t) * step, 128), step)]

    for cp in outs + [lse_out, gate_save]:
        cp.wait()
    middle_math(attn_v, lambda rows: x_v[pl.ds(pl.multiple_of(t * half + rows.start, 128), rows.size), :],
                lambda: whole(out_w, slice(None)), lambda at: whole(in_w, at), lambda at: whole(hid_w, at),
                b_out, bin_of, b_hid, g1, c1, g2, c2, cot_v, length[0], t * half,
                outs_v, dz1_v, gout_v, dat_v, small_v, hat1_v, s1_v, h1b_v, ht_v, act_v, dg_v, z_v, hat2_v, zt_v,
                put(0), put(1), ready, outs_save.start)
    ends = [pltpu.make_async_copy(a, b, loc.at[1 + n]) for n, (a, b) in enumerate((
        (dz1_v, dz1_o), (gout_v, gout_o), (dat_v, dat_o), (small_v, small_o)))]
    for cp in ends:
        cp.start()
    x_copy().wait_send()
    P_Q.finish()
    for w in (WO, WI, WH):
        w.finish()
    for j in range(heads):
        for n in range(2):
            save(j, n).wait()
    outs_save.wait()
    for cp in ends:
        cp.wait()


def forward(deep, x, ml, nz, qkv, w_out_t, w_in, w_hid_t, b_in, cot, b_qv, length, vectors):
    half, width = x.shape
    seq = 2 * half
    heads, blk, _ = ml.shape
    pairs = heads // 2
    Z, Y, C = deep // 4, 2, 2
    n_out, n_in = w_out_t.shape[1], w_in.shape[1]
    r = w_in.shape[0]
    wide = 2 * n_in
    tall = (width // (Y * C * blk), Y, C, blk)
    rows = 6 * width // 128 + wide // 128
    rows += -rows % 8
    sd, vm = jax.ShapeDtypeStruct, pltpu.VMEM
    dma = pltpu.SemaphoreType.DMA
    out_shape = (
        sd((pairs, seq, 128), BF), sd((pairs, seq, 128), BF), sd((pairs, seq, 128), BF),
        sd((pairs, seq, 128), F32),
        sd((seq, width), BF),
        sd((heads, Z, Y, C, blk, seq), BF),
        sd((Z, Y, C) + qkv.shape, BF), sd((heads * blk, seq), F32),
        sd((half, width), BF), sd((half, width), F32), sd(tall + (wide,), BF), sd(tall + (wide,), BF),
        sd((width, width), BF), sd((half, width), BF), sd((rows, 128), F32),
    )
    pair = vm((pairs, seq, 128), BF)
    return pl.pallas_call(
        functools.partial(fwd_kernel, deep),
        out_shape=out_shape,
        in_specs=[ANY] * 9 + [VM, pl.BlockSpec(memory_space=pltpu.SMEM)] + [ANY] * 6,
        out_specs=[ANY] * len(out_shape),
        scratch_shapes=[
            vm((seq, width), BF),
            vm((Z, Y, C) + qkv.shape, BF),
            vm((heads, Z, Y, C, blk, seq), BF),
            pair, pair, pair, pair, vm((pairs, seq, 128), F32),
            vm((Z, Y, C, r, 2 * n_out), BF), vm((Z, Y, C, r, wide), BF), vm((Z, Y, C, r, wide), BF), vm((2, 1) + b_in.shape, F32),
            vm((half, width), BF), vm((1, seq), F32),
            vm((half, width), F32), vm((half, 128), F32), vm((half, width), BF), vm((width, half), BF), vm((half, wide), BF), vm((half, wide), F32),
            vm((half, width), F32), vm((half, width), BF), vm((width, half), BF),
            vm((half, width), BF), vm((half, width), F32), vm((width, width), BF), vm((half, width), BF), vm((half, width), F32), vm((rows, 128), F32), vm((8, width), F32),
            dma((24,)), dma((heads, 2)), dma((2,)), dma((2,)), dma((pairs,)), dma((pairs,)),
            *pass_sems(), *pass_sems(heads), *pass_sems(3),
        ],
        compiler_params=pltpu.CompilerParams(collective_id=1, has_side_effects=True, vmem_limit_bytes=62 << 20),
        name="forward_attention",
    )(x, ml.reshape(heads * blk, seq), nz.reshape(heads * blk, seq), qkv, w_out_t, w_in, w_hid_t, b_in, cot, b_qv, length, *vectors)


class Fold:
    def __init__(self, me, near_part, far_part, lc, bufs, sems, final, lx=None, early=False, cols=None):
        self.me, self.own, self.away, self.lc = me, near_part, far_part, lc
        self.ly, self.lz, self.lr = bufs
        self.s, self.r = sems
        self.final, self.lx, self.early, self.cols = final, lx, early, cols

    def base(self):
        return self.lc if self.lx is None else self.lx

    def c_copy(self):
        return rcopy(self.away, self.lc, self.s(0), self.r(0), self.me.over_c)

    def c_add(self):
        self.c_copy().wait_recv()

        def one(i, carry):
            for j in range(self.me.Y):
                self.lc[i, j] = self.lc[i, j] + self.own(i, j)
            return carry

        lax.fori_loop(0, self.me.Z, one, 0)

    def x_copy(self):
        me = self.me
        return rcopy(self.lc.at[:, :, :, self.cols(1 - me.t)], self.lx, self.s(1), self.r(1), me.over_t)

    def x_add(self):
        self.x_copy().wait_recv()
        at = self.cols(self.me.t)

        def one(i, carry):
            for j in range(self.me.Y):
                self.lx[i, j] = self.lx[i, j] + self.lc[i, j, :, at]
            return carry

        lax.fori_loop(0, self.me.Z, one, 0)

    def y_copy(self):
        me = self.me
        src = self.base().at[me.z, 1 - me.y] if self.early else self.base().at[:, 1 - me.y]
        return rcopy(src, self.ly, self.s(2), self.r(2), me.over_y)

    def y_add(self):
        self.y_copy().wait_recv()
        base, y = self.base(), self.me.y

        def one(i, carry):
            self.ly[i] = self.ly[i] + base[i, y]
            return carry

        lax.fori_loop(0, self.me.Z, one, 0)

    def along(self):
        return self.base() if self.early else self.ly

    def near(self):
        me = self.me
        return rcopy(self.along().at[me.z_near], self.lz.at[0], self.s(3), self.r(3), me.dev(z=me.z_near))

    def through(self, n):
        me = self.me
        place = self.along().at[me.z_far_inner if n == 0 else me.z_far_outer]
        return rcopy(place, self.lr.at[n], self.s(4 + n), self.r(4 + n), me.dev(z=me.z_near))

    def onward(self, n):
        me = self.me
        z = me.z_far_inner if n == 0 else me.z_far_outer
        return rcopy(self.along().at[z], self.lz.at[1], self.s(6 + n), self.r(6), me.dev(z=z))

    def z_start(self):
        @pl.when(self.me.outer == 1)
        def _():
            for n in range(2):
                self.through(n).start()

        self.near().start()

    def relay(self):
        me = self.me

        @pl.when(me.outer == 0)
        def _():
            for n in range(2):
                self.through(n).wait_recv()
                z = me.z_far_inner if n == 0 else me.z_far_outer
                self.along()[z] = self.along()[z] + self.lr[n]
                self.onward(n).start()

    def z_sum(self):
        self.near().wait_recv()
        self.onward(0).wait_recv()
        total = self.along()[self.me.z].astype(F32) + self.lz[0].astype(F32)
        return total + self.lz[1].astype(F32)

    def z_end(self):
        self.final(self.z_sum())

    def early_z_end(self):
        self.base()[self.me.z] = self.z_sum().astype(BF)
        self.y_copy().start()

    def early_y_end(self):
        self.y_copy().wait_recv()
        self.final(self.base()[self.me.z, self.me.y].astype(F32) + self.ly[...].astype(F32))

    def finish(self, skip_c=False):
        if not skip_c:
            self.c_copy().wait_send()
        if self.lx is not None:
            self.x_copy().wait_send()
        self.y_copy().wait_send()
        self.near().wait_send()

        @pl.when(self.me.outer == 1)
        def _():
            for n in range(2):
                self.through(n).wait_send()

        @pl.when(self.me.outer == 0)
        def _():
            for n in range(2):
                self.onward(n).wait_send()


def bwd_kernel(deep, dat, q_h, k_h, v_h, mask_h, lse_h, x_h, qkv_h, hid_h, in_h, out_h, dz1_h, sg_h, small_h, bias,
               dx_o, gqkv_o, ghid_o, gin_o, gout_o, gmask_o, small_o,
               q_v, k_v, v_v, do_v, lse_v, m_v, p_v, dq_v, dk_v, dv_v, acck, accv,
               lc_m, ly_m, lz_m, lr_m, gm_v,
               own_w, lc_hid, lx_hid, ly_hid, lz_hid, lr_hid, lc_in, lx_in, ly_in, lz_in, lr_in, lc_out, lx_out, ly_out, lz_out, lr_out,
               fin_hid, fin_in, fin_out,
               p_q, lc_q, ly_q, lz_q, lr_q, fin_q,
               x_v, w_v, sx_v, lx_x, dx_v, dz_v,
               s_v, sc_v, sy_v, sz_v, sx2_v,
               loc, msem, ds_, dr, wl, w_s, w_r, m_s, m_r, q_s, q_r, xs, xr, s1s, s1r, szs, szr):
    me = Place(deep)
    Z, y, c, z, t = me.Z, me.y, me.c, me.z, me.t
    pairs, seq, _ = q_v.shape
    heads = 2 * pairs
    half = seq // 2
    width = x_v.shape[1]
    zs = range(1, Z)
    rows_own = pl.ds(pl.multiple_of(t * half, 128), half)

    def dat_cols(p, who):
        return pl.ds(pl.multiple_of(who * (pairs * 128) + p * 128, 128), 128)

    def dat_local(p):
        return pltpu.make_async_copy(dat.at[:, dat_cols(p, t)], do_v.at[p, rows_own], loc.at[p])

    def dat_copy(p):
        return rcopy(dat.at[:, dat_cols(p, 1 - t)], do_v.at[p, rows_own], ds_.at[p], dr.at[p], me.over_t)

    loads = [pltpu.make_async_copy(a, b, loc.at[3 + n]) for n, (a, b) in enumerate((
        (q_h, q_v), (k_h, k_v), (v_h, v_v), (lse_h, lse_v), (x_h, x_v), (qkv_h, w_v), (dz1_h, dz_v), (small_h, s_v.at[pl.ds(0, small_h.shape[0])])))]

    def m_load(h, slot):
        return pltpu.make_async_copy(mask_h.at[h], m_v.at[slot], msem.at[slot])

    def sg_load(h):
        return pltpu.make_async_copy(sg_h.at[h], gm_v.at[h], loc.at[11 + h])

    def gm_save(h):
        return pltpu.make_async_copy(gm_v.at[h], gmask_o.at[h], loc.at[17 + h])

    def M(h, slot=None):
        def own(i, j):
            return p_v[slot, i, j, c]

        def final(total):
            sg_load(h).wait()
            gm_v[h] = total * gm_v[h]
            gm_save(h).start()

        away = None if slot is None else p_v.at[slot, :, :, 1 - c]
        return Fold(me, own, p_v.at[0, :, :, 1 - c] if away is None else away, lc_m.at[h],
                    (ly_m.at[h], lz_m.at[h], lr_m.at[h]), (lambda n: m_s.at[h, n], lambda n: m_r.at[h, n]), final)

    def W(k, part, lc, lx, ly, lz, lr, fin, out, early):
        n = lx.shape[-1]

        def own(i, j):
            return own_w[i, j, :, 0:2 * n]

        def final(total):
            fin[...] = total
            pltpu.make_async_copy(fin, out, wl.at[3 + k]).start()

        fold = Fold(me, own, part.at[:, :, 1 - c], lc, (ly, lz, lr), (lambda i: w_s.at[k, i], lambda i: w_r.at[k, i]), final,
                    lx, early, lambda who: pl.ds(pl.multiple_of(who * n, 128), n))
        fold.own_load = lambda: pltpu.make_async_copy(part.at[:, :, c], own_w.at[:, :, :, pl.ds(0, 2 * n)], wl.at[k])
        fold.saved = lambda: pltpu.make_async_copy(fin, out, wl.at[3 + k])
        return fold

    WH = W(0, hid_h, lc_hid, lx_hid, ly_hid, lz_hid, lr_hid, fin_hid, ghid_o, False)
    WI = W(1, in_h, lc_in, lx_in, ly_in, lz_in, lr_in, fin_in, gin_o, True)
    WO = W(2, out_h, lc_out, lx_out, ly_out, lz_out, lr_out, fin_out, gout_o, False)

    def q_final(total):
        fin_q[...] = total
        pltpu.make_async_copy(fin_q, gqkv_o, loc.at[24]).start()

    Q = Fold(me, lambda i, j: p_q[i, j, c], p_q.at[:, :, 1 - c], lc_q, (ly_q, lz_q, lr_q),
             (lambda n: q_s.at[n], lambda n: q_r.at[n]), q_final)

    def x_copy():
        return rcopy(sx_v, lx_x, xs, xr, me.over_t)

    def s_c():
        return rcopy(s_v, sc_v, s1s.at[0], s1r.at[0], me.over_c)

    def s_y():
        return rcopy(sc_v, sy_v, s1s.at[1], s1r.at[1], me.over_y)

    def s_z(d):
        return rcopy(sy_v, sz_v.at[z], szs.at[d - 1], szr.at[d - 1], me.along_z(d))

    def s_z_in(d):
        return rcopy(sy_v, sz_v.at[me.source_z(d)], szs.at[d - 1], szr.at[d - 1], me.along_z(d))

    def s_x():
        return rcopy(s_v, sx2_v, s1s.at[2], s1r.at[2], me.over_t)

    m_load(0, 0).start()
    for cp in loads[:4]:
        cp.start()
    for p in range(pairs):
        dat_local(p).start()
    WH.own_load().start()
    for cp in loads[4:]:
        cp.start()
    me.greet()
    for p in range(pairs):
        dat_copy(p).start()
    for w in (WH, WI, WO):
        w.c_copy().start()
    for h in range(heads):
        sg_load(h).start()
    for cp in loads:
        cp.wait()

    blk = seq // Z
    shape4 = p_v.shape[2:]

    def attend(p, u, slot):
        sl = slice(64 * u, 64 * u + 64)
        acck[...] = jnp.zeros_like(acck)
        accv[...] = jnp.zeros_like(accv)

        def rows_of(n, carry):
            b = lax.rem(t * (Z // 2) + n, Z)
            if u == 0:
                @pl.when(n == Z // 2)
                def _():
                    dat_copy(p).wait_recv()

            rows = pl.ds(pl.multiple_of(b * blk, blk), blk)
            qb, dob = q_v[p, rows, sl], do_v[p, rows, sl]
            kk, vv = k_v[p, :, sl], v_v[p, :, sl]
            s = dot_t(qb, kk) + m_v[u, b].reshape(blk, seq).astype(F32) + bias[...]
            pr = jnp.exp(s - lse_v[p, rows, u:u + 1])
            dp = dot_t(dob, vv)
            tt = pr * dp
            delta = jnp.sum(tt, axis=-1, keepdims=True)
            dsb = (tt - pr * delta).astype(BF)
            p_v[slot, b] = dsb.reshape(shape4)
            dq_v[p, rows, sl] = (dot(dsb, kk) * 0.125).astype(BF)
            acck[...] += dot_0(dsb, qb)
            accv[...] += dot_0(pr.astype(BF), dob)
            return carry

        lax.fori_loop(0, Z, rows_of, 0)
        dk_v[p, :, sl] = acck[...].astype(BF)
        dv_v[p, :, sl] = accv[...].astype(BF)

    def after_0():
        WH.own_load().wait()
        WH.c_add()
        WI.own_load().start()
        WH.x_copy().start()
        M(0, 0).c_add()
        M(0).y_copy().start()

    def after_1():
        WI.own_load().wait()
        WI.c_add()
        WO.own_load().start()
        WI.x_copy().start()
        M(1, 1).c_add()
        M(1).y_copy().start()

    def after_2():
        WO.own_load().wait()
        WO.c_add()
        WO.x_copy().start()
        M(2, 0).c_add()
        M(2).y_copy().start()
        M(0).y_add()
        M(0).z_start()

    def after_3():
        M(3, 1).c_add()
        M(3).y_copy().start()
        WH.x_add()
        WH.y_copy().start()
        M(0).relay()

    def after_4():
        M(1).y_add()
        M(1).z_start()
        M(4, 0).c_add()
        M(4).y_copy().start()

    def after_5():
        M(1).relay()
        M(2).y_add()
        M(2).z_start()
        M(5, 1).c_add()
        M(5).y_copy().start()

    after = (after_0, after_1, after_2, after_3, after_4, after_5)

    def pair_step(p, carry):
        dat_local(p).wait()
        for u in range(2):
            h = 2 * p + u
            m_load(h, u).wait()
            if u == 0:
                m_load(h + 1, 1).start()
            else:
                @pl.when(p < pairs - 1)
                def _():
                    m_load(h + 1, 0).start()

            @pl.when(p > 0)
            def _():
                M(h - 2, u).c_copy().wait_send()

            attend(p, u, u)
            M(h, u).c_copy().start()
            for n in range(pairs):
                pl.when(p == n)(after[2 * n + u])
        return carry

    lax.fori_loop(0, pairs, pair_step, 0)

    step = half // 2

    def d_cat(ref, rows):
        return jnp.concatenate([ref[p, rows, :] for p in range(pairs)], axis=1)

    def weight(j):
        return w_v[:, :, :, j].reshape(width, pairs * 128)

    def terms(rows):
        acc = dot_t(d_cat(dq_v, rows), weight(0))
        acc = acc + dot_t(d_cat(dk_v, rows), weight(1))
        return acc + dot_t(d_cat(dv_v, rows), weight(2))

    def theirs(r, carry):
        at = pl.ds(pl.multiple_of(r * step, step), step)
        rows = pl.ds(pl.multiple_of((1 - t) * half + r * step, step), step)
        sx_v[at, :] = terms(rows).astype(BF)
        return carry

    lax.fori_loop(0, 2, theirs, 0)
    x_copy().start()

    for j, ref in enumerate((dq_v, dk_v, dv_v)):
        g = dot_0(x_v[...], d_cat(ref, slice(None)))
        p_q[:, :, :, j] = g.astype(BF).reshape(p_q.shape[:3] + p_q.shape[4:])
    Q.c_copy().start()
    M(2).relay()
    base = small_h.shape[0]
    for n, ref in enumerate((dq_v, dv_v)):
        for p in range(pairs):
            at = base + n * pairs + p
            s_v[at:at + 1, :] = jnp.sum(ref[p].astype(F32), axis=0, keepdims=True)
    for at in range(base + 2 * pairs, s_v.shape[0]):
        s_v[at:at + 1, :] = jnp.zeros((1, 128), F32)
    s_c().start()
    Q.c_add()
    Q.y_copy().start()

    def mine(r, carry):
        at = pl.ds(pl.multiple_of(r * step, step), step)
        rows = pl.ds(pl.multiple_of(t * half + r * step, step), step)
        dx_v[at, :] = terms(rows) + dz_v[at, :]
        return carry

    lax.fori_loop(0, 2, mine, 0)
    s_c().wait_recv()
    sc_v[...] = sc_v[...] + s_v[...]
    s_y().start()
    M(3).y_add()
    M(3).z_start()
    WI.x_add()
    WI.z_start()
    M(0).z_end()
    WO.x_add()
    WO.y_copy().start()
    M(3).relay()
    WI.relay()
    WH.y_add()
    WH.z_start()
    M(1).z_end()
    M(2).z_end()
    M(4).y_add()
    M(4).z_start()
    WH.relay()
    WI.early_z_end()
    M(3).z_end()
    M(4).relay()
    M(5).y_add()
    M(5).z_start()
    s_y().wait_recv()
    sy_v[...] = sy_v[...] + sc_v[...]
    sz_v[z] = sy_v[...]
    for d in zs:
        s_z(d).start()
    Q.y_add()
    Q.z_start()
    WH.z_end()
    M(5).relay()
    WO.y_add()
    WO.z_start()
    Q.relay()
    M(4).z_end()
    x_copy().wait_recv()
    dx_v[...] = dx_v[...] + lx_x[...].astype(F32)
    dx_save = pltpu.make_async_copy(dx_v, dx_o, loc.at[23])
    dx_save.start()
    WO.relay()
    for d in zs:
        s_z_in(d).wait_recv()
    s_c().wait_send()
    total = sz_v[0]
    for i in range(1, Z):
        total = total + sz_v[i]
    s_v[...] = total
    s_x().start()
    M(5).z_end()
    WI.early_y_end()
    Q.z_end()
    WO.z_end()
    s_x().wait_recv()
    low = sx2_v[...] + s_v[...]
    row = lax.broadcasted_iota(jnp.int32, low.shape, 0)
    s_y().wait_send()
    sc_v[...] = jnp.where(row < base, low, s_v[...])
    s_save = pltpu.make_async_copy(sc_v, small_o, loc.at[25])
    s_save.start()

    for p in range(pairs):
        dat_copy(p).wait_send()
    for w in (WH, WI, WO):
        w.finish()
        w.saved().wait()
    for h in range(heads):
        M(h).finish(h < heads - 2)
        gm_save(h).wait()
    Q.finish()
    for d in zs:
        s_z(d).wait_send()
    x_copy().wait_send()
    s_x().wait_send()
    dx_save.wait()
    pltpu.make_async_copy(fin_q, gqkv_o, loc.at[24]).wait()
    s_save.wait()


def backward(deep, dat, q, k, v, mask, lse, x, qkv, g_hid, g_in, g_out, dz1, sg, small, bias):
    pairs, seq, _ = q.shape
    half, width = dz1.shape
    heads, Z, Y, C, blk, _ = mask.shape
    r, n2 = g_in.shape[3], g_in.shape[4]
    n2o = g_out.shape[4]
    n, no = n2 // 2, n2o // 2
    base = small.shape[0]
    rows_s = base + 8
    sd = jax.ShapeDtypeStruct
    dma = pltpu.SemaphoreType.DMA
    vm = pltpu.VMEM
    out_shape = (
        sd((half, width), F32), sd(qkv.shape[3:], F32), sd((r, n), F32), sd((r, n), F32), sd((r, no), F32),
        sd((heads, blk, seq), F32), sd((rows_s, 128), F32),
    )
    pair = vm((pairs, seq, 128), BF)

    def chain(m, early):
        last = (Y, r, m) if early else (r, m)
        return [vm((Z, Y, r, 2 * m), BF), vm((Z, Y, r, m), BF), vm((r, m) if early else (Z, r, m), BF), vm((2,) + last, BF), vm((2,) + last, BF)]

    three, rq, nq = qkv.shape[3:]
    return pl.pallas_call(
        functools.partial(bwd_kernel, deep),
        out_shape=out_shape,
        in_specs=[ANY] * 14 + [VM],
        out_specs=[ANY] * len(out_shape),
        scratch_shapes=[
            pair, pair, pair, pair, vm((pairs, seq, 128), F32), vm((2, Z, Y, C, blk, seq), BF), vm((2, Z, Y, C, blk, seq), BF),
            pair, pair, pair, vm((seq, 64), F32), vm((seq, 64), F32),
            vm((heads, Z, Y, blk, seq), BF), vm((heads, Z, blk, seq), BF), vm((heads, 2, blk, seq), BF), vm((heads, 2, blk, seq), BF),
            vm((heads, blk, seq), F32),
            vm((Z, Y, r, n2), BF), *chain(n, False), *chain(n, True), *chain(no, False), vm((r, n), F32), vm((r, n), F32), vm((r, no), F32),
            vm((Z, Y, C, three, rq, nq), BF), vm((Z, Y, three, rq, nq), BF), vm((Z, three, rq, nq), BF),
            vm((2, three, rq, nq), BF), vm((2, three, rq, nq), BF), vm((three, rq, nq), F32),
            vm((seq, width), BF), vm((Z, Y, C, three, rq, nq), BF), vm((half, width), BF), vm((half, width), BF), vm((half, width), F32), vm((half, width), F32),
            vm((rows_s, 128), F32), vm((rows_s, 128), F32), vm((rows_s, 128), F32), vm((Z, rows_s, 128), F32), vm((rows_s, 128), F32),
            dma((26,)), dma((2,)), dma((pairs,)), dma((pairs,)),
            dma((6,)), dma((3, 8)), dma((3, 7)), dma((heads, 8)), dma((heads, 7)), dma((8,)), dma((7,)), dma, dma,
            dma((3,)), dma((3,)), dma((Z - 1,)), dma((Z - 1,)),
        ],
        compiler_params=pltpu.CompilerParams(collective_id=2, has_side_effects=True, vmem_limit_bytes=62 << 20),
        name="backward_attention",
    )(dat, q, k, v, mask, lse, x, qkv, g_hid, g_in, g_out, dz1, sg, small, bias)


NEG = -1e30
EPS = 1e-12


def layer_norm(value_rows, scale_vec, shift_vec):
    centre = value_rows - jnp.mean(value_rows, axis=-1, keepdims=True)
    spread = jnp.mean(centre * centre, axis=-1, keepdims=True)
    return centre * lax.rsqrt(spread + EPS) * scale_vec + shift_vec


def gelu_exact(value_rows):
    return jax.nn.gelu(value_rows, approximate=False)


def matmul(left, right):
    return jnp.dot(left, right, preferred_element_type=jnp.float32)


def times_transposed(left, right):
    return lax.dot_general(
        left, right, (((1,), (1,)), ((), ())), preferred_element_type=jnp.float32
    )


def over_rows(left, right):
    return lax.dot_general(
        left, right, (((0,), (0,)), ((), ())), preferred_element_type=jnp.float32
    )


def plain_body(
    inputs,
    lengths,
    w_qkv,
    b_qv,
    w_out,
    b_out,
    ln1_gain,
    ln1_bias,
    w_in,
    b_in,
    w_hid,
    b_hid,
    ln2_gain,
    ln2_bias,
    mask_logits,
    noise,
    cotangent,
):
    seq_count, half_rows, width = inputs.shape
    slot_len = half_rows * lax.axis_size("tensor")
    tensor_rank = lax.axis_index("tensor")
    head_count = mask_logits.shape[0]
    head_dim = w_qkv.shape[2] // head_count
    scale = head_dim ** (-0.5)
    token_count = seq_count * slot_len
    mixed_logits = mask_logits + noise
    local_mask = jax.nn.log_sigmoid(mixed_logits).astype(jnp.bfloat16)
    full_qkv, full_out, full_in, full_hid, full_mask = (
        lax.all_gather(w_qkv, "dp", axis=1, tiled=True),
        lax.all_gather(w_out, "dp", axis=1, tiled=True),
        lax.all_gather(w_in, "dp", axis=0, tiled=True),
        lax.all_gather(w_hid, "dp", axis=1, tiled=True),
        lax.all_gather(local_mask, "dp", axis=1, tiled=True),
    )
    key_valid = jnp.arange(slot_len, dtype=jnp.int32)[None, :] < lengths[:, None]
    own_rows = tensor_rank * half_rows + jnp.arange(half_rows, dtype=jnp.int32)
    row_valid = (own_rows[None, :] < lengths[:, None]).astype(jnp.float32)
    gathered = lax.all_gather(inputs, "tensor", axis=1, tiled=True)
    flat_rows = gathered.reshape(token_count, width)
    query_rows = (matmul(flat_rows, full_qkv[0]) + b_qv[0]).astype(jnp.bfloat16)
    key_rows = matmul(flat_rows, full_qkv[1]).astype(jnp.bfloat16)
    value_rows = (matmul(flat_rows, full_qkv[2]) + b_qv[1]).astype(jnp.bfloat16)

    def split_heads(matrix):
        return matrix.reshape(seq_count, slot_len, head_count, head_dim).transpose(0, 2, 1, 3)

    def join_heads(stacked):
        return stacked.transpose(0, 2, 1, 3).reshape(token_count, head_count * head_dim)

    def masked_scores(query_h, keys_h, mask_h, valid_keys):
        score_matrix = (
            jnp.einsum("qd,kd->qk", query_h, keys_h, preferred_element_type=jnp.float32) * scale
        )
        score_matrix = score_matrix + mask_h.astype(jnp.float32)
        return jnp.where(valid_keys[None, :], score_matrix, NEG)

    def attend_sequence(operands):
        query_s, keys_s, values_s, valid_keys = operands

        def attend_head(head_ops):
            query_h, keys_h, values_h, mask_h = head_ops
            score_matrix = masked_scores(query_h, keys_h, mask_h, valid_keys)
            top_score = jnp.max(score_matrix, axis=-1, keepdims=True)
            expo = jnp.exp(score_matrix - top_score)
            row_total = jnp.sum(expo, axis=-1, keepdims=True)
            attention_probabilities = (expo / row_total).astype(jnp.bfloat16)
            result = jnp.einsum(
                "qk,kd->qd", attention_probabilities, values_h, preferred_element_type=jnp.float32
            )
            return (result.astype(jnp.bfloat16), (top_score + jnp.log(row_total))[:, 0])

        return lax.map(attend_head, (query_s, keys_s, values_s, full_mask))

    head_out, log_total = lax.map(
        attend_sequence,
        (split_heads(query_rows), split_heads(key_rows), split_heads(value_rows), key_valid),
    )
    attn = join_heads(head_out)
    attn_terms = matmul(attn, full_out).reshape(seq_count, slot_len, width)
    attn_part = lax.psum_scatter(attn_terms, "tensor", scatter_dimension=1, tiled=True)
    first_sum = inputs.astype(jnp.float32) + attn_part + b_out
    hidden_one = layer_norm(first_sum, ln1_gain, ln1_bias)
    hidden_rows = lax.all_gather(
        hidden_one.astype(jnp.bfloat16), "tensor", axis=1, tiled=True
    ).reshape(token_count, width)
    pre_act = matmul(hidden_rows, full_in) + b_in
    activated = gelu_exact(pre_act).astype(jnp.bfloat16)
    ffn_terms = matmul(activated, full_hid).reshape(seq_count, slot_len, width)
    ffn_part = lax.psum_scatter(ffn_terms, "tensor", scatter_dimension=1, tiled=True)
    second_sum = hidden_one + ffn_part + b_hid
    outputs = layer_norm(second_sum, ln2_gain, ln2_bias).astype(jnp.bfloat16)
    back_qkv, back_out, back_in, back_hid, back_mask = (
        lax.all_gather(w_qkv, "dp", axis=1, tiled=True),
        lax.all_gather(w_out, "dp", axis=1, tiled=True),
        lax.all_gather(w_in, "dp", axis=0, tiled=True),
        lax.all_gather(w_hid, "dp", axis=1, tiled=True),
        lax.all_gather(local_mask, "dp", axis=1, tiled=True),
    )
    grad_output = cotangent * row_valid[:, :, None]
    _, pull_second = jax.vjp(layer_norm, second_sum, ln2_gain, ln2_bias)
    grad_second, ln2_gain_part, ln2_bias_part = pull_second(grad_output)
    b_hid_part = jnp.sum(grad_second, axis=(0, 1))
    second_rows = lax.all_gather(
        grad_second.astype(jnp.bfloat16), "tensor", axis=1, tiled=True
    ).reshape(token_count, width)
    w_hid_grad = over_rows(activated, second_rows)
    grad_act = times_transposed(second_rows, back_hid)
    _, pull_gelu = jax.vjp(gelu_exact, pre_act)
    grad_pre = pull_gelu(grad_act)[0].astype(jnp.bfloat16)
    b_in_part = jnp.sum(grad_pre.astype(jnp.float32), axis=0)
    w_in_grad = over_rows(hidden_rows, grad_pre)
    hidden_terms = times_transposed(grad_pre, back_in).reshape(seq_count, slot_len, width)
    grad_hidden = grad_second + lax.psum_scatter(
        hidden_terms, "tensor", scatter_dimension=1, tiled=True
    )
    _, pull_first = jax.vjp(layer_norm, first_sum, ln1_gain, ln1_bias)
    grad_first, ln1_gain_part, ln1_bias_part = pull_first(grad_hidden)
    b_out_part = jnp.sum(grad_first, axis=(0, 1))
    first_rows = lax.all_gather(
        grad_first.astype(jnp.bfloat16), "tensor", axis=1, tiled=True
    ).reshape(token_count, width)
    w_out_grad = over_rows(attn, first_rows)
    grad_attn = times_transposed(first_rows, back_out).astype(jnp.bfloat16)

    def sequence_back(mask_acc, operands):
        query_s, keys_s, values_s, grad_s, total_s, valid_keys = operands

        def head_back(head_ops):
            query_h, keys_h, values_h, mask_h, grad_h, total_h = head_ops
            score_matrix = masked_scores(query_h, keys_h, mask_h, valid_keys)
            attention_probabilities = jnp.exp(score_matrix - total_h[:, None])
            grad_probs = jnp.einsum(
                "qd,kd->qk", grad_h, values_h, preferred_element_type=jnp.float32
            )
            centre = jnp.sum(attention_probabilities * grad_probs, axis=-1, keepdims=True)
            grad_scores = (attention_probabilities * (grad_probs - centre)).astype(jnp.bfloat16)
            grad_q = (
                jnp.einsum("qk,kd->qd", grad_scores, keys_h, preferred_element_type=jnp.float32)
                * scale
            ).astype(jnp.bfloat16)
            grad_k = (
                jnp.einsum("qk,qd->kd", grad_scores, query_h, preferred_element_type=jnp.float32)
                * scale
            ).astype(jnp.bfloat16)
            grad_v = jnp.einsum(
                "qk,qd->kd",
                attention_probabilities.astype(jnp.bfloat16),
                grad_h,
                preferred_element_type=jnp.float32,
            ).astype(jnp.bfloat16)
            return (grad_q, grad_k, grad_v, grad_scores)

        grad_q, grad_k, grad_v, grad_sc = lax.map(
            head_back, (query_s, keys_s, values_s, back_mask, grad_s, total_s)
        )
        return (mask_acc + grad_sc.astype(jnp.float32), (grad_q, grad_k, grad_v))

    mask_zero = jnp.zeros(back_mask.shape, jnp.float32)
    mask_grad, (heads_q, heads_k, heads_v) = lax.scan(
        sequence_back,
        mask_zero,
        (
            split_heads(query_rows),
            split_heads(key_rows),
            split_heads(value_rows),
            split_heads(grad_attn),
            log_total,
            key_valid,
        ),
    )
    query_grad = join_heads(heads_q)
    keys_grad = join_heads(heads_k)
    values_grad = join_heads(heads_v)
    b_qv_part = jnp.stack(
        [
            jnp.sum(query_grad.astype(jnp.float32), axis=0),
            jnp.sum(values_grad.astype(jnp.float32), axis=0),
        ]
    )
    w_qkv_grad = jnp.stack(
        [
            over_rows(flat_rows, query_grad),
            over_rows(flat_rows, keys_grad),
            over_rows(flat_rows, values_grad),
        ]
    )
    input_terms = (
        times_transposed(query_grad, back_qkv[0])
        + times_transposed(keys_grad, back_qkv[1])
        + times_transposed(values_grad, back_qkv[2])
    ).reshape(seq_count, slot_len, width)
    input_grad = grad_first + lax.psum_scatter(
        input_terms.astype(jnp.bfloat16), "tensor", scatter_dimension=1, tiled=True
    ).astype(jnp.float32)
    qkv_total, out_total, in_total, hid_total, mask_total = (
        lax.psum_scatter(w_qkv_grad, "dp", scatter_dimension=1, tiled=True),
        lax.psum_scatter(w_out_grad, "dp", scatter_dimension=1, tiled=True),
        lax.psum_scatter(w_in_grad, "dp", scatter_dimension=0, tiled=True),
        lax.psum_scatter(w_hid_grad, "dp", scatter_dimension=1, tiled=True),
        lax.psum_scatter(mask_grad, "dp", scatter_dimension=1, tiled=True),
    )
    mask_logit_grad = mask_total * jax.nn.sigmoid(-mixed_logits)
    ln1_gain_total, ln1_bias_total, ln2_gain_total, ln2_bias_total, b_out_total, b_hid_total = (
        lax.psum(
            (ln1_gain_part, ln1_bias_part, ln2_gain_part, ln2_bias_part, b_out_part, b_hid_part),
            ("dp", "tensor"),
        )
    )
    b_qv_total, b_in_total = lax.psum((b_qv_part, b_in_part), "dp")
    return (
        outputs,
        input_grad,
        qkv_total,
        b_qv_total,
        out_total,
        b_out_total,
        ln1_gain_total,
        ln1_bias_total,
        in_total,
        b_in_total,
        hid_total,
        b_hid_total,
        ln2_gain_total,
        ln2_bias_total,
        mask_logit_grad,
    )


def last_kernel(place, total, *refs):
    n = (len(refs) - 10) // 3
    ins, rest = refs[:n], refs[n:]
    (bqv_o, bin_o), vecs, outs = rest[:2], rest[2:8], rest[8:8 + n]
    held, tot_v, sems = rest[8 + n:8 + 2 * n], rest[8 + 2 * n], rest[9 + 2 * n]
    first = pltpu.make_async_copy(total, tot_v, sems.at[n])
    first.start()
    loads = [pltpu.make_async_copy(a, b, sems.at[i]) for i, (a, b) in enumerate(zip(ins, held))]
    saves = [pltpu.make_async_copy(a, b, sems.at[i]) for i, (a, b) in enumerate(zip(held, outs))]
    for cp in loads:
        cp.start()
    for a, b in zip(loads, saves):
        a.wait()
        b.start()
    first.wait()
    t = place[0]
    per = vecs[0].shape[0] // 128
    for k, ref in enumerate(vecs):
        for i in range(per):
            ref[pl.ds(i * 128, 128)] = tot_v[k * per + i, :]
    m = bin_o.shape[0] // 128
    for i in range(m):
        bin_o[pl.ds(i * 128, 128)] = tot_v[6 * per + t * m + i, :]
    base = total.shape[0] - 8
    nq = bqv_o.shape[1] // 128
    for j in range(2):
        for i in range(nq):
            bqv_o[j:j + 1, i * 128:(i + 1) * 128] = tot_v[base + j * nq + i:base + j * nq + i + 1, :]
    for cp in saves:
        cp.wait()


def last(t, total, arrays, width, n_bin, bqv_shape):
    sd, vm = jax.ShapeDtypeStruct, pltpu.VMEM
    n = len(arrays)
    return pl.pallas_call(
        last_kernel,
        out_shape=(sd(bqv_shape, F32), sd((n_bin,), F32)) + (sd((width,), F32),) * 6 + tuple(sd(a.shape, a.dtype) for a in arrays),
        in_specs=[pl.BlockSpec(memory_space=pltpu.SMEM)] + [ANY] * (n + 1),
        out_specs=[VM] * 8 + [ANY] * n,
        scratch_shapes=[vm(a.shape, a.dtype) for a in arrays] + [vm(total.shape, F32), pltpu.SemaphoreType.DMA((n + 1,))],
        compiler_params=pltpu.CompilerParams(vmem_limit_bytes=60 << 20),
        name="hand_over",
    )(t, total, *arrays)


def body(
    inputs, lengths, w_qkv, b_qv, w_out, b_out, ln1_gain, ln1_bias, w_in, b_in, w_hid, b_hid,
    ln2_gain, ln2_bias, mask_logits, noise, cotangent,
):
    deep = lax.axis_size("dp")
    x = inputs[0]
    half, width = x.shape
    seq = 2 * half
    bias = jnp.where(jnp.arange(seq, dtype=jnp.int32) < lengths[0], 0.0, NEG).astype(F32).reshape(1, seq)
    vectors = (b_out, b_hid, ln1_gain, ln1_bias, ln2_gain, ln2_bias)
    q, k, v, lse, x_all, mask_all, qkv_all, gate, outputs, dz1, g_hid, g_in, g_out, dattn, small = forward(
        deep, x, mask_logits, noise, w_qkv, w_out.T, w_in, w_hid.T, b_in, cotangent[0], b_qv, lengths, vectors)
    place = (deep // 4, 2, 2, w_in.shape[0])
    dx, gqkv, ghid, gin, gout, gmask, total = backward(
        deep, dattn, q, k, v, mask_all, lse, x_all, qkv_all,
        g_hid.reshape(place + (-1,)), g_in.reshape(place + (-1,)), g_out.reshape(place + (-1,)), dz1, gate.reshape(mask_logits.shape), small, bias)
    t = lax.axis_index("tensor").astype(jnp.int32).reshape(1)
    g_bqv, g_bin, v0, v1, v2, v3, v4, v5, outputs, dx, gqkv, gout, gin, ghid, gmask = last(
        t, total, (outputs, dx, gqkv, gout, gin, ghid, gmask), width, b_in.shape[0], b_qv.shape)
    return (outputs[None], dx[None], gqkv, g_bqv, gout.T, v4, v0, v1, gin, g_bin, ghid.T, v5, v2, v3, gmask)


def solution(mesh):
    placed = (
        P("dp", "tensor", None),
        P("dp"),
        P(None, "dp", "tensor"),
        P(None, "tensor"),
        P("tensor", "dp"),
        P(),
        P(),
        P(),
        P("dp", "tensor"),
        P("tensor"),
        P("tensor", "dp"),
        P(),
        P(),
        P(),
        P("tensor", "dp", None),
        P("tensor", "dp", None),
        P("dp", "tensor", None),
    )

    def run(*args):
        w_rows, m_rows = args[8].shape[0], args[14].shape[1]
        tiled = w_rows % 16 == 0 and m_rows % 16 == 0 and args[0].shape[0] == 1 and mesh.shape["dp"] == 16
        return (body if tiled else plain_body)(*args)

    return jax.shard_map(
        run,
        mesh=mesh,
        in_specs=placed,
        out_specs=(
            P("dp", "tensor", None),
            P("dp", "tensor", None),
            P(None, "dp", "tensor"),
            P(None, "tensor"),
            P("tensor", "dp"),
            P(),
            P(),
            P(),
            P("dp", "tensor"),
            P("tensor"),
            P("tensor", "dp"),
            P(),
            P(),
            P(),
            P("tensor", "dp", None),
        ),
        check_vma=False,
    )
```

```python
import functools

import jax
import jax.numpy as jnp
from jax import lax
from jax.experimental import pallas as pl
from jax.experimental.pallas import tpu as pltpu
from jax.sharding import PartitionSpec as P

MESH = pl.DeviceIdType.MESH
BF, F32 = jnp.bfloat16, jnp.float32
ANY = pl.BlockSpec(memory_space=pl.ANY)
VM = pl.BlockSpec(memory_space=pltpu.VMEM)


class Place:
    def __init__(self, deep):
        self.Z, self.Y, self.C = deep // 4, 2, 2
        i = lax.axis_index("dp")
        self.t = lax.axis_index("tensor")
        self.c = lax.rem(i, 2)
        self.y = lax.rem(i // 2, 2)
        self.z = i // 4
        far = self.z // 2
        self.outer = 1 - lax.rem(self.z + far, 2)
        self.z_near = self.z + 1 - 2 * lax.rem(self.z, 2)
        self.z_far_inner = 2 - far
        self.z_far_outer = 3 - 3 * far

    def dev(self, z=None, y=None, c=None, t=None):
        z = self.z if z is None else z
        y = self.y if y is None else y
        c = self.c if c is None else c
        t = self.t if t is None else t
        return ((z * self.Y + y) * self.C + c, t)

    def along_z(self, d):
        return self.dev(z=lax.rem(self.z + d, self.Z))

    def source_z(self, d):
        return lax.rem(self.z - d + self.Z, self.Z)

    @property
    def over_y(self):
        return self.dev(y=1 - self.y)

    @property
    def over_c(self):
        return self.dev(c=1 - self.c)

    @property
    def over_t(self):
        return self.dev(t=1 - self.t)

    def greet(self):
        bar = pltpu.get_barrier_semaphore()
        peers = [self.along_z(d) for d in range(1, self.Z)] + [self.over_y, self.over_c, self.over_t]
        for p in peers:
            pl.semaphore_signal(bar, inc=1, device_id=p, device_id_type=MESH)
        pl.semaphore_wait(bar, len(peers))


def rcopy(src, dst, ssem, rsem, dev):
    return pltpu.make_async_remote_copy(src_ref=src, dst_ref=dst, send_sem=ssem, recv_sem=rsem, device_id=dev, device_id_type=MESH)


def dot(a, b):
    return jnp.dot(a, b, preferred_element_type=F32)


def dot_t(a, b):
    return lax.dot_general(a, b, (((1,), (1,)), ((), ())), preferred_element_type=F32)


def dot_0(a, b):
    return lax.dot_general(a, b, (((0,), (0,)), ((), ())), preferred_element_type=F32)


def norm_stats(rows):
    centre = rows - jnp.mean(rows, axis=-1, keepdims=True)
    scale = lax.rsqrt(jnp.mean(centre * centre, axis=-1, keepdims=True) + EPS)
    return centre * scale, scale


def norm_back(e, hat, scale):
    return (e - jnp.mean(e, axis=-1, keepdims=True) - hat * jnp.mean(e * hat, axis=-1, keepdims=True)) * scale


def middle_math(attn, x, wo, wi, wh, b_out, b_in, b_hid, g1, c1, g2, c2, cot, length, first,
                out, dz1, gout, dat, small, hat1_v, s1_v, h1b_v, ht_v, act_v, dg_v, z_v, hat2_v, zt_v,
                put_hid, put_in, ready, turned):
    half, width = hat1_v.shape
    wide = act_v.shape[1]
    rb, step = half // 2, 512

    def by_rows(body):
        def one(r, carry):
            body(pl.ds(pl.multiple_of(r * rb, rb), rb), r)
            return carry

        lax.fori_loop(0, half // rb, one, 0)

    def by_cols(body):
        def one(j, carry):
            body(pl.ds(pl.multiple_of(j * step, step), step), j)
            return carry

        lax.fori_loop(0, wide // step, one, 0)

    def put(n, vec, add):
        for i in range(width // 128):
            at = n * (width // 128) + i
            piece = vec[:, i * 128:(i + 1) * 128]
            small[at:at + 1, :] = small[at:at + 1, :] + piece if add else piece

    small[...] = jnp.zeros_like(small)

    def first_norm(rows, r):
        z1 = x(rows).astype(F32) + dot_t(attn[rows, :], wo()) + b_out[...]
        hat, scale = norm_stats(z1)
        hat1_v[rows, :] = hat
        s1_v[rows, 0:1] = scale
        h1 = hat * g1[...] + c1[...]
        h1b_v[rows, :] = h1.astype(BF)
        z_v[rows, :] = h1 + b_hid[...]

    by_rows(first_norm)

    def up(cols, j):
        pre = dot(h1b_v[...], wi(cols)) + b_in(j)
        phi = jnp.exp(pre * pre * -0.5) * 0.3989422804014327
        cdf = 0.5 + 0.5 * lax.erf(pre * 0.7071067811865476)
        act = (pre * cdf).astype(BF)
        act_v[:, cols] = act
        dg_v[:, cols] = cdf + pre * phi
        z_v[...] += dot_t(act, wh(cols))

    by_cols(up)

    def second_norm(rows, r):
        hat, scale = norm_stats(z_v[rows, :])
        out[rows, :] = (hat * g2[...] + c2[...]).astype(BF)
        at = first + r * rb + lax.broadcasted_iota(jnp.int32, (rb, width), 0)
        dy = jnp.where(at < length, cot[rows, :], 0.0)
        put(2, jnp.sum(dy * hat, axis=0, keepdims=True), True)
        put(3, jnp.sum(dy, axis=0, keepdims=True), True)
        dz2 = norm_back(dy * g2[...], hat, scale)
        put(5, jnp.sum(dz2, axis=0, keepdims=True), True)
        z_v[rows, :] = dz2
        hat2_v[rows, :] = dz2.astype(BF)

    by_rows(second_norm)
    turned()
    zt_v[...] = hat2_v[...].T
    ht_v[...] = h1b_v[...].T
    ready()

    def down(cols, j):
        put_hid(j, dot(zt_v[...], act_v[:, cols]).astype(BF))
        dpre = (dot(hat2_v[...], wh(cols)) * dg_v[:, cols]).astype(BF)
        sums = jnp.sum(dpre.astype(F32), axis=0, keepdims=True)
        for i in range(step // 128):
            small[pl.ds(6 * (width // 128) + j * (step // 128) + i, 1), :] = sums[:, i * 128:(i + 1) * 128]
        put_in(j, dot(ht_v[...], dpre).astype(BF))
        z_v[...] += dot_t(dpre, wi(cols))

    by_cols(down)

    def first_back(rows, r):
        dh1, hat = z_v[rows, :], hat1_v[rows, :]
        put(0, jnp.sum(dh1 * hat, axis=0, keepdims=True), True)
        put(1, jnp.sum(dh1, axis=0, keepdims=True), True)
        d = norm_back(dh1 * g1[...], hat, s1_v[rows, 0:1])
        put(4, jnp.sum(d, axis=0, keepdims=True), True)
        dz1[rows, :] = d
        db = d.astype(BF)
        hat2_v[rows, :] = db
        dat[rows, :] = dot(db, wo()).astype(BF)

    by_rows(first_back)
    zt_v[...] = hat2_v[...].T
    gout[...] = dot(zt_v[...], attn[...]).astype(BF)


class Pass:
    def __init__(self, me, own, view, pair, sems, early=False, wide=False):
        self.me, self.own, self.view, self.pair, self.early, self.wide = me, own, view, pair, early, wide
        self.zs, self.zr, self.fs, self.ys, self.yr, self.xs, self.xr, self.cs, self.cr = sems

    def held(self, z):
        me = self.me
        return self.view(z, slice(None) if self.early else me.y, me.t)

    def source(self):
        return self.held(self.me.z) if self.early else self.own

    def near(self):
        me = self.me
        return rcopy(self.source(), self.held(me.z), self.zs.at[0], self.zr.at[0], me.dev(z=me.z_near))

    def far(self):
        me = self.me
        return rcopy(self.source(), self.held(me.z), self.zs.at[1], self.zr.at[1 + me.outer], me.dev(z=me.z_far_inner))

    def onward(self, n):
        me = self.me
        place = self.held(me.z_far_inner if n == 0 else me.z_far_outer)
        return rcopy(place, place, self.fs.at[n], self.zr.at[1 + n], me.dev(z=me.z_near))

    def z_start(self):
        self.near().start()
        self.far().start()

    def relay(self):
        @pl.when(self.me.outer == 0)
        def _():
            for n in range(2):
                self.onward(n).wait_recv()
                self.onward(n).start()

    def z_wait(self):
        @pl.when(self.me.outer == 1)
        def _():
            for n in range(2):
                self.onward(n).wait_recv()

        self.near().wait_recv()

    def y_copy(self):
        me = self.me
        place = self.view(me.z if self.early else slice(None), me.y, me.t)
        return rcopy(self.own if self.early else place, place, self.ys, self.yr, me.over_y)

    def x_copy(self):
        me = self.me
        place = self.view(slice(None), slice(None), me.t)
        return rcopy(place, place, self.xs, self.xr, me.over_t)

    def c_copy(self):
        return rcopy(self.pair(), self.pair(), self.cs, self.cr, self.me.over_c)

    def finish(self):
        self.near().wait_send()
        self.far().wait_send()

        @pl.when(self.me.outer == 0)
        def _():
            for n in range(2):
                self.onward(n).wait_send()

        self.y_copy().wait_send()
        if self.wide:
            self.x_copy().wait_send()
        self.c_copy().wait_send()


def pass_sems(*lead):
    dma = pltpu.SemaphoreType.DMA
    return [dma(lead + (2,)), dma(lead + (3,)), dma(lead + (2,))] + [dma(lead or (1,))] * 6


def fwd_kernel(deep, x_sh, ml_sh, nz_sh, qkv_sh, out_sh, in_sh, hid_sh, bin_sh, cot_h, bqv, length, *rest):
    fwd_steps(deep, x_sh, ml_sh, nz_sh, qkv_sh, out_sh, in_sh, hid_sh, bin_sh, cot_h, bqv, length, rest[:6], *rest[6:])


def fwd_steps(deep, x_sh, ml_sh, nz_sh, qkv_sh, out_sh, in_sh, hid_sh, bin_sh, cot_h, bqv, length, vec_h,
               q_o, k_o, v_o, lse_o, x_o, mask_o, qkv_o, gate_o, outs_o, dz1_o, ghid_o, gin_o, gout_o, dat_o, small_o,
               x_v, w_v, m_v, q_v, k_v, v_v, a_v, lse_v, out_w, in_w, hid_w, bin_v, attn_v, bias,
               hat1_v, s1_v, h1b_v, ht_v, act_v, dg_v, z_v, hat2_v, zt_v, outs_v, dz1_v, gout_v, dat_v, cot_v, small_v, vec_v,
               loc, gs, xs, xr, as_, ar, *sems):
    me = Place(deep)
    Z = me.Z
    y, c, z, t = me.y, me.c, me.z, me.t
    half = x_sh.shape[0]
    seq, width = x_v.shape
    pairs = q_v.shape[0]
    heads = 2 * pairs
    q_sems, m_sems, w_sems = sems[0:9], sems[9:18], sems[18:27]

    def cols(n):
        return pl.ds(pl.multiple_of(t * n, 128), n)

    rows_own = pl.ds(pl.multiple_of(t * half, 128), half)
    rows_other = pl.ds(pl.multiple_of((1 - t) * half, 128), half)

    P_Q = Pass(me, qkv_sh, lambda zs, ys, ts: w_v.at[zs, ys, c], lambda: w_v.at[:, :, c],
               list(q_sems[:3]) + [s.at[0] for s in q_sems[3:]])

    def M(h):
        return Pass(me, m_v.at[h, z, y, c], lambda zs, ys, ts: m_v.at[h, zs, ys, c], lambda: m_v.at[h, :, :, c],
                    [s.at[h] for s in m_sems])

    def W(k, shard, whole, early):
        n = shard.shape[1]

        def view(zs, ys, ts):
            return whole.at[zs, ys, c, :, pl.ds(pl.multiple_of(ts * n, 128), n)]

        return Pass(me, shard, view, lambda: whole.at[:, :, c], [s.at[k] for s in w_sems], early, True)

    WO, WI, WH = W(0, out_sh, out_w, False), W(1, in_sh, in_w, True), W(2, hid_sh, hid_w, False)

    locals_ = [
        pltpu.make_async_copy(qkv_sh, w_v.at[z, y, c], loc.at[17]),
        pltpu.make_async_copy(x_sh, x_v.at[rows_own], loc.at[16]),
        pltpu.make_async_copy(bin_sh, bin_v.at[t, 0], loc.at[3]),
    ] + [pltpu.make_async_copy(w.own, w.view(z, y, t), loc.at[4 + k]) for k, w in enumerate((WO, WI, WH))]
    raw = ml_sh.shape
    mixed = [pltpu.make_async_copy(a, dg_v.at[pl.ds(0, raw[0]), pl.ds(n * raw[1], raw[1])], loc.at[n])
             for a, n in ((ml_sh, 0), (nz_sh, 1))]
    late = [pltpu.make_async_copy(cot_h, cot_v, loc.at[2])] + [
        pltpu.make_async_copy(a, vec_v.at[n], loc.at[18 + n]) for n, a in enumerate(vec_h)]
    b_out, b_hid, g1, c1, g2, c2 = (vec_v.at[pl.ds(n, 1)] for n in range(6))
    for cp in mixed + locals_ + late:
        cp.start()
    me.greet()

    def x_copy():
        return rcopy(x_sh, x_v.at[rows_own], xs.at[0], xr.at[0], me.over_t)

    def b_copy():
        return rcopy(bin_sh, bin_v.at[t, 0], xs.at[1], xr.at[1], me.over_t)

    def a_cols(p):
        return pl.ds(pl.multiple_of(t * (pairs * 128) + p * 128, 128), 128)

    def a_copy(p):
        return rcopy(a_v.at[p, rows_other], attn_v.at[:, a_cols(p)], as_.at[p], ar.at[p], me.over_t)

    def a_local(p):
        return pltpu.make_async_copy(a_v.at[p, rows_own], attn_v.at[:, a_cols(p)], loc.at[7 + p])

    def mask_save(h):
        return pltpu.make_async_copy(m_v.at[h], mask_o.at[h], loc.at[10 + h])

    P_Q.z_start()
    WI.y_copy().start()
    x_copy().start()
    b_copy().start()
    for cp in mixed:
        cp.wait()
    per = raw[0] // heads

    def mask_of(h):
        rows = pl.ds(pl.multiple_of(h * per, per), per)
        v = dg_v[rows, 0:raw[1]] + dg_v[rows, raw[1]:2 * raw[1]]
        m_v[h, z, y, c] = (jnp.minimum(v, 0.0) - jnp.log1p(jnp.exp(-jnp.abs(v)))).astype(BF)
        dg_v[rows, 2 * raw[1]:3 * raw[1]] = jax.nn.sigmoid(-v)

    mask_of(0)
    M(0).z_start()
    gate_save = pltpu.make_async_copy(dg_v.at[pl.ds(0, raw[0]), pl.ds(2 * raw[1], raw[1])], gate_o, loc.at[0])
    key = lax.broadcasted_iota(jnp.int32, bias.shape, 1)
    bias[...] = jnp.where(key < length[0], 0.0, NEG)
    for cp in locals_:
        cp.wait()
    P_Q.relay()
    P_Q.z_wait()
    P_Q.y_copy().start()
    WH.z_start()
    mask_of(1)
    M(0).relay()
    M(0).z_wait()
    M(0).y_copy().start()
    WI.y_copy().wait_recv()
    WI.z_start()
    WH.relay()
    WH.z_wait()
    WH.y_copy().start()
    M(1).z_start()
    for h in range(2, heads):
        mask_of(h)
    gate_save.start()
    P_Q.y_copy().wait_recv()
    P_Q.c_copy().start()
    x_copy().wait_recv()
    P_Q.c_copy().wait_recv()

    step = half // 2

    def project(r, carry):
        rows = pl.ds(pl.multiple_of(r * step, step), step)
        xb = x_v[rows, :]
        for j, dst in enumerate((q_v, k_v, v_v)):
            w = w_v[:, :, :, j].reshape(width, pairs * 128)
            acc = dot(xb, w)
            if j == 0:
                acc = acc + bqv[0:1, :]
            elif j == 2:
                acc = acc + bqv[1:2, :]
            out = acc.astype(BF)
            if j == 0:
                out = out * jnp.asarray(0.125, BF)
            for p in range(pairs):
                dst[p, rows, :] = out[:, p * 128:(p + 1) * 128]
        return carry

    lax.fori_loop(0, seq // step, project, 0)
    outs = [
        pltpu.make_async_copy(q_v, q_o, loc.at[6]),
        pltpu.make_async_copy(k_v, k_o, loc.at[1]),
        pltpu.make_async_copy(v_v, v_o, loc.at[2]),
        pltpu.make_async_copy(x_v, x_o, loc.at[3]),
        pltpu.make_async_copy(w_v, qkv_o, loc.at[4]),
    ]
    for cp in outs:
        cp.start()
    blk = seq // Z

    def attend(p, u):
        h = 2 * p + u
        sl = slice(64 * u, 64 * u + 64)

        def rows_of(n, carry):
            b = lax.rem((1 - t) * (Z // 2) + n, Z)
            if u == 1:
                @pl.when(n == Z // 2)
                def _():
                    a_copy(p).start()

            rows = pl.ds(pl.multiple_of(b * blk, blk), blk)
            s = dot_t(q_v[p, rows, sl], k_v[p, :, sl])
            s = s + m_v[h, b].reshape(blk, seq).astype(F32) + bias[...]
            top = jnp.max(s, axis=-1, keepdims=True)
            e = jnp.exp(s - top)
            total = jnp.sum(e, axis=-1, keepdims=True)
            o = dot(e.astype(BF), v_v[p, :, sl])
            a_v[p, rows, sl] = (o / total).astype(BF)
            lse_v[p, rows, u:u + 1] = top + jnp.log(total)
            return carry

        lax.fori_loop(0, Z, rows_of, 0)

    def with_0():
        M(1).relay()
        M(1).z_wait()
        M(1).y_copy().start()
        M(2).z_start()

    def with_1():
        M(3).z_start()

    def with_2():
        pass

    def with_3():
        WI.x_copy().wait_recv()
        WI.c_copy().start()

    def with_4():
        WH.x_copy().wait_recv()
        WH.c_copy().start()

    def with_5():
        WO.y_copy().wait_recv()
        WO.x_copy().start()

    def ahead_0():
        pass

    def ahead_1():
        WI.relay()
        WI.z_wait()
        WI.x_copy().start()
        WH.y_copy().wait_recv()
        WH.x_copy().start()
        M(2).relay()
        M(2).z_wait()
        M(2).y_copy().start()

    def ahead_2():
        M(3).relay()
        M(3).z_wait()
        M(3).y_copy().start()
        M(4).z_start()
        WO.z_start()

    def ahead_3():
        M(4).relay()
        M(4).z_wait()
        M(4).y_copy().start()
        M(5).z_start()

    def ahead_4():
        WO.relay()
        WO.z_wait()
        WO.y_copy().start()
        M(5).relay()
        M(5).z_wait()
        M(5).y_copy().start()

    def ahead_5():
        pass

    ahead = (ahead_0, ahead_1, ahead_2, ahead_3, ahead_4, ahead_5)
    beside = (with_0, with_1, with_2, with_3, with_4, with_5)

    def pair_step(p, carry):
        for u in range(2):
            h = 2 * p + u
            for n in range(pairs):
                pl.when(p == n)(ahead[2 * n + u])
            M(h).y_copy().wait_recv()
            M(h).c_copy().start()
            for n in range(pairs):
                pl.when(p == n)(beside[2 * n + u])
            M(h).c_copy().wait_recv()
            mask_save(h).start()
            attend(p, u)
        a_local(p).start()
        return carry

    lax.fori_loop(0, pairs, pair_step, 0)
    lse_out = pltpu.make_async_copy(lse_v, lse_o, loc.at[5])
    lse_out.start()
    WO.x_copy().wait_recv()
    WO.c_copy().start()
    for p in range(pairs):
        a_local(p).wait()
        a_copy(p).wait()
    b_copy().wait()
    for cp in late:
        cp.wait()
    for w in (WI, WH, WO):
        w.c_copy().wait_recv()

    quarter = m_v.shape[1:5]
    deep_w = width // (quarter[0 + 1] * quarter[2] * quarter[3])
    step = seq // 2
    flat = width

    def whole(ref, at):
        return ref[:, :, :, :, at].reshape(flat, -1)

    def slab(j, n):
        return m_v.at[j, pl.ds(0, deep_w), :, :, :, pl.ds(n * step, step)]

    def save(j, n):
        out = (ghid_o, gin_o)[n]
        return pltpu.make_async_copy(slab(j, n), out.at[:, :, :, :, pl.ds(pl.multiple_of(j * step, 128), step)], gs.at[j, n])

    def put(n):
        def one(j, value):
            m_v[j, 0:deep_w, :, :, :, n * step:(n + 1) * step] = value.reshape((deep_w,) + quarter[1:] + (step,))
            save(j, n).start()

        return one

    def ready():
        for h in range(heads):
            M(h).finish()
            mask_save(h).wait()

    outs_save = pltpu.make_async_copy(outs_v, outs_o, loc.at[0])
    per_t = bin_v.shape[2] // step

    def bin_of(j):
        return bin_v[j // per_t, :, pl.ds(pl.multiple_of(lax.rem(j, per_t) * step, 128), step)]

    for cp in outs + [lse_out, gate_save]:
        cp.wait()
    middle_math(attn_v, lambda rows: x_v[pl.ds(pl.multiple_of(t * half + rows.start, 128), rows.size), :],
                lambda: whole(out_w, slice(None)), lambda at: whole(in_w, at), lambda at: whole(hid_w, at),
                b_out, bin_of, b_hid, g1, c1, g2, c2, cot_v, length[0], t * half,
                outs_v, dz1_v, gout_v, dat_v, small_v, hat1_v, s1_v, h1b_v, ht_v, act_v, dg_v, z_v, hat2_v, zt_v,
                put(0), put(1), ready, outs_save.start)
    ends = [pltpu.make_async_copy(a, b, loc.at[1 + n]) for n, (a, b) in enumerate((
        (dz1_v, dz1_o), (gout_v, gout_o), (dat_v, dat_o), (small_v, small_o)))]
    for cp in ends:
        cp.start()
    x_copy().wait_send()
    P_Q.finish()
    for w in (WO, WI, WH):
        w.finish()
    for j in range(heads):
        for n in range(2):
            save(j, n).wait()
    outs_save.wait()
    for cp in ends:
        cp.wait()


def forward(deep, x, ml, nz, qkv, w_out_t, w_in, w_hid_t, b_in, cot, b_qv, length, vectors):
    half, width = x.shape
    seq = 2 * half
    heads, blk, _ = ml.shape
    pairs = heads // 2
    Z, Y, C = deep // 4, 2, 2
    n_out, n_in = w_out_t.shape[1], w_in.shape[1]
    r = w_in.shape[0]
    wide = 2 * n_in
    tall = (width // (Y * C * blk), Y, C, blk)
    rows = 6 * width // 128 + wide // 128
    rows += -rows % 8
    sd, vm = jax.ShapeDtypeStruct, pltpu.VMEM
    dma = pltpu.SemaphoreType.DMA
    out_shape = (
        sd((pairs, seq, 128), BF), sd((pairs, seq, 128), BF), sd((pairs, seq, 128), BF),
        sd((pairs, seq, 128), F32),
        sd((seq, width), BF),
        sd((heads, Z, Y, C, blk, seq), BF),
        sd((Z, Y, C) + qkv.shape, BF), sd((heads * blk, seq), F32),
        sd((half, width), BF), sd((half, width), F32), sd(tall + (wide,), BF), sd(tall + (wide,), BF),
        sd((width, width), BF), sd((half, width), BF), sd((rows, 128), F32),
    )
    pair = vm((pairs, seq, 128), BF)
    return pl.pallas_call(
        functools.partial(fwd_kernel, deep),
        out_shape=out_shape,
        in_specs=[ANY] * 9 + [VM, pl.BlockSpec(memory_space=pltpu.SMEM)] + [ANY] * 6,
        out_specs=[ANY] * len(out_shape),
        scratch_shapes=[
            vm((seq, width), BF),
            vm((Z, Y, C) + qkv.shape, BF),
            vm((heads, Z, Y, C, blk, seq), BF),
            pair, pair, pair, pair, vm((pairs, seq, 128), F32),
            vm((Z, Y, C, r, 2 * n_out), BF), vm((Z, Y, C, r, wide), BF), vm((Z, Y, C, r, wide), BF), vm((2, 1) + b_in.shape, F32),
            vm((half, width), BF), vm((1, seq), F32),
            vm((half, width), F32), vm((half, 128), F32), vm((half, width), BF), vm((width, half), BF), vm((half, wide), BF), vm((half, wide), F32),
            vm((half, width), F32), vm((half, width), BF), vm((width, half), BF),
            vm((half, width), BF), vm((half, width), F32), vm((width, width), BF), vm((half, width), BF), vm((half, width), F32), vm((rows, 128), F32), vm((8, width), F32),
            dma((24,)), dma((heads, 2)), dma((2,)), dma((2,)), dma((pairs,)), dma((pairs,)),
            *pass_sems(), *pass_sems(heads), *pass_sems(3),
        ],
        compiler_params=pltpu.CompilerParams(collective_id=1, has_side_effects=True, vmem_limit_bytes=62 << 20),
        name="forward_attention",
    )(x, ml.reshape(heads * blk, seq), nz.reshape(heads * blk, seq), qkv, w_out_t, w_in, w_hid_t, b_in, cot, b_qv, length, *vectors)


class Fold:
    def __init__(self, me, near_part, far_part, lc, bufs, sems, final, lx=None, early=False, cols=None):
        self.me, self.own, self.away, self.lc = me, near_part, far_part, lc
        self.ly, self.lz, self.lr = bufs
        self.s, self.r = sems
        self.final, self.lx, self.early, self.cols = final, lx, early, cols

    def base(self):
        return self.lc if self.lx is None else self.lx

    def c_copy(self):
        return rcopy(self.away, self.lc, self.s(0), self.r(0), self.me.over_c)

    def c_add(self):
        self.c_copy().wait_recv()

        def one(i, carry):
            for j in range(self.me.Y):
                self.lc[i, j] = self.lc[i, j] + self.own(i, j)
            return carry

        lax.fori_loop(0, self.me.Z, one, 0)

    def x_copy(self):
        me = self.me
        return rcopy(self.lc.at[:, :, :, self.cols(1 - me.t)], self.lx, self.s(1), self.r(1), me.over_t)

    def x_add(self):
        self.x_copy().wait_recv()
        at = self.cols(self.me.t)

        def one(i, carry):
            for j in range(self.me.Y):
                self.lx[i, j] = self.lx[i, j] + self.lc[i, j, :, at]
            return carry

        lax.fori_loop(0, self.me.Z, one, 0)

    def y_copy(self):
        me = self.me
        src = self.base().at[me.z, 1 - me.y] if self.early else self.base().at[:, 1 - me.y]
        return rcopy(src, self.ly, self.s(2), self.r(2), me.over_y)

    def y_add(self):
        self.y_copy().wait_recv()
        base, y = self.base(), self.me.y

        def one(i, carry):
            self.ly[i] = self.ly[i] + base[i, y]
            return carry

        lax.fori_loop(0, self.me.Z, one, 0)

    def along(self):
        return self.base() if self.early else self.ly

    def near(self):
        me = self.me
        return rcopy(self.along().at[me.z_near], self.lz.at[0], self.s(3), self.r(3), me.dev(z=me.z_near))

    def through(self, n):
        me = self.me
        place = self.along().at[me.z_far_inner if n == 0 else me.z_far_outer]
        return rcopy(place, self.lr.at[n], self.s(4 + n), self.r(4 + n), me.dev(z=me.z_near))

    def onward(self, n):
        me = self.me
        z = me.z_far_inner if n == 0 else me.z_far_outer
        return rcopy(self.along().at[z], self.lz.at[1], self.s(6 + n), self.r(6), me.dev(z=z))

    def z_start(self):
        @pl.when(self.me.outer == 1)
        def _():
            for n in range(2):
                self.through(n).start()

        self.near().start()

    def relay(self):
        me = self.me

        @pl.when(me.outer == 0)
        def _():
            for n in range(2):
                self.through(n).wait_recv()
                z = me.z_far_inner if n == 0 else me.z_far_outer
                self.along()[z] = self.along()[z] + self.lr[n]
                self.onward(n).start()

    def z_sum(self):
        self.near().wait_recv()
        self.onward(0).wait_recv()
        total = self.along()[self.me.z].astype(F32) + self.lz[0].astype(F32)
        return total + self.lz[1].astype(F32)

    def z_end(self):
        self.final(self.z_sum())

    def early_z_end(self):
        self.base()[self.me.z] = self.z_sum().astype(BF)
        self.y_copy().start()

    def early_y_end(self):
        self.y_copy().wait_recv()
        self.final(self.base()[self.me.z, self.me.y].astype(F32) + self.ly[...].astype(F32))

    def finish(self, skip_c=False):
        if not skip_c:
            self.c_copy().wait_send()
        if self.lx is not None:
            self.x_copy().wait_send()
        self.y_copy().wait_send()
        self.near().wait_send()

        @pl.when(self.me.outer == 1)
        def _():
            for n in range(2):
                self.through(n).wait_send()

        @pl.when(self.me.outer == 0)
        def _():
            for n in range(2):
                self.onward(n).wait_send()


def bwd_kernel(deep, dat, q_h, k_h, v_h, mask_h, lse_h, x_h, qkv_h, hid_h, in_h, out_h, dz1_h, sg_h, small_h, bias,
               dx_o, gqkv_o, ghid_o, gin_o, gout_o, gmask_o, small_o,
               q_v, k_v, v_v, do_v, lse_v, m_v, p_v, dq_v, dk_v, dv_v, acck, accv,
               lc_m, ly_m, lz_m, lr_m, lz_e, lr_e, gm_v,
               own_w, lc_hid, lx_hid, ly_hid, lz_hid, lr_hid, lc_in, lx_in, ly_in, lz_in, lr_in, lc_out, lx_out, ly_out, lz_out, lr_out,
               fin_hid, fin_in, fin_out,
               p_q, lc_q, ly_q, lz_q, lr_q, fin_q,
               x_v, w_v, sx_v, lx_x, dx_v, dz_v,
               s_v, sc_v, sy_v, sz_v, sx2_v,
               loc, msem, ds_, dr, wl, w_s, w_r, m_s, m_r, q_s, q_r, xs, xr, s1s, s1r, szs, szr):
    me = Place(deep)
    Z, y, c, z, t = me.Z, me.y, me.c, me.z, me.t
    pairs, seq, _ = q_v.shape
    heads = 2 * pairs
    half = seq // 2
    width = x_v.shape[1]
    zs = range(1, Z)
    rows_own = pl.ds(pl.multiple_of(t * half, 128), half)

    def dat_cols(p, who):
        return pl.ds(pl.multiple_of(who * (pairs * 128) + p * 128, 128), 128)

    def dat_local(p):
        return pltpu.make_async_copy(dat.at[:, dat_cols(p, t)], do_v.at[p, rows_own], loc.at[p])

    def dat_copy(p):
        return rcopy(dat.at[:, dat_cols(p, 1 - t)], do_v.at[p, rows_own], ds_.at[p], dr.at[p], me.over_t)

    loads = [pltpu.make_async_copy(a, b, loc.at[3 + n]) for n, (a, b) in enumerate((
        (q_h, q_v), (k_h, k_v), (v_h, v_v), (lse_h, lse_v), (x_h, x_v), (qkv_h, w_v), (dz1_h, dz_v), (small_h, s_v.at[pl.ds(0, small_h.shape[0])])))]

    def m_load(h, slot):
        return pltpu.make_async_copy(mask_h.at[h], m_v.at[slot], msem.at[slot])

    def sg_load(h):
        return pltpu.make_async_copy(sg_h.at[h], gm_v.at[h], loc.at[11 + h])

    def gm_save(h):
        return pltpu.make_async_copy(gm_v.at[h], gmask_o.at[h], loc.at[17 + h])

    def M(h, slot=None):
        early = isinstance(h, int) and h == 1

        def own(i, j):
            return p_v[slot, i, j, c]

        def final(total):
            sg_load(h).wait()
            gm_v[h] = total * gm_v[h]
            gm_save(h).start()

        away = None if slot is None else p_v.at[slot, :, :, 1 - c]
        return Fold(me, own, p_v.at[0, :, :, 1 - c] if away is None else away, lc_m.at[h],
                    (ly_m.at[h, 0], lz_e, lr_e) if early else (ly_m.at[h], lz_m.at[h], lr_m.at[h]),
                    (lambda n: m_s.at[h, n], lambda n: m_r.at[h, n]), final, early=early)

    def W(k, part, lc, lx, ly, lz, lr, fin, out, early):
        n = lx.shape[-1]

        def own(i, j):
            return own_w[i, j, :, 0:2 * n]

        def final(total):
            fin[...] = total
            pltpu.make_async_copy(fin, out, wl.at[3 + k]).start()

        fold = Fold(me, own, part.at[:, :, 1 - c], lc, (ly, lz, lr), (lambda i: w_s.at[k, i], lambda i: w_r.at[k, i]), final,
                    lx, early, lambda who: pl.ds(pl.multiple_of(who * n, 128), n))
        fold.own_load = lambda: pltpu.make_async_copy(part.at[:, :, c], own_w.at[:, :, :, pl.ds(0, 2 * n)], wl.at[k])
        fold.saved = lambda: pltpu.make_async_copy(fin, out, wl.at[3 + k])
        return fold

    WH = W(0, hid_h, lc_hid, lx_hid, ly_hid, lz_hid, lr_hid, fin_hid, ghid_o, False)
    WI = W(1, in_h, lc_in, lx_in, ly_in, lz_in, lr_in, fin_in, gin_o, True)
    WO = W(2, out_h, lc_out, lx_out, ly_out, lz_out, lr_out, fin_out, gout_o, False)

    def q_final(total):
        fin_q[...] = total
        pltpu.make_async_copy(fin_q, gqkv_o, loc.at[24]).start()

    Q = Fold(me, lambda i, j: p_q[i, j, c], p_q.at[:, :, 1 - c], lc_q, (ly_q, lz_q, lr_q),
             (lambda n: q_s.at[n], lambda n: q_r.at[n]), q_final)

    def x_copy():
        return rcopy(sx_v, lx_x, xs, xr, me.over_t)

    def s_c():
        return rcopy(s_v, sc_v, s1s.at[0], s1r.at[0], me.over_c)

    def s_y():
        return rcopy(sc_v, sy_v, s1s.at[1], s1r.at[1], me.over_y)

    def s_z(d):
        return rcopy(sy_v, sz_v.at[z], szs.at[d - 1], szr.at[d - 1], me.along_z(d))

    def s_z_in(d):
        return rcopy(sy_v, sz_v.at[me.source_z(d)], szs.at[d - 1], szr.at[d - 1], me.along_z(d))

    def s_x():
        return rcopy(s_v, sx2_v, s1s.at[2], s1r.at[2], me.over_t)

    m_load(0, 0).start()
    for cp in loads[:4]:
        cp.start()
    for p in range(pairs):
        dat_local(p).start()
    WH.own_load().start()
    for cp in loads[4:]:
        cp.start()
    me.greet()
    for p in range(pairs):
        dat_copy(p).start()
    for w in (WH, WI, WO):
        w.c_copy().start()
    for h in range(heads):
        sg_load(h).start()
    for cp in loads[:4]:
        cp.wait()

    blk = seq // Z
    shape4 = p_v.shape[2:]

    def attend(p, u, slot):
        sl = slice(64 * u, 64 * u + 64)
        acck[...] = jnp.zeros_like(acck)
        accv[...] = jnp.zeros_like(accv)

        def rows_of(n, carry):
            b = lax.rem(t * (Z // 2) + n, Z)
            if u == 0:
                @pl.when(n == Z // 2)
                def _():
                    dat_copy(p).wait_recv()

                @pl.when(jnp.logical_and(n == Z // 2, p == 0))
                def _():
                    WH.own_load().wait()
                    WH.c_add()
                    WI.own_load().start()
                    WH.x_copy().start()

                @pl.when(jnp.logical_and(n == Z // 2 + 1, p == 0))
                def _():
                    WI.own_load().wait()
                    WI.c_add()
                    WO.own_load().start()
                    WI.x_copy().start()

            rows = pl.ds(pl.multiple_of(b * blk, blk), blk)
            qb, dob = q_v[p, rows, sl], do_v[p, rows, sl]
            kk, vv = k_v[p, :, sl], v_v[p, :, sl]
            s = dot_t(qb, kk) + m_v[u, b].reshape(blk, seq).astype(F32) + bias[...]
            pr = jnp.exp(s - lse_v[p, rows, u:u + 1])
            dp = dot_t(dob, vv)
            tt = pr * dp
            delta = jnp.sum(tt, axis=-1, keepdims=True)
            dsb = (tt - pr * delta).astype(BF)
            p_v[slot, b] = dsb.reshape(shape4)
            dq_v[p, rows, sl] = (dot(dsb, kk) * 0.125).astype(BF)
            acck[...] += dot_0(dsb, qb)
            accv[...] += dot_0(pr.astype(BF), dob)
            return carry

        lax.fori_loop(0, Z, rows_of, 0)
        dk_v[p, :, sl] = acck[...].astype(BF)
        dv_v[p, :, sl] = accv[...].astype(BF)

    def after_0():
        M(0, 0).c_add()
        WO.own_load().wait()
        WO.c_add()
        WO.x_copy().start()
        M(0).y_copy().start()

    def after_1():
        M(1, 1).c_add()
        M(1).z_start()

    def after_2():
        M(2, 0).c_add()
        M(2).y_copy().start()
        M(1).relay()
        M(0).y_add()
        M(0).z_start()

    def after_3():
        M(3, 1).c_add()
        M(3).y_copy().start()
        WH.x_add()
        WH.y_copy().start()
        M(0).relay()

    def after_4():
        M(4, 0).c_add()
        M(4).y_copy().start()
        M(2).y_add()
        M(2).z_start()
        M(1).early_z_end()

    def after_5():
        M(5, 1).c_add()
        M(5).y_copy().start()
        M(2).relay()
        M(3).y_add()
        M(3).z_start()

    after = (after_0, after_1, after_2, after_3, after_4, after_5)

    def pair_step(p, carry):
        dat_local(p).wait()
        for u in range(2):
            h = 2 * p + u
            m_load(h, u).wait()
            if u == 0:
                m_load(h + 1, 1).start()
            else:
                @pl.when(p < pairs - 1)
                def _():
                    m_load(h + 1, 0).start()

            @pl.when(p > 0)
            def _():
                M(h - 2, u).c_copy().wait_send()

            attend(p, u, u)
            M(h, u).c_copy().start()
            for n in range(pairs):
                pl.when(p == n)(after[2 * n + u])
        return carry

    lax.fori_loop(0, pairs, pair_step, 0)
    for cp in loads[4:]:
        cp.wait()

    step = half // 2

    def d_cat(ref, rows):
        return jnp.concatenate([ref[p, rows, :] for p in range(pairs)], axis=1)

    def weight(j):
        return w_v[:, :, :, j].reshape(width, pairs * 128)

    def terms(rows):
        acc = dot_t(d_cat(dq_v, rows), weight(0))
        acc = acc + dot_t(d_cat(dk_v, rows), weight(1))
        return acc + dot_t(d_cat(dv_v, rows), weight(2))

    def theirs(r, carry):
        at = pl.ds(pl.multiple_of(r * step, step), step)
        rows = pl.ds(pl.multiple_of((1 - t) * half + r * step, step), step)
        sx_v[at, :] = terms(rows).astype(BF)
        return carry

    lax.fori_loop(0, 2, theirs, 0)
    x_copy().start()
    M(3).relay()
    WI.x_add()
    WI.z_start()
    M(0).z_end()
    WO.x_add()
    WO.y_copy().start()

    for j, ref in enumerate((dq_v, dk_v, dv_v)):
        g = dot_0(x_v[...], d_cat(ref, slice(None)))
        p_q[:, :, :, j] = g.astype(BF).reshape(p_q.shape[:3] + p_q.shape[4:])
    Q.c_copy().start()
    WI.relay()
    base = small_h.shape[0]
    for n, ref in enumerate((dq_v, dv_v)):
        for p in range(pairs):
            at = base + n * pairs + p
            s_v[at:at + 1, :] = jnp.sum(ref[p].astype(F32), axis=0, keepdims=True)
    for at in range(base + 2 * pairs, s_v.shape[0]):
        s_v[at:at + 1, :] = jnp.zeros((1, 128), F32)
    s_c().start()
    Q.c_add()
    Q.y_copy().start()

    def mine(r, carry):
        at = pl.ds(pl.multiple_of(r * step, step), step)
        rows = pl.ds(pl.multiple_of(t * half + r * step, step), step)
        dx_v[at, :] = terms(rows) + dz_v[at, :]
        return carry

    lax.fori_loop(0, 2, mine, 0)
    s_c().wait_recv()
    sc_v[...] = sc_v[...] + s_v[...]
    s_y().start()
    WH.y_add()
    WH.z_start()
    M(2).z_end()
    M(4).y_add()
    M(4).z_start()
    WH.relay()
    WI.early_z_end()
    M(3).z_end()
    M(4).relay()
    M(5).y_add()
    M(5).z_start()
    s_y().wait_recv()
    sy_v[...] = sy_v[...] + sc_v[...]
    sz_v[z] = sy_v[...]
    for d in zs:
        s_z(d).start()
    Q.y_add()
    Q.z_start()
    WH.z_end()
    M(5).relay()
    WO.y_add()
    WO.z_start()
    Q.relay()
    M(4).z_end()
    x_copy().wait_recv()
    dx_v[...] = dx_v[...] + lx_x[...].astype(F32)
    dx_save = pltpu.make_async_copy(dx_v, dx_o, loc.at[23])
    dx_save.start()
    WO.relay()
    for d in zs:
        s_z_in(d).wait_recv()
    s_c().wait_send()
    total = sz_v[0]
    for i in range(1, Z):
        total = total + sz_v[i]
    s_v[...] = total
    s_x().start()
    M(5).z_end()
    M(1).early_y_end()
    WI.early_y_end()
    Q.z_end()
    WO.z_end()
    s_x().wait_recv()
    low = sx2_v[...] + s_v[...]
    row = lax.broadcasted_iota(jnp.int32, low.shape, 0)
    s_y().wait_send()
    sc_v[...] = jnp.where(row < base, low, s_v[...])
    s_save = pltpu.make_async_copy(sc_v, small_o, loc.at[25])
    s_save.start()

    for p in range(pairs):
        dat_copy(p).wait_send()
    for w in (WH, WI, WO):
        w.finish()
        w.saved().wait()
    for h in range(heads):
        M(h).finish(h < heads - 2)
        gm_save(h).wait()
    Q.finish()
    for d in zs:
        s_z(d).wait_send()
    x_copy().wait_send()
    s_x().wait_send()
    dx_save.wait()
    pltpu.make_async_copy(fin_q, gqkv_o, loc.at[24]).wait()
    s_save.wait()


def backward(deep, dat, q, k, v, mask, lse, x, qkv, g_hid, g_in, g_out, dz1, sg, small, bias):
    pairs, seq, _ = q.shape
    half, width = dz1.shape
    heads, Z, Y, C, blk, _ = mask.shape
    r, n2 = g_in.shape[3], g_in.shape[4]
    n2o = g_out.shape[4]
    n, no = n2 // 2, n2o // 2
    base = small.shape[0]
    rows_s = base + 8
    sd = jax.ShapeDtypeStruct
    dma = pltpu.SemaphoreType.DMA
    vm = pltpu.VMEM
    out_shape = (
        sd((half, width), F32), sd(qkv.shape[3:], F32), sd((r, n), F32), sd((r, n), F32), sd((r, no), F32),
        sd((heads, blk, seq), F32), sd((rows_s, 128), F32),
    )
    pair = vm((pairs, seq, 128), BF)

    def chain(m, early):
        last = (Y, r, m) if early else (r, m)
        return [vm((Z, Y, r, 2 * m), BF), vm((Z, Y, r, m), BF), vm((r, m) if early else (Z, r, m), BF), vm((2,) + last, BF), vm((2,) + last, BF)]

    three, rq, nq = qkv.shape[3:]
    return pl.pallas_call(
        functools.partial(bwd_kernel, deep),
        out_shape=out_shape,
        in_specs=[ANY] * 14 + [VM],
        out_specs=[ANY] * len(out_shape),
        scratch_shapes=[
            pair, pair, pair, pair, vm((pairs, seq, 128), F32), vm((2, Z, Y, C, blk, seq), BF), vm((2, Z, Y, C, blk, seq), BF),
            pair, pair, pair, vm((seq, 64), F32), vm((seq, 64), F32),
            vm((heads, Z, Y, blk, seq), BF), vm((heads, Z, blk, seq), BF), vm((heads, 2, blk, seq), BF), vm((heads, 2, blk, seq), BF),
            vm((2, Y, blk, seq), BF), vm((2, Y, blk, seq), BF), vm((heads, blk, seq), F32),
            vm((Z, Y, r, n2), BF), *chain(n, False), *chain(n, True), *chain(no, False), vm((r, n), F32), vm((r, n), F32), vm((r, no), F32),
            vm((Z, Y, C, three, rq, nq), BF), vm((Z, Y, three, rq, nq), BF), vm((Z, three, rq, nq), BF),
            vm((2, three, rq, nq), BF), vm((2, three, rq, nq), BF), vm((three, rq, nq), F32),
            vm((seq, width), BF), vm((Z, Y, C, three, rq, nq), BF), vm((half, width), BF), vm((half, width), BF), vm((half, width), F32), vm((half, width), F32),
            vm((rows_s, 128), F32), vm((rows_s, 128), F32), vm((rows_s, 128), F32), vm((Z, rows_s, 128), F32), vm((rows_s, 128), F32),
            dma((26,)), dma((2,)), dma((pairs,)), dma((pairs,)),
            dma((6,)), dma((3, 8)), dma((3, 7)), dma((heads, 8)), dma((heads, 7)), dma((8,)), dma((7,)), dma, dma,
            dma((3,)), dma((3,)), dma((Z - 1,)), dma((Z - 1,)),
        ],
        compiler_params=pltpu.CompilerParams(collective_id=2, has_side_effects=True, vmem_limit_bytes=62 << 20),
        name="backward_attention",
    )(dat, q, k, v, mask, lse, x, qkv, g_hid, g_in, g_out, dz1, sg, small, bias)


NEG = -1e30
EPS = 1e-12


def layer_norm(value_rows, scale_vec, shift_vec):
    centre = value_rows - jnp.mean(value_rows, axis=-1, keepdims=True)
    spread = jnp.mean(centre * centre, axis=-1, keepdims=True)
    return centre * lax.rsqrt(spread + EPS) * scale_vec + shift_vec


def gelu_exact(value_rows):
    return jax.nn.gelu(value_rows, approximate=False)


def matmul(left, right):
    return jnp.dot(left, right, preferred_element_type=jnp.float32)


def times_transposed(left, right):
    return lax.dot_general(
        left, right, (((1,), (1,)), ((), ())), preferred_element_type=jnp.float32
    )


def over_rows(left, right):
    return lax.dot_general(
        left, right, (((0,), (0,)), ((), ())), preferred_element_type=jnp.float32
    )


def plain_body(
    inputs,
    lengths,
    w_qkv,
    b_qv,
    w_out,
    b_out,
    ln1_gain,
    ln1_bias,
    w_in,
    b_in,
    w_hid,
    b_hid,
    ln2_gain,
    ln2_bias,
    mask_logits,
    noise,
    cotangent,
):
    seq_count, half_rows, width = inputs.shape
    slot_len = half_rows * lax.axis_size("tensor")
    tensor_rank = lax.axis_index("tensor")
    head_count = mask_logits.shape[0]
    head_dim = w_qkv.shape[2] // head_count
    scale = head_dim ** (-0.5)
    token_count = seq_count * slot_len
    mixed_logits = mask_logits + noise
    local_mask = jax.nn.log_sigmoid(mixed_logits).astype(jnp.bfloat16)
    full_qkv, full_out, full_in, full_hid, full_mask = (
        lax.all_gather(w_qkv, "dp", axis=1, tiled=True),
        lax.all_gather(w_out, "dp", axis=1, tiled=True),
        lax.all_gather(w_in, "dp", axis=0, tiled=True),
        lax.all_gather(w_hid, "dp", axis=1, tiled=True),
        lax.all_gather(local_mask, "dp", axis=1, tiled=True),
    )
    key_valid = jnp.arange(slot_len, dtype=jnp.int32)[None, :] < lengths[:, None]
    own_rows = tensor_rank * half_rows + jnp.arange(half_rows, dtype=jnp.int32)
    row_valid = (own_rows[None, :] < lengths[:, None]).astype(jnp.float32)
    gathered = lax.all_gather(inputs, "tensor", axis=1, tiled=True)
    flat_rows = gathered.reshape(token_count, width)
    query_rows = (matmul(flat_rows, full_qkv[0]) + b_qv[0]).astype(jnp.bfloat16)
    key_rows = matmul(flat_rows, full_qkv[1]).astype(jnp.bfloat16)
    value_rows = (matmul(flat_rows, full_qkv[2]) + b_qv[1]).astype(jnp.bfloat16)

    def split_heads(matrix):
        return matrix.reshape(seq_count, slot_len, head_count, head_dim).transpose(0, 2, 1, 3)

    def join_heads(stacked):
        return stacked.transpose(0, 2, 1, 3).reshape(token_count, head_count * head_dim)

    def masked_scores(query_h, keys_h, mask_h, valid_keys):
        score_matrix = (
            jnp.einsum("qd,kd->qk", query_h, keys_h, preferred_element_type=jnp.float32) * scale
        )
        score_matrix = score_matrix + mask_h.astype(jnp.float32)
        return jnp.where(valid_keys[None, :], score_matrix, NEG)

    def attend_sequence(operands):
        query_s, keys_s, values_s, valid_keys = operands

        def attend_head(head_ops):
            query_h, keys_h, values_h, mask_h = head_ops
            score_matrix = masked_scores(query_h, keys_h, mask_h, valid_keys)
            top_score = jnp.max(score_matrix, axis=-1, keepdims=True)
            expo = jnp.exp(score_matrix - top_score)
            row_total = jnp.sum(expo, axis=-1, keepdims=True)
            attention_probabilities = (expo / row_total).astype(jnp.bfloat16)
            result = jnp.einsum(
                "qk,kd->qd", attention_probabilities, values_h, preferred_element_type=jnp.float32
            )
            return (result.astype(jnp.bfloat16), (top_score + jnp.log(row_total))[:, 0])

        return lax.map(attend_head, (query_s, keys_s, values_s, full_mask))

    head_out, log_total = lax.map(
        attend_sequence,
        (split_heads(query_rows), split_heads(key_rows), split_heads(value_rows), key_valid),
    )
    attn = join_heads(head_out)
    attn_terms = matmul(attn, full_out).reshape(seq_count, slot_len, width)
    attn_part = lax.psum_scatter(attn_terms, "tensor", scatter_dimension=1, tiled=True)
    first_sum = inputs.astype(jnp.float32) + attn_part + b_out
    hidden_one = layer_norm(first_sum, ln1_gain, ln1_bias)
    hidden_rows = lax.all_gather(
        hidden_one.astype(jnp.bfloat16), "tensor", axis=1, tiled=True
    ).reshape(token_count, width)
    pre_act = matmul(hidden_rows, full_in) + b_in
    activated = gelu_exact(pre_act).astype(jnp.bfloat16)
    ffn_terms = matmul(activated, full_hid).reshape(seq_count, slot_len, width)
    ffn_part = lax.psum_scatter(ffn_terms, "tensor", scatter_dimension=1, tiled=True)
    second_sum = hidden_one + ffn_part + b_hid
    outputs = layer_norm(second_sum, ln2_gain, ln2_bias).astype(jnp.bfloat16)
    back_qkv, back_out, back_in, back_hid, back_mask = (
        lax.all_gather(w_qkv, "dp", axis=1, tiled=True),
        lax.all_gather(w_out, "dp", axis=1, tiled=True),
        lax.all_gather(w_in, "dp", axis=0, tiled=True),
        lax.all_gather(w_hid, "dp", axis=1, tiled=True),
        lax.all_gather(local_mask, "dp", axis=1, tiled=True),
    )
    grad_output = cotangent * row_valid[:, :, None]
    _, pull_second = jax.vjp(layer_norm, second_sum, ln2_gain, ln2_bias)
    grad_second, ln2_gain_part, ln2_bias_part = pull_second(grad_output)
    b_hid_part = jnp.sum(grad_second, axis=(0, 1))
    second_rows = lax.all_gather(
        grad_second.astype(jnp.bfloat16), "tensor", axis=1, tiled=True
    ).reshape(token_count, width)
    w_hid_grad = over_rows(activated, second_rows)
    grad_act = times_transposed(second_rows, back_hid)
    _, pull_gelu = jax.vjp(gelu_exact, pre_act)
    grad_pre = pull_gelu(grad_act)[0].astype(jnp.bfloat16)
    b_in_part = jnp.sum(grad_pre.astype(jnp.float32), axis=0)
    w_in_grad = over_rows(hidden_rows, grad_pre)
    hidden_terms = times_transposed(grad_pre, back_in).reshape(seq_count, slot_len, width)
    grad_hidden = grad_second + lax.psum_scatter(
        hidden_terms, "tensor", scatter_dimension=1, tiled=True
    )
    _, pull_first = jax.vjp(layer_norm, first_sum, ln1_gain, ln1_bias)
    grad_first, ln1_gain_part, ln1_bias_part = pull_first(grad_hidden)
    b_out_part = jnp.sum(grad_first, axis=(0, 1))
    first_rows = lax.all_gather(
        grad_first.astype(jnp.bfloat16), "tensor", axis=1, tiled=True
    ).reshape(token_count, width)
    w_out_grad = over_rows(attn, first_rows)
    grad_attn = times_transposed(first_rows, back_out).astype(jnp.bfloat16)

    def sequence_back(mask_acc, operands):
        query_s, keys_s, values_s, grad_s, total_s, valid_keys = operands

        def head_back(head_ops):
            query_h, keys_h, values_h, mask_h, grad_h, total_h = head_ops
            score_matrix = masked_scores(query_h, keys_h, mask_h, valid_keys)
            attention_probabilities = jnp.exp(score_matrix - total_h[:, None])
            grad_probs = jnp.einsum(
                "qd,kd->qk", grad_h, values_h, preferred_element_type=jnp.float32
            )
            centre = jnp.sum(attention_probabilities * grad_probs, axis=-1, keepdims=True)
            grad_scores = (attention_probabilities * (grad_probs - centre)).astype(jnp.bfloat16)
            grad_q = (
                jnp.einsum("qk,kd->qd", grad_scores, keys_h, preferred_element_type=jnp.float32)
                * scale
            ).astype(jnp.bfloat16)
            grad_k = (
                jnp.einsum("qk,qd->kd", grad_scores, query_h, preferred_element_type=jnp.float32)
                * scale
            ).astype(jnp.bfloat16)
            grad_v = jnp.einsum(
                "qk,qd->kd",
                attention_probabilities.astype(jnp.bfloat16),
                grad_h,
                preferred_element_type=jnp.float32,
            ).astype(jnp.bfloat16)
            return (grad_q, grad_k, grad_v, grad_scores)

        grad_q, grad_k, grad_v, grad_sc = lax.map(
            head_back, (query_s, keys_s, values_s, back_mask, grad_s, total_s)
        )
        return (mask_acc + grad_sc.astype(jnp.float32), (grad_q, grad_k, grad_v))

    mask_zero = jnp.zeros(back_mask.shape, jnp.float32)
    mask_grad, (heads_q, heads_k, heads_v) = lax.scan(
        sequence_back,
        mask_zero,
        (
            split_heads(query_rows),
            split_heads(key_rows),
            split_heads(value_rows),
            split_heads(grad_attn),
            log_total,
            key_valid,
        ),
    )
    query_grad = join_heads(heads_q)
    keys_grad = join_heads(heads_k)
    values_grad = join_heads(heads_v)
    b_qv_part = jnp.stack(
        [
            jnp.sum(query_grad.astype(jnp.float32), axis=0),
            jnp.sum(values_grad.astype(jnp.float32), axis=0),
        ]
    )
    w_qkv_grad = jnp.stack(
        [
            over_rows(flat_rows, query_grad),
            over_rows(flat_rows, keys_grad),
            over_rows(flat_rows, values_grad),
        ]
    )
    input_terms = (
        times_transposed(query_grad, back_qkv[0])
        + times_transposed(keys_grad, back_qkv[1])
        + times_transposed(values_grad, back_qkv[2])
    ).reshape(seq_count, slot_len, width)
    input_grad = grad_first + lax.psum_scatter(
        input_terms.astype(jnp.bfloat16), "tensor", scatter_dimension=1, tiled=True
    ).astype(jnp.float32)
    qkv_total, out_total, in_total, hid_total, mask_total = (
        lax.psum_scatter(w_qkv_grad, "dp", scatter_dimension=1, tiled=True),
        lax.psum_scatter(w_out_grad, "dp", scatter_dimension=1, tiled=True),
        lax.psum_scatter(w_in_grad, "dp", scatter_dimension=0, tiled=True),
        lax.psum_scatter(w_hid_grad, "dp", scatter_dimension=1, tiled=True),
        lax.psum_scatter(mask_grad, "dp", scatter_dimension=1, tiled=True),
    )
    mask_logit_grad = mask_total * jax.nn.sigmoid(-mixed_logits)
    ln1_gain_total, ln1_bias_total, ln2_gain_total, ln2_bias_total, b_out_total, b_hid_total = (
        lax.psum(
            (ln1_gain_part, ln1_bias_part, ln2_gain_part, ln2_bias_part, b_out_part, b_hid_part),
            ("dp", "tensor"),
        )
    )
    b_qv_total, b_in_total = lax.psum((b_qv_part, b_in_part), "dp")
    return (
        outputs,
        input_grad,
        qkv_total,
        b_qv_total,
        out_total,
        b_out_total,
        ln1_gain_total,
        ln1_bias_total,
        in_total,
        b_in_total,
        hid_total,
        b_hid_total,
        ln2_gain_total,
        ln2_bias_total,
        mask_logit_grad,
    )


def last_kernel(place, total, *refs):
    n = (len(refs) - 10) // 3
    ins, rest = refs[:n], refs[n:]
    (bqv_o, bin_o), vecs, outs = rest[:2], rest[2:8], rest[8:8 + n]
    held, tot_v, sems = rest[8 + n:8 + 2 * n], rest[8 + 2 * n], rest[9 + 2 * n]
    first = pltpu.make_async_copy(total, tot_v, sems.at[n])
    first.start()
    loads = [pltpu.make_async_copy(a, b, sems.at[i]) for i, (a, b) in enumerate(zip(ins, held))]
    saves = [pltpu.make_async_copy(a, b, sems.at[i]) for i, (a, b) in enumerate(zip(held, outs))]
    for cp in loads:
        cp.start()
    for a, b in zip(loads, saves):
        a.wait()
        b.start()
    first.wait()
    t = place[0]
    per = vecs[0].shape[0] // 128
    for k, ref in enumerate(vecs):
        for i in range(per):
            ref[pl.ds(i * 128, 128)] = tot_v[k * per + i, :]
    m = bin_o.shape[0] // 128
    for i in range(m):
        bin_o[pl.ds(i * 128, 128)] = tot_v[6 * per + t * m + i, :]
    base = total.shape[0] - 8
    nq = bqv_o.shape[1] // 128
    for j in range(2):
        for i in range(nq):
            bqv_o[j:j + 1, i * 128:(i + 1) * 128] = tot_v[base + j * nq + i:base + j * nq + i + 1, :]
    for cp in saves:
        cp.wait()


def last(t, total, arrays, width, n_bin, bqv_shape):
    sd, vm = jax.ShapeDtypeStruct, pltpu.VMEM
    n = len(arrays)
    return pl.pallas_call(
        last_kernel,
        out_shape=(sd(bqv_shape, F32), sd((n_bin,), F32)) + (sd((width,), F32),) * 6 + tuple(sd(a.shape, a.dtype) for a in arrays),
        in_specs=[pl.BlockSpec(memory_space=pltpu.SMEM)] + [ANY] * (n + 1),
        out_specs=[VM] * 8 + [ANY] * n,
        scratch_shapes=[vm(a.shape, a.dtype) for a in arrays] + [vm(total.shape, F32), pltpu.SemaphoreType.DMA((n + 1,))],
        compiler_params=pltpu.CompilerParams(vmem_limit_bytes=60 << 20),
        name="hand_over",
    )(t, total, *arrays)


def body(
    inputs, lengths, w_qkv, b_qv, w_out, b_out, ln1_gain, ln1_bias, w_in, b_in, w_hid, b_hid,
    ln2_gain, ln2_bias, mask_logits, noise, cotangent,
):
    deep = lax.axis_size("dp")
    x = inputs[0]
    half, width = x.shape
    seq = 2 * half
    bias = jnp.where(jnp.arange(seq, dtype=jnp.int32) < lengths[0], 0.0, NEG).astype(F32).reshape(1, seq)
    vectors = (b_out, b_hid, ln1_gain, ln1_bias, ln2_gain, ln2_bias)
    q, k, v, lse, x_all, mask_all, qkv_all, gate, outputs, dz1, g_hid, g_in, g_out, dattn, small = forward(
        deep, x, mask_logits, noise, w_qkv, w_out.T, w_in, w_hid.T, b_in, cotangent[0], b_qv, lengths, vectors)
    place = (deep // 4, 2, 2, w_in.shape[0])
    dx, gqkv, ghid, gin, gout, gmask, total = backward(
        deep, dattn, q, k, v, mask_all, lse, x_all, qkv_all,
        g_hid.reshape(place + (-1,)), g_in.reshape(place + (-1,)), g_out.reshape(place + (-1,)), dz1, gate.reshape(mask_logits.shape), small, bias)
    t = lax.axis_index("tensor").astype(jnp.int32).reshape(1)
    g_bqv, g_bin, v0, v1, v2, v3, v4, v5, outputs, dx, gqkv, gout, gin, ghid, gmask = last(
        t, total, (outputs, dx, gqkv, gout, gin, ghid, gmask), width, b_in.shape[0], b_qv.shape)
    return (outputs[None], dx[None], gqkv, g_bqv, gout.T, v4, v0, v1, gin, g_bin, ghid.T, v5, v2, v3, gmask)


def solution(mesh):
    placed = (
        P("dp", "tensor", None),
        P("dp"),
        P(None, "dp", "tensor"),
        P(None, "tensor"),
        P("tensor", "dp"),
        P(),
        P(),
        P(),
        P("dp", "tensor"),
        P("tensor"),
        P("tensor", "dp"),
        P(),
        P(),
        P(),
        P("tensor", "dp", None),
        P("tensor", "dp", None),
        P("dp", "tensor", None),
    )

    def run(*args):
        w_rows, m_rows = args[8].shape[0], args[14].shape[1]
        tiled = w_rows % 16 == 0 and m_rows % 16 == 0 and args[0].shape[0] == 1 and mesh.shape["dp"] == 16
        return (body if tiled else plain_body)(*args)

    return jax.shard_map(
        run,
        mesh=mesh,
        in_specs=placed,
        out_specs=(
            P("dp", "tensor", None),
            P("dp", "tensor", None),
            P(None, "dp", "tensor"),
            P(None, "tensor"),
            P("tensor", "dp"),
            P(),
            P(),
            P(),
            P("dp", "tensor"),
            P("tensor"),
            P("tensor", "dp"),
            P(),
            P(),
            P(),
            P("tensor", "dp", None),
        ),
        check_vma=False,
    )
```

```python
import functools

import jax
import jax.numpy as jnp
from jax import lax
from jax.experimental import pallas as pl
from jax.experimental.pallas import tpu as pltpu
from jax.sharding import PartitionSpec as P

MESH = pl.DeviceIdType.MESH
BF, F32 = jnp.bfloat16, jnp.float32
ANY = pl.BlockSpec(memory_space=pl.ANY)
VM = pl.BlockSpec(memory_space=pltpu.VMEM)


class Place:
    def __init__(self, deep):
        self.Z, self.Y, self.C = deep // 4, 2, 2
        i = lax.axis_index("dp")
        self.t = lax.axis_index("tensor")
        self.c = lax.rem(i, 2)
        self.y = lax.rem(i // 2, 2)
        self.z = i // 4
        far = self.z // 2
        self.outer = 1 - lax.rem(self.z + far, 2)
        self.z_near = self.z + 1 - 2 * lax.rem(self.z, 2)
        self.z_far_inner = 2 - far
        self.z_far_outer = 3 - 3 * far

    def dev(self, z=None, y=None, c=None, t=None):
        z = self.z if z is None else z
        y = self.y if y is None else y
        c = self.c if c is None else c
        t = self.t if t is None else t
        return ((z * self.Y + y) * self.C + c, t)

    def along_z(self, d):
        return self.dev(z=lax.rem(self.z + d, self.Z))

    def source_z(self, d):
        return lax.rem(self.z - d + self.Z, self.Z)

    @property
    def over_y(self):
        return self.dev(y=1 - self.y)

    @property
    def over_c(self):
        return self.dev(c=1 - self.c)

    @property
    def over_t(self):
        return self.dev(t=1 - self.t)

    def greet(self):
        bar = pltpu.get_barrier_semaphore()
        peers = [self.along_z(d) for d in range(1, self.Z)] + [self.over_y, self.over_c, self.over_t]
        for p in peers:
            pl.semaphore_signal(bar, inc=1, device_id=p, device_id_type=MESH)
        pl.semaphore_wait(bar, len(peers))


def rcopy(src, dst, ssem, rsem, dev):
    return pltpu.make_async_remote_copy(src_ref=src, dst_ref=dst, send_sem=ssem, recv_sem=rsem, device_id=dev, device_id_type=MESH)


def dot(a, b):
    return jnp.dot(a, b, preferred_element_type=F32)


def dot_t(a, b):
    return lax.dot_general(a, b, (((1,), (1,)), ((), ())), preferred_element_type=F32)


def dot_0(a, b):
    return lax.dot_general(a, b, (((0,), (0,)), ((), ())), preferred_element_type=F32)


def norm_stats(rows):
    centre = rows - jnp.mean(rows, axis=-1, keepdims=True)
    scale = lax.rsqrt(jnp.mean(centre * centre, axis=-1, keepdims=True) + EPS)
    return centre * scale, scale


def norm_back(e, hat, scale):
    return (e - jnp.mean(e, axis=-1, keepdims=True) - hat * jnp.mean(e * hat, axis=-1, keepdims=True)) * scale


def middle_math(attn, x, wo, wi, wh, b_out, b_in, b_hid, g1, c1, g2, c2, cot, length, first,
                out, dz1, gout, dat, small, hat1_v, s1_v, h1b_v, ht_v, act_v, dg_v, z_v, hat2_v, zt_v,
                put_hid, put_in, ready, turned):
    half, width = hat1_v.shape
    wide = act_v.shape[1]
    rb, step = half, 512

    def by_rows(body):
        def one(r, carry):
            body(pl.ds(pl.multiple_of(r * rb, rb), rb), r)
            return carry

        lax.fori_loop(0, half // rb, one, 0)

    def by_cols(body):
        def one(j, carry):
            body(pl.ds(pl.multiple_of(j * step, step), step), j)
            return carry

        lax.fori_loop(0, wide // step, one, 0, unroll=3)

    def put(n, vec, add):
        for i in range(width // 128):
            at = n * (width // 128) + i
            piece = vec[:, i * 128:(i + 1) * 128]
            small[at:at + 1, :] = small[at:at + 1, :] + piece if add else piece

    small[...] = jnp.zeros_like(small)

    def first_norm(rows, r):
        z1 = x(rows).astype(F32) + dot_t(attn[rows, :], wo()) + b_out[...]
        hat, scale = norm_stats(z1)
        hat1_v[rows, :] = hat
        s1_v[rows, 0:1] = scale
        h1 = hat * g1[...] + c1[...]
        h1b_v[rows, :] = h1.astype(BF)
        z_v[rows, :] = h1 + b_hid[...]

    by_rows(first_norm)

    def up(cols, j):
        pre = dot(h1b_v[...], wi(cols)) + b_in(j)
        phi = jnp.exp(pre * pre * -0.5) * 0.3989422804014327
        cdf = 0.5 + 0.5 * lax.erf(pre * 0.7071067811865476)
        act = (pre * cdf).astype(BF)
        act_v[:, cols] = act
        dg_v[:, cols] = cdf + pre * phi
        z_v[...] += dot_t(act, wh(cols))

    by_cols(up)

    def second_norm(rows, r):
        hat, scale = norm_stats(z_v[rows, :])
        out[rows, :] = (hat * g2[...] + c2[...]).astype(BF)
        at = first + r * rb + lax.broadcasted_iota(jnp.int32, (rb, width), 0)
        dy = jnp.where(at < length, cot[rows, :], 0.0)
        put(2, jnp.sum(dy * hat, axis=0, keepdims=True), True)
        put(3, jnp.sum(dy, axis=0, keepdims=True), True)
        dz2 = norm_back(dy * g2[...], hat, scale)
        put(5, jnp.sum(dz2, axis=0, keepdims=True), True)
        z_v[rows, :] = dz2
        hat2_v[rows, :] = dz2.astype(BF)

    by_rows(second_norm)
    turned()
    zt_v[...] = hat2_v[...].T
    ht_v[...] = h1b_v[...].T
    ready()

    def down(cols, j):
        put_hid(j, dot(zt_v[...], act_v[:, cols]).astype(BF))
        dpre = (dot(hat2_v[...], wh(cols)) * dg_v[:, cols]).astype(BF)
        sums = jnp.sum(dpre.astype(F32), axis=0, keepdims=True)
        for i in range(step // 128):
            small[pl.ds(6 * (width // 128) + j * (step // 128) + i, 1), :] = sums[:, i * 128:(i + 1) * 128]
        put_in(j, dot(ht_v[...], dpre).astype(BF))
        z_v[...] += dot_t(dpre, wi(cols))

    by_cols(down)

    def first_back(rows, r):
        dh1, hat = z_v[rows, :], hat1_v[rows, :]
        put(0, jnp.sum(dh1 * hat, axis=0, keepdims=True), True)
        put(1, jnp.sum(dh1, axis=0, keepdims=True), True)
        d = norm_back(dh1 * g1[...], hat, s1_v[rows, 0:1])
        put(4, jnp.sum(d, axis=0, keepdims=True), True)
        dz1[rows, :] = d
        db = d.astype(BF)
        hat2_v[rows, :] = db
        dat[rows, :] = dot(db, wo()).astype(BF)

    by_rows(first_back)
    zt_v[...] = hat2_v[...].T
    gout[...] = dot(zt_v[...], attn[...]).astype(BF)


class Pass:
    def __init__(self, me, own, view, pair, sems, early=False, wide=False):
        self.me, self.own, self.view, self.pair, self.early, self.wide = me, own, view, pair, early, wide
        self.zs, self.zr, self.fs, self.ys, self.yr, self.xs, self.xr, self.cs, self.cr = sems

    def held(self, z):
        me = self.me
        return self.view(z, slice(None) if self.early else me.y, me.t)

    def source(self):
        return self.held(self.me.z) if self.early else self.own

    def near(self):
        me = self.me
        return rcopy(self.source(), self.held(me.z), self.zs.at[0], self.zr.at[0], me.dev(z=me.z_near))

    def far(self):
        me = self.me
        return rcopy(self.source(), self.held(me.z), self.zs.at[1], self.zr.at[1 + me.outer], me.dev(z=me.z_far_inner))

    def onward(self, n):
        me = self.me
        place = self.held(me.z_far_inner if n == 0 else me.z_far_outer)
        return rcopy(place, place, self.fs.at[n], self.zr.at[1 + n], me.dev(z=me.z_near))

    def z_start(self):
        self.near().start()
        self.far().start()

    def relay(self):
        @pl.when(self.me.outer == 0)
        def _():
            for n in range(2):
                self.onward(n).wait_recv()
                self.onward(n).start()

    def z_wait(self):
        @pl.when(self.me.outer == 1)
        def _():
            for n in range(2):
                self.onward(n).wait_recv()

        self.near().wait_recv()

    def y_copy(self):
        me = self.me
        place = self.view(me.z if self.early else slice(None), me.y, me.t)
        return rcopy(self.own if self.early else place, place, self.ys, self.yr, me.over_y)

    def x_copy(self):
        me = self.me
        place = self.view(slice(None), slice(None), me.t)
        return rcopy(place, place, self.xs, self.xr, me.over_t)

    def c_copy(self):
        return rcopy(self.pair(), self.pair(), self.cs, self.cr, self.me.over_c)

    def finish(self):
        self.near().wait_send()
        self.far().wait_send()

        @pl.when(self.me.outer == 0)
        def _():
            for n in range(2):
                self.onward(n).wait_send()

        self.y_copy().wait_send()
        if self.wide:
            self.x_copy().wait_send()
        self.c_copy().wait_send()


def pass_sems(*lead):
    dma = pltpu.SemaphoreType.DMA
    return [dma(lead + (2,)), dma(lead + (3,)), dma(lead + (2,))] + [dma(lead or (1,))] * 6


def fwd_kernel(deep, x_sh, ml_sh, nz_sh, qkv_sh, out_sh, in_sh, hid_sh, bin_sh, cot_h, bqv, length, *rest):
    fwd_steps(deep, x_sh, ml_sh, nz_sh, qkv_sh, out_sh, in_sh, hid_sh, bin_sh, cot_h, bqv, length, rest[:6], *rest[6:])


def fwd_steps(deep, x_sh, ml_sh, nz_sh, qkv_sh, out_sh, in_sh, hid_sh, bin_sh, cot_h, bqv, length, vec_h,
               q_o, k_o, v_o, lse_o, x_o, mask_o, qkv_o, gate_o, outs_o, dz1_o, ghid_o, gin_o, gout_o, dat_o, small_o,
               x_v, w_v, m_v, q_v, k_v, v_v, a_v, lse_v, out_w, in_w, hid_w, bin_v, attn_v, bias,
               hat1_v, s1_v, h1b_v, ht_v, act_v, dg_v, z_v, hat2_v, zt_v, outs_v, dz1_v, gout_v, dat_v, cot_v, small_v, vec_v,
               loc, gs, xs, xr, as_, ar, *sems):
    me = Place(deep)
    Z = me.Z
    y, c, z, t = me.y, me.c, me.z, me.t
    half = x_sh.shape[0]
    seq, width = x_v.shape
    pairs = q_v.shape[0]
    heads = 2 * pairs
    q_sems, m_sems, w_sems = sems[0:9], sems[9:18], sems[18:27]

    def cols(n):
        return pl.ds(pl.multiple_of(t * n, 128), n)

    rows_own = pl.ds(pl.multiple_of(t * half, 128), half)
    rows_other = pl.ds(pl.multiple_of((1 - t) * half, 128), half)

    P_Q = Pass(me, qkv_sh, lambda zs, ys, ts: w_v.at[zs, ys, c], lambda: w_v.at[:, :, c],
               list(q_sems[:3]) + [s.at[0] for s in q_sems[3:]])

    def M(h):
        return Pass(me, m_v.at[h, z, y, c], lambda zs, ys, ts: m_v.at[h, zs, ys, c], lambda: m_v.at[h, :, :, c],
                    [s.at[h] for s in m_sems])

    def W(k, shard, whole, early):
        n = shard.shape[1]

        def view(zs, ys, ts):
            return whole.at[zs, ys, c, :, pl.ds(pl.multiple_of(ts * n, 128), n)]

        return Pass(me, shard, view, lambda: whole.at[:, :, c], [s.at[k] for s in w_sems], early, True)

    WO, WI, WH = W(0, out_sh, out_w, False), W(1, in_sh, in_w, True), W(2, hid_sh, hid_w, False)

    locals_ = [
        pltpu.make_async_copy(qkv_sh, w_v.at[z, y, c], loc.at[17]),
        pltpu.make_async_copy(x_sh, x_v.at[rows_own], loc.at[16]),
        pltpu.make_async_copy(bin_sh, bin_v.at[t, 0], loc.at[3]),
    ] + [pltpu.make_async_copy(w.own, w.view(z, y, t), loc.at[4 + k]) for k, w in enumerate((WO, WI, WH))]
    raw = ml_sh.shape
    mixed = [pltpu.make_async_copy(a, dg_v.at[pl.ds(0, raw[0]), pl.ds(n * raw[1], raw[1])], loc.at[n])
             for a, n in ((ml_sh, 0), (nz_sh, 1))]
    late = [pltpu.make_async_copy(cot_h, cot_v, loc.at[2])] + [
        pltpu.make_async_copy(a, vec_v.at[n], loc.at[18 + n]) for n, a in enumerate(vec_h)]
    b_out, b_hid, g1, c1, g2, c2 = (vec_v.at[pl.ds(n, 1)] for n in range(6))
    for cp in mixed + locals_ + late:
        cp.start()
    me.greet()

    def x_copy():
        return rcopy(x_sh, x_v.at[rows_own], xs.at[0], xr.at[0], me.over_t)

    def b_copy():
        return rcopy(bin_sh, bin_v.at[t, 0], xs.at[1], xr.at[1], me.over_t)

    def a_cols(p):
        return pl.ds(pl.multiple_of(t * (pairs * 128) + p * 128, 128), 128)

    def a_copy(p):
        return rcopy(a_v.at[p, rows_other], attn_v.at[:, a_cols(p)], as_.at[p], ar.at[p], me.over_t)

    def a_local(p):
        return pltpu.make_async_copy(a_v.at[p, rows_own], attn_v.at[:, a_cols(p)], loc.at[7 + p])

    def mask_save(h):
        return pltpu.make_async_copy(m_v.at[h], mask_o.at[h], loc.at[10 + h])

    P_Q.z_start()
    WI.y_copy().start()
    x_copy().start()
    b_copy().start()
    for cp in mixed:
        cp.wait()
    per = raw[0] // heads

    def mask_of(h):
        rows = pl.ds(pl.multiple_of(h * per, per), per)
        v = dg_v[rows, 0:raw[1]] + dg_v[rows, raw[1]:2 * raw[1]]
        m_v[h, z, y, c] = (jnp.minimum(v, 0.0) - jnp.log1p(jnp.exp(-jnp.abs(v)))).astype(BF)
        dg_v[rows, 2 * raw[1]:3 * raw[1]] = jax.nn.sigmoid(-v)

    mask_of(0)
    M(0).z_start()
    gate_save = pltpu.make_async_copy(dg_v.at[pl.ds(0, raw[0]), pl.ds(2 * raw[1], raw[1])], gate_o, loc.at[0])
    key = lax.broadcasted_iota(jnp.int32, bias.shape, 1)
    bias[...] = jnp.where(key < length[0], 0.0, NEG)
    for cp in locals_:
        cp.wait()
    P_Q.relay()
    P_Q.z_wait()
    P_Q.y_copy().start()
    WH.z_start()
    mask_of(1)
    M(0).relay()
    M(0).z_wait()
    M(0).y_copy().start()
    WI.y_copy().wait_recv()
    WI.z_start()
    WH.relay()
    WH.z_wait()
    WH.y_copy().start()
    M(1).z_start()
    for h in range(2, heads):
        mask_of(h)
    gate_save.start()
    P_Q.y_copy().wait_recv()
    P_Q.c_copy().start()
    x_copy().wait_recv()
    P_Q.c_copy().wait_recv()

    step = half // 2

    def project(r, carry):
        rows = pl.ds(pl.multiple_of(r * step, step), step)
        xb = x_v[rows, :]
        for j, dst in enumerate((q_v, k_v, v_v)):
            w = w_v[:, :, :, j].reshape(width, pairs * 128)
            acc = dot(xb, w)
            if j == 0:
                acc = acc + bqv[0:1, :]
            elif j == 2:
                acc = acc + bqv[1:2, :]
            out = acc.astype(BF)
            if j == 0:
                out = out * jnp.asarray(0.125, BF)
            for p in range(pairs):
                dst[p, rows, :] = out[:, p * 128:(p + 1) * 128]
        return carry

    lax.fori_loop(0, seq // step, project, 0)
    outs = [
        pltpu.make_async_copy(q_v, q_o, loc.at[6]),
        pltpu.make_async_copy(k_v, k_o, loc.at[1]),
        pltpu.make_async_copy(v_v, v_o, loc.at[2]),
        pltpu.make_async_copy(x_v, x_o, loc.at[3]),
        pltpu.make_async_copy(w_v, qkv_o, loc.at[4]),
    ]
    for cp in outs:
        cp.start()
    blk = seq // Z

    def attend(p, u):
        h = 2 * p + u
        sl = slice(64 * u, 64 * u + 64)

        def rows_of(n, carry):
            b = lax.rem((1 - t) * (Z // 2) + n, Z)
            if u == 1:
                @pl.when(n == Z // 2)
                def _():
                    a_copy(p).start()

            rows = pl.ds(pl.multiple_of(b * blk, blk), blk)
            s = dot_t(q_v[p, rows, sl], k_v[p, :, sl])
            s = s + m_v[h, b].reshape(blk, seq).astype(F32) + bias[...]
            top = jnp.max(s, axis=-1, keepdims=True)
            e = jnp.exp(s - top)
            total = jnp.sum(e, axis=-1, keepdims=True)
            o = dot(e.astype(BF), v_v[p, :, sl])
            a_v[p, rows, sl] = (o / total).astype(BF)
            lse_v[p, rows, u:u + 1] = top + jnp.log(total)
            return carry

        lax.fori_loop(0, Z, rows_of, 0, unroll=2)

    def with_0():
        M(1).relay()
        M(1).z_wait()
        M(1).y_copy().start()
        M(2).z_start()

    def with_1():
        M(3).z_start()

    def with_2():
        pass

    def with_3():
        WI.x_copy().wait_recv()
        WI.c_copy().start()

    def with_4():
        WH.x_copy().wait_recv()
        WH.c_copy().start()

    def with_5():
        WO.y_copy().wait_recv()
        WO.x_copy().start()

    def ahead_0():
        pass

    def ahead_1():
        WI.relay()
        WI.z_wait()
        WI.x_copy().start()
        WH.y_copy().wait_recv()
        WH.x_copy().start()
        M(2).relay()
        M(2).z_wait()
        M(2).y_copy().start()

    def ahead_2():
        M(3).relay()
        M(3).z_wait()
        M(3).y_copy().start()
        M(4).z_start()
        WO.z_start()

    def ahead_3():
        M(4).relay()
        M(4).z_wait()
        M(4).y_copy().start()
        M(5).z_start()

    def ahead_4():
        WO.relay()
        WO.z_wait()
        WO.y_copy().start()
        M(5).relay()
        M(5).z_wait()
        M(5).y_copy().start()

    def ahead_5():
        pass

    ahead = (ahead_0, ahead_1, ahead_2, ahead_3, ahead_4, ahead_5)
    beside = (with_0, with_1, with_2, with_3, with_4, with_5)

    def pair_step(p, carry):
        for u in range(2):
            h = 2 * p + u
            for n in range(pairs):
                pl.when(p == n)(ahead[2 * n + u])
            M(h).y_copy().wait_recv()
            M(h).c_copy().start()
            for n in range(pairs):
                pl.when(p == n)(beside[2 * n + u])
            M(h).c_copy().wait_recv()
            mask_save(h).start()
            attend(p, u)
        a_local(p).start()
        return carry

    lax.fori_loop(0, pairs, pair_step, 0)
    lse_out = pltpu.make_async_copy(lse_v, lse_o, loc.at[5])
    lse_out.start()
    WO.x_copy().wait_recv()
    WO.c_copy().start()
    for p in range(pairs):
        a_local(p).wait()
        a_copy(p).wait()
    b_copy().wait()
    for cp in late:
        cp.wait()
    for w in (WI, WH, WO):
        w.c_copy().wait_recv()

    quarter = m_v.shape[1:5]
    deep_w = width // (quarter[0 + 1] * quarter[2] * quarter[3])
    step = seq // 2
    flat = width

    def whole(ref, at):
        return ref[:, :, :, :, at].reshape(flat, -1)

    def slab(j, n):
        return m_v.at[j, pl.ds(0, deep_w), :, :, :, pl.ds(n * step, step)]

    def save(j, n):
        out = (ghid_o, gin_o)[n]
        return pltpu.make_async_copy(slab(j, n), out.at[:, :, :, :, pl.ds(pl.multiple_of(j * step, 128), step)], gs.at[j, n])

    def put(n):
        def one(j, value):
            m_v[j, 0:deep_w, :, :, :, n * step:(n + 1) * step] = value.reshape((deep_w,) + quarter[1:] + (step,))
            save(j, n).start()

        return one

    def ready():
        for h in range(heads):
            M(h).finish()
            mask_save(h).wait()

    outs_save = pltpu.make_async_copy(outs_v, outs_o, loc.at[0])
    per_t = bin_v.shape[2] // step

    def bin_of(j):
        return bin_v[j // per_t, :, pl.ds(pl.multiple_of(lax.rem(j, per_t) * step, 128), step)]

    for cp in outs + [lse_out, gate_save]:
        cp.wait()
    middle_math(attn_v, lambda rows: x_v[pl.ds(pl.multiple_of(t * half + rows.start, 128), rows.size), :],
                lambda: whole(out_w, slice(None)), lambda at: whole(in_w, at), lambda at: whole(hid_w, at),
                b_out, bin_of, b_hid, g1, c1, g2, c2, cot_v, length[0], t * half,
                outs_v, dz1_v, gout_v, dat_v, small_v, hat1_v, s1_v, h1b_v, ht_v, act_v, dg_v, z_v, hat2_v, zt_v,
                put(0), put(1), ready, outs_save.start)
    ends = [pltpu.make_async_copy(a, b, loc.at[1 + n]) for n, (a, b) in enumerate((
        (dz1_v, dz1_o), (gout_v, gout_o), (dat_v, dat_o), (small_v, small_o)))]
    for cp in ends:
        cp.start()
    x_copy().wait_send()
    P_Q.finish()
    for w in (WO, WI, WH):
        w.finish()
    for j in range(heads):
        for n in range(2):
            save(j, n).wait()
    outs_save.wait()
    for cp in ends:
        cp.wait()


def forward(deep, x, ml, nz, qkv, w_out_t, w_in, w_hid_t, b_in, cot, b_qv, length, vectors):
    half, width = x.shape
    seq = 2 * half
    heads, blk, _ = ml.shape
    pairs = heads // 2
    Z, Y, C = deep // 4, 2, 2
    n_out, n_in = w_out_t.shape[1], w_in.shape[1]
    r = w_in.shape[0]
    wide = 2 * n_in
    tall = (width // (Y * C * blk), Y, C, blk)
    rows = 6 * width // 128 + wide // 128
    rows += -rows % 8
    sd, vm = jax.ShapeDtypeStruct, pltpu.VMEM
    dma = pltpu.SemaphoreType.DMA
    out_shape = (
        sd((pairs, seq, 128), BF), sd((pairs, seq, 128), BF), sd((pairs, seq, 128), BF),
        sd((pairs, seq, 128), F32),
        sd((seq, width), BF),
        sd((heads, Z, Y, C, blk, seq), BF),
        sd((Z, Y, C) + qkv.shape, BF), sd((heads * blk, seq), F32),
        sd((half, width), BF), sd((half, width), F32), sd(tall + (wide,), BF), sd(tall + (wide,), BF),
        sd((width, width), BF), sd((half, width), BF), sd((rows, 128), F32),
    )
    pair = vm((pairs, seq, 128), BF)
    return pl.pallas_call(
        functools.partial(fwd_kernel, deep),
        out_shape=out_shape,
        in_specs=[ANY] * 9 + [VM, pl.BlockSpec(memory_space=pltpu.SMEM)] + [ANY] * 6,
        out_specs=[ANY] * len(out_shape),
        scratch_shapes=[
            vm((seq, width), BF),
            vm((Z, Y, C) + qkv.shape, BF),
            vm((heads, Z, Y, C, blk, seq), BF),
            pair, pair, pair, pair, vm((pairs, seq, 128), F32),
            vm((Z, Y, C, r, 2 * n_out), BF), vm((Z, Y, C, r, wide), BF), vm((Z, Y, C, r, wide), BF), vm((2, 1) + b_in.shape, F32),
            vm((half, width), BF), vm((1, seq), F32),
            vm((half, width), F32), vm((half, 128), F32), vm((half, width), BF), vm((width, half), BF), vm((half, wide), BF), vm((half, wide), F32),
            vm((half, width), F32), vm((half, width), BF), vm((width, half), BF),
            vm((half, width), BF), vm((half, width), F32), vm((width, width), BF), vm((half, width), BF), vm((half, width), F32), vm((rows, 128), F32), vm((8, width), F32),
            dma((24,)), dma((heads, 2)), dma((2,)), dma((2,)), dma((pairs,)), dma((pairs,)),
            *pass_sems(), *pass_sems(heads), *pass_sems(3),
        ],
        compiler_params=pltpu.CompilerParams(collective_id=1, has_side_effects=True, vmem_limit_bytes=62 << 20),
        name="forward_attention",
    )(x, ml.reshape(heads * blk, seq), nz.reshape(heads * blk, seq), qkv, w_out_t, w_in, w_hid_t, b_in, cot, b_qv, length, *vectors)


class Fold:
    def __init__(self, me, near_part, far_part, lc, bufs, sems, final, lx=None, early=False, cols=None):
        self.me, self.own, self.away, self.lc = me, near_part, far_part, lc
        self.ly, self.lz, self.lr = bufs
        self.s, self.r = sems
        self.final, self.lx, self.early, self.cols = final, lx, early, cols

    def base(self):
        return self.lc if self.lx is None else self.lx

    def c_copy(self):
        return rcopy(self.away, self.lc, self.s(0), self.r(0), self.me.over_c)

    def c_add(self):
        self.c_copy().wait_recv()

        def one(i, carry):
            for j in range(self.me.Y):
                self.lc[i, j] = self.lc[i, j] + self.own(i, j)
            return carry

        lax.fori_loop(0, self.me.Z, one, 0)

    def x_copy(self):
        me = self.me
        return rcopy(self.lc.at[:, :, :, self.cols(1 - me.t)], self.lx, self.s(1), self.r(1), me.over_t)

    def x_add(self):
        self.x_copy().wait_recv()
        at = self.cols(self.me.t)

        def one(i, carry):
            for j in range(self.me.Y):
                self.lx[i, j] = self.lx[i, j] + self.lc[i, j, :, at]
            return carry

        lax.fori_loop(0, self.me.Z, one, 0)

    def y_copy(self):
        me = self.me
        src = self.base().at[me.z, 1 - me.y] if self.early else self.base().at[:, 1 - me.y]
        return rcopy(src, self.ly, self.s(2), self.r(2), me.over_y)

    def y_add(self):
        self.y_copy().wait_recv()
        base, y = self.base(), self.me.y

        def one(i, carry):
            self.ly[i] = self.ly[i] + base[i, y]
            return carry

        lax.fori_loop(0, self.me.Z, one, 0)

    def along(self):
        return self.base() if self.early else self.ly

    def near(self):
        me = self.me
        return rcopy(self.along().at[me.z_near], self.lz.at[0], self.s(3), self.r(3), me.dev(z=me.z_near))

    def through(self, n):
        me = self.me
        place = self.along().at[me.z_far_inner if n == 0 else me.z_far_outer]
        return rcopy(place, self.lr.at[n], self.s(4 + n), self.r(4 + n), me.dev(z=me.z_near))

    def onward(self, n):
        me = self.me
        z = me.z_far_inner if n == 0 else me.z_far_outer
        return rcopy(self.along().at[z], self.lz.at[1], self.s(6 + n), self.r(6), me.dev(z=z))

    def z_start(self):
        @pl.when(self.me.outer == 1)
        def _():
            for n in range(2):
                self.through(n).start()

        self.near().start()

    def relay(self):
        me = self.me

        @pl.when(me.outer == 0)
        def _():
            for n in range(2):
                self.through(n).wait_recv()
                z = me.z_far_inner if n == 0 else me.z_far_outer
                self.along()[z] = self.along()[z] + self.lr[n]
                self.onward(n).start()

    def z_sum(self):
        self.near().wait_recv()
        self.onward(0).wait_recv()
        total = self.along()[self.me.z].astype(F32) + self.lz[0].astype(F32)
        return total + self.lz[1].astype(F32)

    def z_end(self):
        self.final(self.z_sum())

    def early_z_end(self):
        self.base()[self.me.z] = self.z_sum().astype(BF)
        self.y_copy().start()

    def early_y_end(self):
        self.y_copy().wait_recv()
        self.final(self.base()[self.me.z, self.me.y].astype(F32) + self.ly[...].astype(F32))

    def finish(self, skip_c=False):
        if not skip_c:
            self.c_copy().wait_send()
        if self.lx is not None:
            self.x_copy().wait_send()
        self.y_copy().wait_send()
        self.near().wait_send()

        @pl.when(self.me.outer == 1)
        def _():
            for n in range(2):
                self.through(n).wait_send()

        @pl.when(self.me.outer == 0)
        def _():
            for n in range(2):
                self.onward(n).wait_send()


def bwd_kernel(deep, dat, q_h, k_h, v_h, mask_h, lse_h, x_h, qkv_h, hid_h, in_h, out_h, dz1_h, sg_h, small_h, bias,
               dx_o, gqkv_o, ghid_o, gin_o, gout_o, gmask_o, small_o,
               q_v, k_v, v_v, do_v, lse_v, m_v, p_v, dq_v, dk_v, dv_v, acck, accv,
               lc_m, ly_m, lz_m, lr_m, lz_e, lr_e, gm_v,
               own_w, lc_hid, lx_hid, ly_hid, lz_hid, lr_hid, lc_in, lx_in, ly_in, lz_in, lr_in, lc_out, lx_out, ly_out, lz_out, lr_out,
               fin_hid, fin_in, fin_out,
               p_q, lc_q, ly_q, lz_q, lr_q, fin_q,
               x_v, w_v, sx_v, lx_x, dx_v, dz_v,
               s_v, sc_v, sy_v, sz_v, sx2_v,
               loc, msem, ds_, dr, wl, w_s, w_r, m_s, m_r, q_s, q_r, xs, xr, s1s, s1r, szs, szr):
    me = Place(deep)
    Z, y, c, z, t = me.Z, me.y, me.c, me.z, me.t
    pairs, seq, _ = q_v.shape
    heads = 2 * pairs
    half = seq // 2
    width = x_v.shape[1]
    zs = range(1, Z)
    rows_own = pl.ds(pl.multiple_of(t * half, 128), half)

    def dat_cols(p, who):
        return pl.ds(pl.multiple_of(who * (pairs * 128) + p * 128, 128), 128)

    def dat_local(p):
        return pltpu.make_async_copy(dat.at[:, dat_cols(p, t)], do_v.at[p, rows_own], loc.at[p])

    def dat_copy(p):
        return rcopy(dat.at[:, dat_cols(p, 1 - t)], do_v.at[p, rows_own], ds_.at[p], dr.at[p], me.over_t)

    loads = [pltpu.make_async_copy(a, b, loc.at[3 + n]) for n, (a, b) in enumerate((
        (q_h, q_v), (k_h, k_v), (v_h, v_v), (lse_h, lse_v), (x_h, x_v), (qkv_h, w_v), (dz1_h, dz_v), (small_h, s_v.at[pl.ds(0, small_h.shape[0])])))]

    def m_load(h, slot):
        return pltpu.make_async_copy(mask_h.at[h], m_v.at[slot], msem.at[slot])

    def sg_load(h):
        return pltpu.make_async_copy(sg_h.at[h], gm_v.at[h], loc.at[11 + h])

    def gm_save(h):
        return pltpu.make_async_copy(gm_v.at[h], gmask_o.at[h], loc.at[17 + h])

    def M(h, slot=None):
        early = isinstance(h, int) and h == 1

        def own(i, j):
            return p_v[slot, i, j, c]

        def final(total):
            sg_load(h).wait()
            gm_v[h] = total * gm_v[h]
            gm_save(h).start()

        away = None if slot is None else p_v.at[slot, :, :, 1 - c]
        return Fold(me, own, p_v.at[0, :, :, 1 - c] if away is None else away, lc_m.at[h],
                    (ly_m.at[h, 0], lz_e, lr_e) if early else (ly_m.at[h], lz_m.at[h], lr_m.at[h]),
                    (lambda n: m_s.at[h, n], lambda n: m_r.at[h, n]), final, early=early)

    def W(k, part, lc, lx, ly, lz, lr, fin, out, early):
        n = lx.shape[-1]

        def own(i, j):
            return own_w[i, j, :, 0:2 * n]

        def final(total):
            fin[...] = total
            pltpu.make_async_copy(fin, out, wl.at[3 + k]).start()

        fold = Fold(me, own, part.at[:, :, 1 - c], lc, (ly, lz, lr), (lambda i: w_s.at[k, i], lambda i: w_r.at[k, i]), final,
                    lx, early, lambda who: pl.ds(pl.multiple_of(who * n, 128), n))
        fold.own_load = lambda: pltpu.make_async_copy(part.at[:, :, c], own_w.at[:, :, :, pl.ds(0, 2 * n)], wl.at[k])
        fold.saved = lambda: pltpu.make_async_copy(fin, out, wl.at[3 + k])
        return fold

    WH = W(0, hid_h, lc_hid, lx_hid, ly_hid, lz_hid, lr_hid, fin_hid, ghid_o, False)
    WI = W(1, in_h, lc_in, lx_in, ly_in, lz_in, lr_in, fin_in, gin_o, True)
    WO = W(2, out_h, lc_out, lx_out, ly_out, lz_out, lr_out, fin_out, gout_o, False)

    def q_final(total):
        fin_q[...] = total
        pltpu.make_async_copy(fin_q, gqkv_o, loc.at[24]).start()

    Q = Fold(me, lambda i, j: p_q[i, j, c], p_q.at[:, :, 1 - c], lc_q, (ly_q, lz_q, lr_q),
             (lambda n: q_s.at[n], lambda n: q_r.at[n]), q_final)

    def x_copy():
        return rcopy(sx_v, lx_x, xs, xr, me.over_t)

    def s_c():
        return rcopy(s_v, sc_v, s1s.at[0], s1r.at[0], me.over_c)

    def s_y():
        return rcopy(sc_v, sy_v, s1s.at[1], s1r.at[1], me.over_y)

    def s_z(d):
        return rcopy(sy_v, sz_v.at[z], szs.at[d - 1], szr.at[d - 1], me.along_z(d))

    def s_z_in(d):
        return rcopy(sy_v, sz_v.at[me.source_z(d)], szs.at[d - 1], szr.at[d - 1], me.along_z(d))

    def s_x():
        return rcopy(s_v, sx2_v, s1s.at[2], s1r.at[2], me.over_t)

    m_load(0, 0).start()
    for cp in loads[:4]:
        cp.start()
    for p in range(pairs):
        dat_local(p).start()
    WH.own_load().start()
    for cp in loads[4:]:
        cp.start()
    me.greet()
    for p in range(pairs):
        dat_copy(p).start()
    for w in (WH, WI, WO):
        w.c_copy().start()
    for h in range(heads):
        sg_load(h).start()
    for cp in loads[:4]:
        cp.wait()

    blk = seq // Z
    shape4 = p_v.shape[2:]

    def attend(p, u, slot):
        sl = slice(64 * u, 64 * u + 64)
        acck[...] = jnp.zeros_like(acck)
        accv[...] = jnp.zeros_like(accv)

        def rows_of(n, carry):
            b = lax.rem(t * (Z // 2) + n, Z)
            if u == 0:
                @pl.when(n == Z // 2)
                def _():
                    dat_copy(p).wait_recv()

                @pl.when(jnp.logical_and(n == Z // 2, p == 0))
                def _():
                    WH.own_load().wait()
                    WH.c_add()
                    WI.own_load().start()
                    WH.x_copy().start()

                @pl.when(jnp.logical_and(n == Z // 2 + 1, p == 0))
                def _():
                    WI.own_load().wait()
                    WI.c_add()
                    WO.own_load().start()
                    WI.x_copy().start()

            rows = pl.ds(pl.multiple_of(b * blk, blk), blk)
            qb, dob = q_v[p, rows, sl], do_v[p, rows, sl]
            kk, vv = k_v[p, :, sl], v_v[p, :, sl]
            s = dot_t(qb, kk) + m_v[u, b].reshape(blk, seq).astype(F32) + bias[...]
            pr = jnp.exp(s - lse_v[p, rows, u:u + 1])
            dp = dot_t(dob, vv)
            tt = pr * dp
            delta = jnp.sum(tt, axis=-1, keepdims=True)
            dsb = (tt - pr * delta).astype(BF)
            p_v[slot, b] = dsb.reshape(shape4)
            dq_v[p, rows, sl] = (dot(dsb, kk) * 0.125).astype(BF)
            acck[...] += dot_0(dsb, qb)
            accv[...] += dot_0(pr.astype(BF), dob)
            return carry

        lax.fori_loop(0, Z, rows_of, 0, unroll=2)
        dk_v[p, :, sl] = acck[...].astype(BF)
        dv_v[p, :, sl] = accv[...].astype(BF)

    def after_0():
        M(0, 0).c_add()
        WO.own_load().wait()
        WO.c_add()
        WO.x_copy().start()
        M(0).y_copy().start()

    def after_1():
        M(1, 1).c_add()
        M(1).z_start()

    def after_2():
        M(2, 0).c_add()
        M(2).y_copy().start()
        M(1).relay()
        M(0).y_add()
        M(0).z_start()

    def after_3():
        M(3, 1).c_add()
        M(3).y_copy().start()
        WH.x_add()
        WH.y_copy().start()
        M(0).relay()

    def after_4():
        M(4, 0).c_add()
        M(4).y_copy().start()
        M(2).y_add()
        M(2).z_start()
        M(1).early_z_end()

    def after_5():
        M(5, 1).c_add()
        M(5).y_copy().start()
        M(2).relay()
        M(3).y_add()
        M(3).z_start()

    after = (after_0, after_1, after_2, after_3, after_4, after_5)

    def pair_step(p, carry):
        dat_local(p).wait()
        for u in range(2):
            h = 2 * p + u
            m_load(h, u).wait()
            if u == 0:
                m_load(h + 1, 1).start()
            else:
                @pl.when(p < pairs - 1)
                def _():
                    m_load(h + 1, 0).start()

            @pl.when(p > 0)
            def _():
                M(h - 2, u).c_copy().wait_send()

            attend(p, u, u)
            M(h, u).c_copy().start()
            for n in range(pairs):
                pl.when(p == n)(after[2 * n + u])
        return carry

    lax.fori_loop(0, pairs, pair_step, 0)
    for cp in loads[4:]:
        cp.wait()

    step = half // 2

    def d_cat(ref, rows):
        return jnp.concatenate([ref[p, rows, :] for p in range(pairs)], axis=1)

    def weight(j):
        return w_v[:, :, :, j].reshape(width, pairs * 128)

    def terms(rows):
        acc = dot_t(d_cat(dq_v, rows), weight(0))
        acc = acc + dot_t(d_cat(dk_v, rows), weight(1))
        return acc + dot_t(d_cat(dv_v, rows), weight(2))

    def theirs(r, carry):
        at = pl.ds(pl.multiple_of(r * step, step), step)
        rows = pl.ds(pl.multiple_of((1 - t) * half + r * step, step), step)
        sx_v[at, :] = terms(rows).astype(BF)
        return carry

    lax.fori_loop(0, 2, theirs, 0)
    x_copy().start()
    M(3).relay()
    WI.x_add()
    WI.z_start()
    M(0).z_end()
    WO.x_add()
    WO.y_copy().start()

    for j, ref in enumerate((dq_v, dk_v, dv_v)):
        g = dot_0(x_v[...], d_cat(ref, slice(None)))
        p_q[:, :, :, j] = g.astype(BF).reshape(p_q.shape[:3] + p_q.shape[4:])
    Q.c_copy().start()
    WI.relay()
    base = small_h.shape[0]
    for n, ref in enumerate((dq_v, dv_v)):
        for p in range(pairs):
            at = base + n * pairs + p
            s_v[at:at + 1, :] = jnp.sum(ref[p].astype(F32), axis=0, keepdims=True)
    for at in range(base + 2 * pairs, s_v.shape[0]):
        s_v[at:at + 1, :] = jnp.zeros((1, 128), F32)
    s_c().start()
    Q.c_add()
    Q.y_copy().start()

    def mine(r, carry):
        at = pl.ds(pl.multiple_of(r * step, step), step)
        rows = pl.ds(pl.multiple_of(t * half + r * step, step), step)
        dx_v[at, :] = terms(rows) + dz_v[at, :]
        return carry

    lax.fori_loop(0, 2, mine, 0)
    s_c().wait_recv()
    sc_v[...] = sc_v[...] + s_v[...]
    s_y().start()
    WH.y_add()
    WH.z_start()
    M(2).z_end()
    M(4).y_add()
    M(4).z_start()
    WH.relay()
    WI.early_z_end()
    M(3).z_end()
    M(4).relay()
    M(5).y_add()
    M(5).z_start()
    s_y().wait_recv()
    sy_v[...] = sy_v[...] + sc_v[...]
    sz_v[z] = sy_v[...]
    for d in zs:
        s_z(d).start()
    Q.y_add()
    Q.z_start()
    WH.z_end()
    M(5).relay()
    WO.y_add()
    WO.z_start()
    Q.relay()
    M(4).z_end()
    x_copy().wait_recv()
    dx_v[...] = dx_v[...] + lx_x[...].astype(F32)
    dx_save = pltpu.make_async_copy(dx_v, dx_o, loc.at[23])
    dx_save.start()
    WO.relay()
    for d in zs:
        s_z_in(d).wait_recv()
    s_c().wait_send()
    total = sz_v[0]
    for i in range(1, Z):
        total = total + sz_v[i]
    s_v[...] = total
    s_x().start()
    M(5).z_end()
    M(1).early_y_end()
    WI.early_y_end()
    Q.z_end()
    WO.z_end()
    s_x().wait_recv()
    low = sx2_v[...] + s_v[...]
    row = lax.broadcasted_iota(jnp.int32, low.shape, 0)
    s_y().wait_send()
    sc_v[...] = jnp.where(row < base, low, s_v[...])
    s_save = pltpu.make_async_copy(sc_v, small_o, loc.at[25])
    s_save.start()

    for p in range(pairs):
        dat_copy(p).wait_send()
    for w in (WH, WI, WO):
        w.finish()
        w.saved().wait()
    for h in range(heads):
        M(h).finish(h < heads - 2)
        gm_save(h).wait()
    Q.finish()
    for d in zs:
        s_z(d).wait_send()
    x_copy().wait_send()
    s_x().wait_send()
    dx_save.wait()
    pltpu.make_async_copy(fin_q, gqkv_o, loc.at[24]).wait()
    s_save.wait()


def backward(deep, dat, q, k, v, mask, lse, x, qkv, g_hid, g_in, g_out, dz1, sg, small, bias):
    pairs, seq, _ = q.shape
    half, width = dz1.shape
    heads, Z, Y, C, blk, _ = mask.shape
    r, n2 = g_in.shape[3], g_in.shape[4]
    n2o = g_out.shape[4]
    n, no = n2 // 2, n2o // 2
    base = small.shape[0]
    rows_s = base + 8
    sd = jax.ShapeDtypeStruct
    dma = pltpu.SemaphoreType.DMA
    vm = pltpu.VMEM
    out_shape = (
        sd((half, width), F32), sd(qkv.shape[3:], F32), sd((r, n), F32), sd((r, n), F32), sd((r, no), F32),
        sd((heads, blk, seq), F32), sd((rows_s, 128), F32),
    )
    pair = vm((pairs, seq, 128), BF)

    def chain(m, early):
        last = (Y, r, m) if early else (r, m)
        return [vm((Z, Y, r, 2 * m), BF), vm((Z, Y, r, m), BF), vm((r, m) if early else (Z, r, m), BF), vm((2,) + last, BF), vm((2,) + last, BF)]

    three, rq, nq = qkv.shape[3:]
    return pl.pallas_call(
        functools.partial(bwd_kernel, deep),
        out_shape=out_shape,
        in_specs=[ANY] * 14 + [VM],
        out_specs=[ANY] * len(out_shape),
        scratch_shapes=[
            pair, pair, pair, pair, vm((pairs, seq, 128), F32), vm((2, Z, Y, C, blk, seq), BF), vm((2, Z, Y, C, blk, seq), BF),
            pair, pair, pair, vm((seq, 64), F32), vm((seq, 64), F32),
            vm((heads, Z, Y, blk, seq), BF), vm((heads, Z, blk, seq), BF), vm((heads, 2, blk, seq), BF), vm((heads, 2, blk, seq), BF),
            vm((2, Y, blk, seq), BF), vm((2, Y, blk, seq), BF), vm((heads, blk, seq), F32),
            vm((Z, Y, r, n2), BF), *chain(n, False), *chain(n, True), *chain(no, False), vm((r, n), F32), vm((r, n), F32), vm((r, no), F32),
            vm((Z, Y, C, three, rq, nq), BF), vm((Z, Y, three, rq, nq), BF), vm((Z, three, rq, nq), BF),
            vm((2, three, rq, nq), BF), vm((2, three, rq, nq), BF), vm((three, rq, nq), F32),
            vm((seq, width), BF), vm((Z, Y, C, three, rq, nq), BF), vm((half, width), BF), vm((half, width), BF), vm((half, width), F32), vm((half, width), F32),
            vm((rows_s, 128), F32), vm((rows_s, 128), F32), vm((rows_s, 128), F32), vm((Z, rows_s, 128), F32), vm((rows_s, 128), F32),
            dma((26,)), dma((2,)), dma((pairs,)), dma((pairs,)),
            dma((6,)), dma((3, 8)), dma((3, 7)), dma((heads, 8)), dma((heads, 7)), dma((8,)), dma((7,)), dma, dma,
            dma((3,)), dma((3,)), dma((Z - 1,)), dma((Z - 1,)),
        ],
        compiler_params=pltpu.CompilerParams(collective_id=2, has_side_effects=True, vmem_limit_bytes=62 << 20),
        name="backward_attention",
    )(dat, q, k, v, mask, lse, x, qkv, g_hid, g_in, g_out, dz1, sg, small, bias)


NEG = -1e30
EPS = 1e-12


def layer_norm(value_rows, scale_vec, shift_vec):
    centre = value_rows - jnp.mean(value_rows, axis=-1, keepdims=True)
    spread = jnp.mean(centre * centre, axis=-1, keepdims=True)
    return centre * lax.rsqrt(spread + EPS) * scale_vec + shift_vec


def gelu_exact(value_rows):
    return jax.nn.gelu(value_rows, approximate=False)


def matmul(left, right):
    return jnp.dot(left, right, preferred_element_type=jnp.float32)


def times_transposed(left, right):
    return lax.dot_general(
        left, right, (((1,), (1,)), ((), ())), preferred_element_type=jnp.float32
    )


def over_rows(left, right):
    return lax.dot_general(
        left, right, (((0,), (0,)), ((), ())), preferred_element_type=jnp.float32
    )


def plain_body(
    inputs,
    lengths,
    w_qkv,
    b_qv,
    w_out,
    b_out,
    ln1_gain,
    ln1_bias,
    w_in,
    b_in,
    w_hid,
    b_hid,
    ln2_gain,
    ln2_bias,
    mask_logits,
    noise,
    cotangent,
):
    seq_count, half_rows, width = inputs.shape
    slot_len = half_rows * lax.axis_size("tensor")
    tensor_rank = lax.axis_index("tensor")
    head_count = mask_logits.shape[0]
    head_dim = w_qkv.shape[2] // head_count
    scale = head_dim ** (-0.5)
    token_count = seq_count * slot_len
    mixed_logits = mask_logits + noise
    local_mask = jax.nn.log_sigmoid(mixed_logits).astype(jnp.bfloat16)
    full_qkv, full_out, full_in, full_hid, full_mask = (
        lax.all_gather(w_qkv, "dp", axis=1, tiled=True),
        lax.all_gather(w_out, "dp", axis=1, tiled=True),
        lax.all_gather(w_in, "dp", axis=0, tiled=True),
        lax.all_gather(w_hid, "dp", axis=1, tiled=True),
        lax.all_gather(local_mask, "dp", axis=1, tiled=True),
    )
    key_valid = jnp.arange(slot_len, dtype=jnp.int32)[None, :] < lengths[:, None]
    own_rows = tensor_rank * half_rows + jnp.arange(half_rows, dtype=jnp.int32)
    row_valid = (own_rows[None, :] < lengths[:, None]).astype(jnp.float32)
    gathered = lax.all_gather(inputs, "tensor", axis=1, tiled=True)
    flat_rows = gathered.reshape(token_count, width)
    query_rows = (matmul(flat_rows, full_qkv[0]) + b_qv[0]).astype(jnp.bfloat16)
    key_rows = matmul(flat_rows, full_qkv[1]).astype(jnp.bfloat16)
    value_rows = (matmul(flat_rows, full_qkv[2]) + b_qv[1]).astype(jnp.bfloat16)

    def split_heads(matrix):
        return matrix.reshape(seq_count, slot_len, head_count, head_dim).transpose(0, 2, 1, 3)

    def join_heads(stacked):
        return stacked.transpose(0, 2, 1, 3).reshape(token_count, head_count * head_dim)

    def masked_scores(query_h, keys_h, mask_h, valid_keys):
        score_matrix = (
            jnp.einsum("qd,kd->qk", query_h, keys_h, preferred_element_type=jnp.float32) * scale
        )
        score_matrix = score_matrix + mask_h.astype(jnp.float32)
        return jnp.where(valid_keys[None, :], score_matrix, NEG)

    def attend_sequence(operands):
        query_s, keys_s, values_s, valid_keys = operands

        def attend_head(head_ops):
            query_h, keys_h, values_h, mask_h = head_ops
            score_matrix = masked_scores(query_h, keys_h, mask_h, valid_keys)
            top_score = jnp.max(score_matrix, axis=-1, keepdims=True)
            expo = jnp.exp(score_matrix - top_score)
            row_total = jnp.sum(expo, axis=-1, keepdims=True)
            attention_probabilities = (expo / row_total).astype(jnp.bfloat16)
            result = jnp.einsum(
                "qk,kd->qd", attention_probabilities, values_h, preferred_element_type=jnp.float32
            )
            return (result.astype(jnp.bfloat16), (top_score + jnp.log(row_total))[:, 0])

        return lax.map(attend_head, (query_s, keys_s, values_s, full_mask))

    head_out, log_total = lax.map(
        attend_sequence,
        (split_heads(query_rows), split_heads(key_rows), split_heads(value_rows), key_valid),
    )
    attn = join_heads(head_out)
    attn_terms = matmul(attn, full_out).reshape(seq_count, slot_len, width)
    attn_part = lax.psum_scatter(attn_terms, "tensor", scatter_dimension=1, tiled=True)
    first_sum = inputs.astype(jnp.float32) + attn_part + b_out
    hidden_one = layer_norm(first_sum, ln1_gain, ln1_bias)
    hidden_rows = lax.all_gather(
        hidden_one.astype(jnp.bfloat16), "tensor", axis=1, tiled=True
    ).reshape(token_count, width)
    pre_act = matmul(hidden_rows, full_in) + b_in
    activated = gelu_exact(pre_act).astype(jnp.bfloat16)
    ffn_terms = matmul(activated, full_hid).reshape(seq_count, slot_len, width)
    ffn_part = lax.psum_scatter(ffn_terms, "tensor", scatter_dimension=1, tiled=True)
    second_sum = hidden_one + ffn_part + b_hid
    outputs = layer_norm(second_sum, ln2_gain, ln2_bias).astype(jnp.bfloat16)
    back_qkv, back_out, back_in, back_hid, back_mask = (
        lax.all_gather(w_qkv, "dp", axis=1, tiled=True),
        lax.all_gather(w_out, "dp", axis=1, tiled=True),
        lax.all_gather(w_in, "dp", axis=0, tiled=True),
        lax.all_gather(w_hid, "dp", axis=1, tiled=True),
        lax.all_gather(local_mask, "dp", axis=1, tiled=True),
    )
    grad_output = cotangent * row_valid[:, :, None]
    _, pull_second = jax.vjp(layer_norm, second_sum, ln2_gain, ln2_bias)
    grad_second, ln2_gain_part, ln2_bias_part = pull_second(grad_output)
    b_hid_part = jnp.sum(grad_second, axis=(0, 1))
    second_rows = lax.all_gather(
        grad_second.astype(jnp.bfloat16), "tensor", axis=1, tiled=True
    ).reshape(token_count, width)
    w_hid_grad = over_rows(activated, second_rows)
    grad_act = times_transposed(second_rows, back_hid)
    _, pull_gelu = jax.vjp(gelu_exact, pre_act)
    grad_pre = pull_gelu(grad_act)[0].astype(jnp.bfloat16)
    b_in_part = jnp.sum(grad_pre.astype(jnp.float32), axis=0)
    w_in_grad = over_rows(hidden_rows, grad_pre)
    hidden_terms = times_transposed(grad_pre, back_in).reshape(seq_count, slot_len, width)
    grad_hidden = grad_second + lax.psum_scatter(
        hidden_terms, "tensor", scatter_dimension=1, tiled=True
    )
    _, pull_first = jax.vjp(layer_norm, first_sum, ln1_gain, ln1_bias)
    grad_first, ln1_gain_part, ln1_bias_part = pull_first(grad_hidden)
    b_out_part = jnp.sum(grad_first, axis=(0, 1))
    first_rows = lax.all_gather(
        grad_first.astype(jnp.bfloat16), "tensor", axis=1, tiled=True
    ).reshape(token_count, width)
    w_out_grad = over_rows(attn, first_rows)
    grad_attn = times_transposed(first_rows, back_out).astype(jnp.bfloat16)

    def sequence_back(mask_acc, operands):
        query_s, keys_s, values_s, grad_s, total_s, valid_keys = operands

        def head_back(head_ops):
            query_h, keys_h, values_h, mask_h, grad_h, total_h = head_ops
            score_matrix = masked_scores(query_h, keys_h, mask_h, valid_keys)
            attention_probabilities = jnp.exp(score_matrix - total_h[:, None])
            grad_probs = jnp.einsum(
                "qd,kd->qk", grad_h, values_h, preferred_element_type=jnp.float32
            )
            centre = jnp.sum(attention_probabilities * grad_probs, axis=-1, keepdims=True)
            grad_scores = (attention_probabilities * (grad_probs - centre)).astype(jnp.bfloat16)
            grad_q = (
                jnp.einsum("qk,kd->qd", grad_scores, keys_h, preferred_element_type=jnp.float32)
                * scale
            ).astype(jnp.bfloat16)
            grad_k = (
                jnp.einsum("qk,qd->kd", grad_scores, query_h, preferred_element_type=jnp.float32)
                * scale
            ).astype(jnp.bfloat16)
            grad_v = jnp.einsum(
                "qk,qd->kd",
                attention_probabilities.astype(jnp.bfloat16),
                grad_h,
                preferred_element_type=jnp.float32,
            ).astype(jnp.bfloat16)
            return (grad_q, grad_k, grad_v, grad_scores)

        grad_q, grad_k, grad_v, grad_sc = lax.map(
            head_back, (query_s, keys_s, values_s, back_mask, grad_s, total_s)
        )
        return (mask_acc + grad_sc.astype(jnp.float32), (grad_q, grad_k, grad_v))

    mask_zero = jnp.zeros(back_mask.shape, jnp.float32)
    mask_grad, (heads_q, heads_k, heads_v) = lax.scan(
        sequence_back,
        mask_zero,
        (
            split_heads(query_rows),
            split_heads(key_rows),
            split_heads(value_rows),
            split_heads(grad_attn),
            log_total,
            key_valid,
        ),
    )
    query_grad = join_heads(heads_q)
    keys_grad = join_heads(heads_k)
    values_grad = join_heads(heads_v)
    b_qv_part = jnp.stack(
        [
            jnp.sum(query_grad.astype(jnp.float32), axis=0),
            jnp.sum(values_grad.astype(jnp.float32), axis=0),
        ]
    )
    w_qkv_grad = jnp.stack(
        [
            over_rows(flat_rows, query_grad),
            over_rows(flat_rows, keys_grad),
            over_rows(flat_rows, values_grad),
        ]
    )
    input_terms = (
        times_transposed(query_grad, back_qkv[0])
        + times_transposed(keys_grad, back_qkv[1])
        + times_transposed(values_grad, back_qkv[2])
    ).reshape(seq_count, slot_len, width)
    input_grad = grad_first + lax.psum_scatter(
        input_terms.astype(jnp.bfloat16), "tensor", scatter_dimension=1, tiled=True
    ).astype(jnp.float32)
    qkv_total, out_total, in_total, hid_total, mask_total = (
        lax.psum_scatter(w_qkv_grad, "dp", scatter_dimension=1, tiled=True),
        lax.psum_scatter(w_out_grad, "dp", scatter_dimension=1, tiled=True),
        lax.psum_scatter(w_in_grad, "dp", scatter_dimension=0, tiled=True),
        lax.psum_scatter(w_hid_grad, "dp", scatter_dimension=1, tiled=True),
        lax.psum_scatter(mask_grad, "dp", scatter_dimension=1, tiled=True),
    )
    mask_logit_grad = mask_total * jax.nn.sigmoid(-mixed_logits)
    ln1_gain_total, ln1_bias_total, ln2_gain_total, ln2_bias_total, b_out_total, b_hid_total = (
        lax.psum(
            (ln1_gain_part, ln1_bias_part, ln2_gain_part, ln2_bias_part, b_out_part, b_hid_part),
            ("dp", "tensor"),
        )
    )
    b_qv_total, b_in_total = lax.psum((b_qv_part, b_in_part), "dp")
    return (
        outputs,
        input_grad,
        qkv_total,
        b_qv_total,
        out_total,
        b_out_total,
        ln1_gain_total,
        ln1_bias_total,
        in_total,
        b_in_total,
        hid_total,
        b_hid_total,
        ln2_gain_total,
        ln2_bias_total,
        mask_logit_grad,
    )


def last_kernel(place, total, *refs):
    n = (len(refs) - 10) // 3
    ins, rest = refs[:n], refs[n:]
    (bqv_o, bin_o), vecs, outs = rest[:2], rest[2:8], rest[8:8 + n]
    held, tot_v, sems = rest[8 + n:8 + 2 * n], rest[8 + 2 * n], rest[9 + 2 * n]
    first = pltpu.make_async_copy(total, tot_v, sems.at[n])
    first.start()
    loads = [pltpu.make_async_copy(a, b, sems.at[i]) for i, (a, b) in enumerate(zip(ins, held))]
    saves = [pltpu.make_async_copy(a, b, sems.at[i]) for i, (a, b) in enumerate(zip(held, outs))]
    for cp in loads:
        cp.start()
    for a, b in zip(loads, saves):
        a.wait()
        b.start()
    first.wait()
    t = place[0]
    per = vecs[0].shape[0] // 128
    for k, ref in enumerate(vecs):
        for i in range(per):
            ref[pl.ds(i * 128, 128)] = tot_v[k * per + i, :]
    m = bin_o.shape[0] // 128
    for i in range(m):
        bin_o[pl.ds(i * 128, 128)] = tot_v[6 * per + t * m + i, :]
    base = total.shape[0] - 8
    nq = bqv_o.shape[1] // 128
    for j in range(2):
        for i in range(nq):
            bqv_o[j:j + 1, i * 128:(i + 1) * 128] = tot_v[base + j * nq + i:base + j * nq + i + 1, :]
    for cp in saves:
        cp.wait()


def last(t, total, arrays, width, n_bin, bqv_shape):
    sd, vm = jax.ShapeDtypeStruct, pltpu.VMEM
    n = len(arrays)
    return pl.pallas_call(
        last_kernel,
        out_shape=(sd(bqv_shape, F32), sd((n_bin,), F32)) + (sd((width,), F32),) * 6 + tuple(sd(a.shape, a.dtype) for a in arrays),
        in_specs=[pl.BlockSpec(memory_space=pltpu.SMEM)] + [ANY] * (n + 1),
        out_specs=[VM] * 8 + [ANY] * n,
        scratch_shapes=[vm(a.shape, a.dtype) for a in arrays] + [vm(total.shape, F32), pltpu.SemaphoreType.DMA((n + 1,))],
        compiler_params=pltpu.CompilerParams(vmem_limit_bytes=60 << 20),
        name="hand_over",
    )(t, total, *arrays)


def body(
    inputs, lengths, w_qkv, b_qv, w_out, b_out, ln1_gain, ln1_bias, w_in, b_in, w_hid, b_hid,
    ln2_gain, ln2_bias, mask_logits, noise, cotangent,
):
    deep = lax.axis_size("dp")
    x = inputs[0]
    half, width = x.shape
    seq = 2 * half
    bias = jnp.where(jnp.arange(seq, dtype=jnp.int32) < lengths[0], 0.0, NEG).astype(F32).reshape(1, seq)
    vectors = (b_out, b_hid, ln1_gain, ln1_bias, ln2_gain, ln2_bias)
    q, k, v, lse, x_all, mask_all, qkv_all, gate, outputs, dz1, g_hid, g_in, g_out, dattn, small = forward(
        deep, x, mask_logits, noise, w_qkv, w_out.T, w_in, w_hid.T, b_in, cotangent[0], b_qv, lengths, vectors)
    place = (deep // 4, 2, 2, w_in.shape[0])
    dx, gqkv, ghid, gin, gout, gmask, total = backward(
        deep, dattn, q, k, v, mask_all, lse, x_all, qkv_all,
        g_hid.reshape(place + (-1,)), g_in.reshape(place + (-1,)), g_out.reshape(place + (-1,)), dz1, gate.reshape(mask_logits.shape), small, bias)
    t = lax.axis_index("tensor").astype(jnp.int32).reshape(1)
    g_bqv, g_bin, v0, v1, v2, v3, v4, v5, outputs, dx, gqkv, gout, gin, ghid, gmask = last(
        t, total, (outputs, dx, gqkv, gout, gin, ghid, gmask), width, b_in.shape[0], b_qv.shape)
    return (outputs[None], dx[None], gqkv, g_bqv, gout.T, v4, v0, v1, gin, g_bin, ghid.T, v5, v2, v3, gmask)


def solution(mesh):
    placed = (
        P("dp", "tensor", None),
        P("dp"),
        P(None, "dp", "tensor"),
        P(None, "tensor"),
        P("tensor", "dp"),
        P(),
        P(),
        P(),
        P("dp", "tensor"),
        P("tensor"),
        P("tensor", "dp"),
        P(),
        P(),
        P(),
        P("tensor", "dp", None),
        P("tensor", "dp", None),
        P("dp", "tensor", None),
    )

    def run(*args):
        w_rows, m_rows = args[8].shape[0], args[14].shape[1]
        tiled = w_rows % 16 == 0 and m_rows % 16 == 0 and args[0].shape[0] == 1 and mesh.shape["dp"] == 16
        return (body if tiled else plain_body)(*args)

    return jax.shard_map(
        run,
        mesh=mesh,
        in_specs=placed,
        out_specs=(
            P("dp", "tensor", None),
            P("dp", "tensor", None),
            P(None, "dp", "tensor"),
            P(None, "tensor"),
            P("tensor", "dp"),
            P(),
            P(),
            P(),
            P("dp", "tensor"),
            P("tensor"),
            P("tensor", "dp"),
            P(),
            P(),
            P(),
            P("tensor", "dp", None),
        ),
        check_vma=False,
    )
```

```python
import functools

import jax
import jax.numpy as jnp
from jax import lax
from jax.experimental import pallas as pl
from jax.experimental.pallas import tpu as pltpu
from jax.sharding import PartitionSpec as P

MESH = pl.DeviceIdType.MESH
BF, F32 = jnp.bfloat16, jnp.float32
ANY = pl.BlockSpec(memory_space=pl.ANY)
VM = pl.BlockSpec(memory_space=pltpu.VMEM)


class Place:
    def __init__(self, deep):
        self.Z, self.Y, self.C = deep // 4, 2, 2
        i = lax.axis_index("dp")
        self.t = lax.axis_index("tensor")
        self.c = lax.rem(i, 2)
        self.y = lax.rem(i // 2, 2)
        self.z = i // 4
        far = self.z // 2
        self.outer = 1 - lax.rem(self.z + far, 2)
        self.z_near = self.z + 1 - 2 * lax.rem(self.z, 2)
        self.z_far_inner = 2 - far
        self.z_far_outer = 3 - 3 * far

    def dev(self, z=None, y=None, c=None, t=None):
        z = self.z if z is None else z
        y = self.y if y is None else y
        c = self.c if c is None else c
        t = self.t if t is None else t
        return ((z * self.Y + y) * self.C + c, t)

    def along_z(self, d):
        return self.dev(z=lax.rem(self.z + d, self.Z))

    def source_z(self, d):
        return lax.rem(self.z - d + self.Z, self.Z)

    @property
    def over_y(self):
        return self.dev(y=1 - self.y)

    @property
    def over_c(self):
        return self.dev(c=1 - self.c)

    @property
    def over_t(self):
        return self.dev(t=1 - self.t)

    def greet(self):
        bar = pltpu.get_barrier_semaphore()
        peers = [self.along_z(d) for d in range(1, self.Z)] + [self.over_y, self.over_c, self.over_t]
        for p in peers:
            pl.semaphore_signal(bar, inc=1, device_id=p, device_id_type=MESH)
        pl.semaphore_wait(bar, len(peers))


def rcopy(src, dst, ssem, rsem, dev):
    return pltpu.make_async_remote_copy(src_ref=src, dst_ref=dst, send_sem=ssem, recv_sem=rsem, device_id=dev, device_id_type=MESH)


def dot(a, b):
    return jnp.dot(a, b, preferred_element_type=F32)


def dot_t(a, b):
    return lax.dot_general(a, b, (((1,), (1,)), ((), ())), preferred_element_type=F32)


def dot_0(a, b):
    return lax.dot_general(a, b, (((0,), (0,)), ((), ())), preferred_element_type=F32)


def norm_stats(rows):
    centre = rows - jnp.mean(rows, axis=-1, keepdims=True)
    scale = lax.rsqrt(jnp.mean(centre * centre, axis=-1, keepdims=True) + EPS)
    return centre * scale, scale


def norm_back(e, hat, scale):
    return (e - jnp.mean(e, axis=-1, keepdims=True) - hat * jnp.mean(e * hat, axis=-1, keepdims=True)) * scale


def middle_math(attn, x, wo, wi, wh, b_out, b_in, b_hid, g1, c1, g2, c2, cot, length, first,
                out, dz1, gout, dat, small, hat1_v, s1_v, h1b_v, ht_v, act_v, dg_v, z_v, hat2_v, zt_v,
                put_hid, put_in, ready, turned):
    half, width = hat1_v.shape
    wide = act_v.shape[1]
    rb, step = half, 512

    def by_rows(body):
        def one(r, carry):
            body(pl.ds(pl.multiple_of(r * rb, rb), rb), r)
            return carry

        lax.fori_loop(0, half // rb, one, 0)

    def by_cols(body):
        def one(j, carry):
            body(pl.ds(pl.multiple_of(j * step, step), step), j)
            return carry

        lax.fori_loop(0, wide // step, one, 0, unroll=3)

    def put(n, vec, add):
        for i in range(width // 128):
            at = n * (width // 128) + i
            piece = vec[:, i * 128:(i + 1) * 128]
            small[at:at + 1, :] = small[at:at + 1, :] + piece if add else piece

    small[...] = jnp.zeros_like(small)

    def first_norm(rows, r):
        z1 = x(rows).astype(F32) + dot_t(attn[rows, :], wo()) + b_out[...]
        hat, scale = norm_stats(z1)
        hat1_v[rows, :] = hat
        s1_v[rows, 0:1] = scale
        h1 = hat * g1[...] + c1[...]
        h1b_v[rows, :] = h1.astype(BF)
        z_v[rows, :] = h1 + b_hid[...]

    by_rows(first_norm)

    def up(cols, j):
        pre = dot(h1b_v[...], wi(cols)) + b_in(j)
        phi = jnp.exp(pre * pre * -0.5) * 0.3989422804014327
        cdf = 0.5 + 0.5 * lax.erf(pre * 0.7071067811865476)
        act = (pre * cdf).astype(BF)
        act_v[:, cols] = act
        dg_v[:, cols] = cdf + pre * phi
        z_v[...] += dot_t(act, wh(cols))

    by_cols(up)

    def second_norm(rows, r):
        hat, scale = norm_stats(z_v[rows, :])
        out[rows, :] = (hat * g2[...] + c2[...]).astype(BF)
        at = first + r * rb + lax.broadcasted_iota(jnp.int32, (rb, width), 0)
        dy = jnp.where(at < length, cot[rows, :], 0.0)
        put(2, jnp.sum(dy * hat, axis=0, keepdims=True), True)
        put(3, jnp.sum(dy, axis=0, keepdims=True), True)
        dz2 = norm_back(dy * g2[...], hat, scale)
        put(5, jnp.sum(dz2, axis=0, keepdims=True), True)
        z_v[rows, :] = dz2
        hat2_v[rows, :] = dz2.astype(BF)

    by_rows(second_norm)
    turned()
    zt_v[...] = hat2_v[...].T
    ht_v[...] = h1b_v[...].T
    ready()

    def down(cols, j):
        put_hid(j, dot(zt_v[...], act_v[:, cols]).astype(BF))
        dpre = (dot(hat2_v[...], wh(cols)) * dg_v[:, cols]).astype(BF)
        sums = jnp.sum(dpre.astype(F32), axis=0, keepdims=True)
        for i in range(step // 128):
            small[pl.ds(6 * (width // 128) + j * (step // 128) + i, 1), :] = sums[:, i * 128:(i + 1) * 128]
        put_in(j, dot(ht_v[...], dpre).astype(BF))
        z_v[...] += dot_t(dpre, wi(cols))

    by_cols(down)

    def first_back(rows, r):
        dh1, hat = z_v[rows, :], hat1_v[rows, :]
        put(0, jnp.sum(dh1 * hat, axis=0, keepdims=True), True)
        put(1, jnp.sum(dh1, axis=0, keepdims=True), True)
        d = norm_back(dh1 * g1[...], hat, s1_v[rows, 0:1])
        put(4, jnp.sum(d, axis=0, keepdims=True), True)
        dz1[rows, :] = d
        db = d.astype(BF)
        hat2_v[rows, :] = db
        dat[rows, :] = dot(db, wo()).astype(BF)

    by_rows(first_back)
    zt_v[...] = hat2_v[...].T
    gout[...] = dot(zt_v[...], attn[...]).astype(BF)


class Pass:
    def __init__(self, me, own, view, pair, sems, early=False, wide=False):
        self.me, self.own, self.view, self.pair, self.early, self.wide = me, own, view, pair, early, wide
        self.zs, self.zr, self.fs, self.ys, self.yr, self.xs, self.xr, self.cs, self.cr = sems

    def held(self, z):
        me = self.me
        return self.view(z, slice(None) if self.early else me.y, me.t)

    def source(self):
        return self.held(self.me.z) if self.early else self.own

    def near(self):
        me = self.me
        return rcopy(self.source(), self.held(me.z), self.zs.at[0], self.zr.at[0], me.dev(z=me.z_near))

    def far(self):
        me = self.me
        return rcopy(self.source(), self.held(me.z), self.zs.at[1], self.zr.at[1 + me.outer], me.dev(z=me.z_far_inner))

    def onward(self, n):
        me = self.me
        place = self.held(me.z_far_inner if n == 0 else me.z_far_outer)
        return rcopy(place, place, self.fs.at[n], self.zr.at[1 + n], me.dev(z=me.z_near))

    def z_start(self):
        self.near().start()
        self.far().start()

    def relay(self):
        @pl.when(self.me.outer == 0)
        def _():
            for n in range(2):
                self.onward(n).wait_recv()
                self.onward(n).start()

    def z_wait(self):
        @pl.when(self.me.outer == 1)
        def _():
            for n in range(2):
                self.onward(n).wait_recv()

        self.near().wait_recv()

    def y_copy(self):
        me = self.me
        place = self.view(me.z if self.early else slice(None), me.y, me.t)
        return rcopy(self.own if self.early else place, place, self.ys, self.yr, me.over_y)

    def x_copy(self):
        me = self.me
        place = self.view(slice(None), slice(None), me.t)
        return rcopy(place, place, self.xs, self.xr, me.over_t)

    def c_copy(self):
        return rcopy(self.pair(), self.pair(), self.cs, self.cr, self.me.over_c)

    def finish(self):
        self.near().wait_send()
        self.far().wait_send()

        @pl.when(self.me.outer == 0)
        def _():
            for n in range(2):
                self.onward(n).wait_send()

        self.y_copy().wait_send()
        if self.wide:
            self.x_copy().wait_send()
        self.c_copy().wait_send()


def pass_sems(*lead):
    dma = pltpu.SemaphoreType.DMA
    return [dma(lead + (2,)), dma(lead + (3,)), dma(lead + (2,))] + [dma(lead or (1,))] * 6


def fwd_kernel(deep, x_sh, ml_sh, nz_sh, qkv_sh, out_sh, in_sh, hid_sh, bin_sh, cot_h, bqv, length, *rest):
    fwd_steps(deep, x_sh, ml_sh, nz_sh, qkv_sh, out_sh, in_sh, hid_sh, bin_sh, cot_h, bqv, length, rest[:6], *rest[6:])


def fwd_steps(deep, x_sh, ml_sh, nz_sh, qkv_sh, out_sh, in_sh, hid_sh, bin_sh, cot_h, bqv, length, vec_h,
               q_o, k_o, v_o, lse_o, x_o, mask_o, qkv_o, gate_o, outs_o, dz1_o, ghid_o, gin_o, gout_o, dat_o, small_o,
               x_v, w_v, m_v, q_v, k_v, v_v, a_v, lse_v, out_w, in_w, hid_w, bin_v, attn_v, bias,
               hat1_v, s1_v, h1b_v, ht_v, act_v, dg_v, z_v, hat2_v, zt_v, outs_v, dz1_v, gout_v, dat_v, cot_v, small_v, vec_v,
               loc, gs, xs, xr, as_, ar, *sems):
    me = Place(deep)
    Z = me.Z
    y, c, z, t = me.y, me.c, me.z, me.t
    half = x_sh.shape[0]
    seq, width = x_v.shape
    pairs = q_v.shape[0]
    heads = 2 * pairs
    q_sems, m_sems, w_sems = sems[0:9], sems[9:18], sems[18:27]

    def cols(n):
        return pl.ds(pl.multiple_of(t * n, 128), n)

    rows_own = pl.ds(pl.multiple_of(t * half, 128), half)
    rows_other = pl.ds(pl.multiple_of((1 - t) * half, 128), half)

    P_Q = Pass(me, qkv_sh, lambda zs, ys, ts: w_v.at[zs, ys, c], lambda: w_v.at[:, :, c],
               list(q_sems[:3]) + [s.at[0] for s in q_sems[3:]])

    def M(h):
        return Pass(me, m_v.at[h, z, y, c], lambda zs, ys, ts: m_v.at[h, zs, ys, c], lambda: m_v.at[h, :, :, c],
                    [s.at[h] for s in m_sems])

    def W(k, shard, whole, early):
        n = shard.shape[1]

        def view(zs, ys, ts):
            return whole.at[zs, ys, c, :, pl.ds(pl.multiple_of(ts * n, 128), n)]

        return Pass(me, shard, view, lambda: whole.at[:, :, c], [s.at[k] for s in w_sems], early, True)

    WO, WI, WH = W(0, out_sh, out_w, False), W(1, in_sh, in_w, True), W(2, hid_sh, hid_w, False)

    locals_ = [
        pltpu.make_async_copy(qkv_sh, w_v.at[z, y, c], loc.at[17]),
        pltpu.make_async_copy(x_sh, x_v.at[rows_own], loc.at[16]),
        pltpu.make_async_copy(bin_sh, bin_v.at[t, 0], loc.at[3]),
    ] + [pltpu.make_async_copy(w.own, w.view(z, y, t), loc.at[4 + k]) for k, w in enumerate((WO, WI, WH))]
    raw = ml_sh.shape
    mixed = [pltpu.make_async_copy(a, dg_v.at[pl.ds(0, raw[0]), pl.ds(n * raw[1], raw[1])], loc.at[n])
             for a, n in ((ml_sh, 0), (nz_sh, 1))]
    late = [pltpu.make_async_copy(cot_h, cot_v, loc.at[2])] + [
        pltpu.make_async_copy(a, vec_v.at[n], loc.at[18 + n]) for n, a in enumerate(vec_h)]
    b_out, b_hid, g1, c1, g2, c2 = (vec_v.at[pl.ds(n, 1)] for n in range(6))
    for cp in mixed + locals_ + late:
        cp.start()
    me.greet()

    def x_copy():
        return rcopy(x_sh, x_v.at[rows_own], xs.at[0], xr.at[0], me.over_t)

    def b_copy():
        return rcopy(bin_sh, bin_v.at[t, 0], xs.at[1], xr.at[1], me.over_t)

    def a_cols(p):
        return pl.ds(pl.multiple_of(t * (pairs * 128) + p * 128, 128), 128)

    def a_copy(p):
        return rcopy(a_v.at[p, rows_other], attn_v.at[:, a_cols(p)], as_.at[p], ar.at[p], me.over_t)

    def a_local(p):
        return pltpu.make_async_copy(a_v.at[p, rows_own], attn_v.at[:, a_cols(p)], loc.at[7 + p])

    def mask_save(h):
        return pltpu.make_async_copy(m_v.at[h], mask_o.at[h], loc.at[10 + h])

    P_Q.z_start()
    WI.y_copy().start()
    x_copy().start()
    b_copy().start()
    for cp in mixed:
        cp.wait()
    per = raw[0] // heads

    def mask_of(h):
        rows = pl.ds(pl.multiple_of(h * per, per), per)
        v = dg_v[rows, 0:raw[1]] + dg_v[rows, raw[1]:2 * raw[1]]
        m_v[h, z, y, c] = (jnp.minimum(v, 0.0) - jnp.log1p(jnp.exp(-jnp.abs(v)))).astype(BF)
        dg_v[rows, 2 * raw[1]:3 * raw[1]] = jax.nn.sigmoid(-v)

    mask_of(0)
    M(0).z_start()
    gate_save = pltpu.make_async_copy(dg_v.at[pl.ds(0, raw[0]), pl.ds(2 * raw[1], raw[1])], gate_o, loc.at[0])
    key = lax.broadcasted_iota(jnp.int32, bias.shape, 1)
    bias[...] = jnp.where(key < length[0], 0.0, NEG)
    for cp in locals_:
        cp.wait()
    P_Q.relay()
    P_Q.z_wait()
    P_Q.y_copy().start()
    WH.z_start()
    mask_of(1)
    M(0).relay()
    M(0).z_wait()
    M(0).y_copy().start()
    WI.y_copy().wait_recv()
    WI.z_start()
    WH.relay()
    WH.z_wait()
    WH.y_copy().start()
    M(1).z_start()
    for h in range(2, heads):
        mask_of(h)
    gate_save.start()
    P_Q.y_copy().wait_recv()
    P_Q.c_copy().start()
    x_copy().wait_recv()
    P_Q.c_copy().wait_recv()

    step = half // 2

    def project(r, carry):
        rows = pl.ds(pl.multiple_of(r * step, step), step)
        xb = x_v[rows, :]
        for j, dst in enumerate((q_v, k_v, v_v)):
            w = w_v[:, :, :, j].reshape(width, pairs * 128)
            acc = dot(xb, w)
            if j == 0:
                acc = acc + bqv[0:1, :]
            elif j == 2:
                acc = acc + bqv[1:2, :]
            out = acc.astype(BF)
            if j == 0:
                out = out * jnp.asarray(0.125, BF)
            for p in range(pairs):
                dst[p, rows, :] = out[:, p * 128:(p + 1) * 128]
        return carry

    lax.fori_loop(0, seq // step, project, 0)
    outs = [
        pltpu.make_async_copy(q_v, q_o, loc.at[6]),
        pltpu.make_async_copy(k_v, k_o, loc.at[1]),
        pltpu.make_async_copy(v_v, v_o, loc.at[2]),
        pltpu.make_async_copy(x_v, x_o, loc.at[3]),
        pltpu.make_async_copy(w_v, qkv_o, loc.at[4]),
    ]
    for cp in outs:
        cp.start()
    blk = seq // Z

    def attend(p, u):
        h = 2 * p + u
        sl = slice(64 * u, 64 * u + 64)

        def rows_of(n, carry):
            b = lax.rem((1 - t) * (Z // 2) + n, Z)
            if u == 1:
                @pl.when(n == Z // 2)
                def _():
                    a_copy(p).start()

            rows = pl.ds(pl.multiple_of(b * blk, blk), blk)
            s = dot_t(q_v[p, rows, sl], k_v[p, :, sl])
            s = s + m_v[h, b].reshape(blk, seq).astype(F32) + bias[...]
            top = jnp.max(s, axis=-1, keepdims=True)
            e = jnp.exp(s - top)
            total = jnp.sum(e, axis=-1, keepdims=True)
            o = dot(e.astype(BF), v_v[p, :, sl])
            a_v[p, rows, sl] = (o / total).astype(BF)
            lse_v[p, rows, u:u + 1] = top + jnp.log(total)
            return carry

        lax.fori_loop(0, Z, rows_of, 0, unroll=2)

    def with_0():
        M(1).relay()
        M(1).z_wait()
        M(1).y_copy().start()
        M(2).z_start()

    def with_1():
        M(3).z_start()

    def with_2():
        pass

    def with_3():
        WI.x_copy().wait_recv()
        WI.c_copy().start()

    def with_4():
        WH.x_copy().wait_recv()
        WH.c_copy().start()

    def with_5():
        WO.y_copy().wait_recv()
        WO.x_copy().start()

    def ahead_0():
        pass

    def ahead_1():
        WI.relay()
        WI.z_wait()
        WI.x_copy().start()
        WH.y_copy().wait_recv()
        WH.x_copy().start()
        M(2).relay()
        M(2).z_wait()
        M(2).y_copy().start()

    def ahead_2():
        M(3).relay()
        M(3).z_wait()
        M(3).y_copy().start()
        M(4).z_start()
        WO.z_start()

    def ahead_3():
        M(4).relay()
        M(4).z_wait()
        M(4).y_copy().start()
        M(5).z_start()

    def ahead_4():
        WO.relay()
        WO.z_wait()
        WO.y_copy().start()
        M(5).relay()
        M(5).z_wait()
        M(5).y_copy().start()

    def ahead_5():
        pass

    ahead = (ahead_0, ahead_1, ahead_2, ahead_3, ahead_4, ahead_5)
    beside = (with_0, with_1, with_2, with_3, with_4, with_5)

    def pair_step(p, carry):
        for u in range(2):
            h = 2 * p + u
            for n in range(pairs):
                pl.when(p == n)(ahead[2 * n + u])
            M(h).y_copy().wait_recv()
            M(h).c_copy().start()
            for n in range(pairs):
                pl.when(p == n)(beside[2 * n + u])
            M(h).c_copy().wait_recv()
            mask_save(h).start()
            attend(p, u)
        a_local(p).start()
        return carry

    lax.fori_loop(0, pairs, pair_step, 0)
    lse_out = pltpu.make_async_copy(lse_v, lse_o, loc.at[5])
    lse_out.start()
    WO.x_copy().wait_recv()
    WO.c_copy().start()
    for p in range(pairs):
        a_local(p).wait()
        a_copy(p).wait()
    b_copy().wait()
    for cp in late:
        cp.wait()
    for w in (WI, WH, WO):
        w.c_copy().wait_recv()

    quarter = m_v.shape[1:5]
    deep_w = width // (quarter[0 + 1] * quarter[2] * quarter[3])
    step = seq // 2
    flat = width

    def whole(ref, at):
        return ref[:, :, :, :, at].reshape(flat, -1)

    def slab(j, n):
        return m_v.at[j, pl.ds(0, deep_w), :, :, :, pl.ds(n * step, step)]

    def save(j, n):
        out = (ghid_o, gin_o)[n]
        return pltpu.make_async_copy(slab(j, n), out.at[:, :, :, :, pl.ds(pl.multiple_of(j * step, 128), step)], gs.at[j, n])

    def put(n):
        def one(j, value):
            m_v[j, 0:deep_w, :, :, :, n * step:(n + 1) * step] = value.reshape((deep_w,) + quarter[1:] + (step,))
            save(j, n).start()

        return one

    def ready():
        for h in range(heads):
            M(h).finish()
            mask_save(h).wait()

    outs_save = pltpu.make_async_copy(outs_v, outs_o, loc.at[0])
    per_t = bin_v.shape[2] // step

    def bin_of(j):
        return bin_v[j // per_t, :, pl.ds(pl.multiple_of(lax.rem(j, per_t) * step, 128), step)]

    for cp in outs + [lse_out, gate_save]:
        cp.wait()
    middle_math(attn_v, lambda rows: x_v[pl.ds(pl.multiple_of(t * half + rows.start, 128), rows.size), :],
                lambda: whole(out_w, slice(None)), lambda at: whole(in_w, at), lambda at: whole(hid_w, at),
                b_out, bin_of, b_hid, g1, c1, g2, c2, cot_v, length[0], t * half,
                outs_v, dz1_v, gout_v, dat_v, small_v, hat1_v, s1_v, h1b_v, ht_v, act_v, dg_v, z_v, hat2_v, zt_v,
                put(0), put(1), ready, outs_save.start)
    ends = [pltpu.make_async_copy(a, b, loc.at[1 + n]) for n, (a, b) in enumerate((
        (dz1_v, dz1_o), (gout_v, gout_o), (dat_v, dat_o), (small_v, small_o)))]
    for cp in ends:
        cp.start()
    x_copy().wait_send()
    P_Q.finish()
    for w in (WO, WI, WH):
        w.finish()
    for j in range(heads):
        for n in range(2):
            save(j, n).wait()
    outs_save.wait()
    for cp in ends:
        cp.wait()


def forward(deep, x, ml, nz, qkv, w_out_t, w_in, w_hid_t, b_in, cot, b_qv, length, vectors):
    half, width = x.shape
    seq = 2 * half
    heads, blk, _ = ml.shape
    pairs = heads // 2
    Z, Y, C = deep // 4, 2, 2
    n_out, n_in = w_out_t.shape[1], w_in.shape[1]
    r = w_in.shape[0]
    wide = 2 * n_in
    tall = (width // (Y * C * blk), Y, C, blk)
    rows = 6 * width // 128 + wide // 128
    rows += -rows % 8
    sd, vm = jax.ShapeDtypeStruct, pltpu.VMEM
    dma = pltpu.SemaphoreType.DMA
    out_shape = (
        sd((pairs, seq, 128), BF), sd((pairs, seq, 128), BF), sd((pairs, seq, 128), BF),
        sd((pairs, seq, 128), F32),
        sd((seq, width), BF),
        sd((heads, Z, Y, C, blk, seq), BF),
        sd((Z, Y, C) + qkv.shape, BF), sd((heads * blk, seq), F32),
        sd((half, width), BF), sd((half, width), F32), sd(tall + (wide,), BF), sd(tall + (wide,), BF),
        sd((width, width), BF), sd((half, width), BF), sd((rows, 128), F32),
    )
    pair = vm((pairs, seq, 128), BF)
    return pl.pallas_call(
        functools.partial(fwd_kernel, deep),
        out_shape=out_shape,
        in_specs=[ANY] * 9 + [VM, pl.BlockSpec(memory_space=pltpu.SMEM)] + [ANY] * 6,
        out_specs=[ANY] * len(out_shape),
        scratch_shapes=[
            vm((seq, width), BF),
            vm((Z, Y, C) + qkv.shape, BF),
            vm((heads, Z, Y, C, blk, seq), BF),
            pair, pair, pair, pair, vm((pairs, seq, 128), F32),
            vm((Z, Y, C, r, 2 * n_out), BF), vm((Z, Y, C, r, wide), BF), vm((Z, Y, C, r, wide), BF), vm((2, 1) + b_in.shape, F32),
            vm((half, width), BF), vm((1, seq), F32),
            vm((half, width), F32), vm((half, 128), F32), vm((half, width), BF), vm((width, half), BF), vm((half, wide), BF), vm((half, wide), F32),
            vm((half, width), F32), vm((half, width), BF), vm((width, half), BF),
            vm((half, width), BF), vm((half, width), F32), vm((width, width), BF), vm((half, width), BF), vm((half, width), F32), vm((rows, 128), F32), vm((8, width), F32),
            dma((24,)), dma((heads, 2)), dma((2,)), dma((2,)), dma((pairs,)), dma((pairs,)),
            *pass_sems(), *pass_sems(heads), *pass_sems(3),
        ],
        compiler_params=pltpu.CompilerParams(collective_id=1, has_side_effects=True, vmem_limit_bytes=62 << 20),
        name="forward_attention",
    )(x, ml.reshape(heads * blk, seq), nz.reshape(heads * blk, seq), qkv, w_out_t, w_in, w_hid_t, b_in, cot, b_qv, length, *vectors)


class Fold:
    def __init__(self, me, near_part, far_part, lc, bufs, sems, final, lx=None, early=False, cols=None):
        self.me, self.own, self.away, self.lc = me, near_part, far_part, lc
        self.ly, self.lz, self.lr = bufs
        self.s, self.r = sems
        self.final, self.lx, self.early, self.cols = final, lx, early, cols

    def base(self):
        return self.lc if self.lx is None else self.lx

    def c_copy(self):
        return rcopy(self.away, self.lc, self.s(0), self.r(0), self.me.over_c)

    def c_add(self):
        self.c_copy().wait_recv()

        def one(i, carry):
            for j in range(self.me.Y):
                self.lc[i, j] = self.lc[i, j] + self.own(i, j)
            return carry

        lax.fori_loop(0, self.me.Z, one, 0)

    def x_copy(self):
        me = self.me
        return rcopy(self.lc.at[:, :, :, self.cols(1 - me.t)], self.lx, self.s(1), self.r(1), me.over_t)

    def x_add(self):
        self.x_copy().wait_recv()
        at = self.cols(self.me.t)

        def one(i, carry):
            for j in range(self.me.Y):
                self.lx[i, j] = self.lx[i, j] + self.lc[i, j, :, at]
            return carry

        lax.fori_loop(0, self.me.Z, one, 0)

    def y_copy(self):
        me = self.me
        src = self.base().at[me.z, 1 - me.y] if self.early else self.base().at[:, 1 - me.y]
        return rcopy(src, self.ly, self.s(2), self.r(2), me.over_y)

    def y_add(self):
        self.y_copy().wait_recv()
        base, y = self.base(), self.me.y

        def one(i, carry):
            self.ly[i] = self.ly[i] + base[i, y]
            return carry

        lax.fori_loop(0, self.me.Z, one, 0)

    def along(self):
        return self.base() if self.early else self.ly

    def near(self):
        me = self.me
        return rcopy(self.along().at[me.z_near], self.lz.at[0], self.s(3), self.r(3), me.dev(z=me.z_near))

    def through(self, n):
        me = self.me
        place = self.along().at[me.z_far_inner if n == 0 else me.z_far_outer]
        return rcopy(place, self.lr.at[n], self.s(4 + n), self.r(4 + n), me.dev(z=me.z_near))

    def onward(self, n):
        me = self.me
        z = me.z_far_inner if n == 0 else me.z_far_outer
        return rcopy(self.along().at[z], self.lz.at[1], self.s(6 + n), self.r(6), me.dev(z=z))

    def z_start(self):
        @pl.when(self.me.outer == 1)
        def _():
            for n in range(2):
                self.through(n).start()

        self.near().start()

    def relay(self):
        me = self.me

        @pl.when(me.outer == 0)
        def _():
            for n in range(2):
                self.through(n).wait_recv()
                z = me.z_far_inner if n == 0 else me.z_far_outer
                self.along()[z] = self.along()[z] + self.lr[n]
                self.onward(n).start()

    def z_sum(self):
        self.near().wait_recv()
        self.onward(0).wait_recv()
        total = self.along()[self.me.z].astype(F32) + self.lz[0].astype(F32)
        return total + self.lz[1].astype(F32)

    def z_end(self):
        self.final(self.z_sum())

    def early_z_end(self):
        self.base()[self.me.z] = self.z_sum().astype(BF)
        self.y_copy().start()

    def early_y_end(self):
        self.y_copy().wait_recv()
        self.final(self.base()[self.me.z, self.me.y].astype(F32) + self.ly[...].astype(F32))

    def finish(self, skip_c=False):
        if not skip_c:
            self.c_copy().wait_send()
        if self.lx is not None:
            self.x_copy().wait_send()
        self.y_copy().wait_send()
        self.near().wait_send()

        @pl.when(self.me.outer == 1)
        def _():
            for n in range(2):
                self.through(n).wait_send()

        @pl.when(self.me.outer == 0)
        def _():
            for n in range(2):
                self.onward(n).wait_send()


def bwd_kernel(deep, dat, q_h, k_h, v_h, mask_h, lse_h, x_h, qkv_h, hid_h, in_h, out_h, dz1_h, sg_h, small_h, bias,
               dx_o, gqkv_o, ghid_o, gin_o, gout_o, gmask_o, small_o,
               q_v, k_v, v_v, do_v, lse_v, m_v, p_v, dq_v, dk_v, dv_v, acck, accv,
               lc_m, ly_m, lz_m, lr_m, lz_e, lr_e, gm_v,
               own_w, lc_hid, lx_hid, ly_hid, lz_hid, lr_hid, lc_in, lx_in, ly_in, lz_in, lr_in, lc_out, lx_out, ly_out, lz_out, lr_out,
               fin_hid, fin_in, fin_out,
               p_q, lc_q, ly_q, lz_q, lr_q, fin_q,
               x_v, w_v, sx_v, lx_x, dx_v, dz_v,
               s_v, sc_v, sy_v, sz_v, sx2_v,
               loc, msem, ds_, dr, wl, w_s, w_r, m_s, m_r, q_s, q_r, xs, xr, s1s, s1r, szs, szr):
    me = Place(deep)
    Z, y, c, z, t = me.Z, me.y, me.c, me.z, me.t
    pairs, seq, _ = q_v.shape
    heads = 2 * pairs
    half = seq // 2
    width = x_v.shape[1]
    zs = range(1, Z)
    rows_own = pl.ds(pl.multiple_of(t * half, 128), half)

    def dat_cols(p, who):
        return pl.ds(pl.multiple_of(who * (pairs * 128) + p * 128, 128), 128)

    def dat_local(p):
        return pltpu.make_async_copy(dat.at[:, dat_cols(p, t)], do_v.at[p, rows_own], loc.at[p])

    def dat_copy(p):
        return rcopy(dat.at[:, dat_cols(p, 1 - t)], do_v.at[p, rows_own], ds_.at[p], dr.at[p], me.over_t)

    loads = [pltpu.make_async_copy(a, b, loc.at[3 + n]) for n, (a, b) in enumerate((
        (q_h, q_v), (k_h, k_v), (v_h, v_v), (lse_h, lse_v), (x_h, x_v), (qkv_h, w_v), (dz1_h, dz_v), (small_h, s_v.at[pl.ds(0, small_h.shape[0])])))]

    def m_load(h, slot):
        return pltpu.make_async_copy(mask_h.at[h], m_v.at[slot], msem.at[slot])

    def sg_load(h):
        return pltpu.make_async_copy(sg_h.at[h], gm_v.at[h], loc.at[11 + h])

    def gm_save(h):
        return pltpu.make_async_copy(gm_v.at[h], gmask_o.at[h], loc.at[17 + h])

    def M(h, slot=None):
        early = isinstance(h, int) and h == 1

        def own(i, j):
            return p_v[slot, i, j, c]

        def final(total):
            sg_load(h).wait()
            gm_v[h] = total * gm_v[h]
            gm_save(h).start()

        away = None if slot is None else p_v.at[slot, :, :, 1 - c]
        return Fold(me, own, p_v.at[0, :, :, 1 - c] if away is None else away, lc_m.at[h],
                    (ly_m.at[h, 0], lz_e, lr_e) if early else (ly_m.at[h], lz_m.at[h], lr_m.at[h]),
                    (lambda n: m_s.at[h, n], lambda n: m_r.at[h, n]), final, early=early)

    def W(k, part, lc, lx, ly, lz, lr, fin, out, early):
        n = lx.shape[-1]

        def own(i, j):
            return own_w[i, j, :, 0:2 * n]

        def final(total):
            fin[...] = total
            pltpu.make_async_copy(fin, out, wl.at[3 + k]).start()

        fold = Fold(me, own, part.at[:, :, 1 - c], lc, (ly, lz, lr), (lambda i: w_s.at[k, i], lambda i: w_r.at[k, i]), final,
                    lx, early, lambda who: pl.ds(pl.multiple_of(who * n, 128), n))
        fold.own_load = lambda: pltpu.make_async_copy(part.at[:, :, c], own_w.at[:, :, :, pl.ds(0, 2 * n)], wl.at[k])
        fold.saved = lambda: pltpu.make_async_copy(fin, out, wl.at[3 + k])
        return fold

    WH = W(0, hid_h, lc_hid, lx_hid, ly_hid, lz_hid, lr_hid, fin_hid, ghid_o, False)
    WI = W(1, in_h, lc_in, lx_in, ly_in, lz_in, lr_in, fin_in, gin_o, True)
    WO = W(2, out_h, lc_out, lx_out, ly_out, lz_out, lr_out, fin_out, gout_o, False)

    def q_final(total):
        fin_q[...] = total
        pltpu.make_async_copy(fin_q, gqkv_o, loc.at[24]).start()

    Q = Fold(me, lambda i, j: p_q[i, j, c], p_q.at[:, :, 1 - c], lc_q, (ly_q, lz_q, lr_q),
             (lambda n: q_s.at[n], lambda n: q_r.at[n]), q_final)

    def x_copy():
        return rcopy(sx_v, lx_x, xs, xr, me.over_t)

    def s_c():
        return rcopy(s_v, sc_v, s1s.at[0], s1r.at[0], me.over_c)

    def s_y():
        return rcopy(sc_v, sy_v, s1s.at[1], s1r.at[1], me.over_y)

    def s_z(d):
        return rcopy(sy_v, sz_v.at[z], szs.at[d - 1], szr.at[d - 1], me.along_z(d))

    def s_z_in(d):
        return rcopy(sy_v, sz_v.at[me.source_z(d)], szs.at[d - 1], szr.at[d - 1], me.along_z(d))

    def s_x():
        return rcopy(s_v, sx2_v, s1s.at[2], s1r.at[2], me.over_t)

    m_load(0, 0).start()
    for cp in loads[:4]:
        cp.start()
    for p in range(pairs):
        dat_local(p).start()
    WH.own_load().start()
    for cp in loads[4:]:
        cp.start()
    me.greet()
    for p in range(pairs):
        dat_copy(p).start()
    for w in (WH, WI, WO):
        w.c_copy().start()
    for h in range(heads):
        sg_load(h).start()
    for cp in loads[:4]:
        cp.wait()

    blk = seq // Z
    shape4 = p_v.shape[2:]

    def attend(p, u, slot):
        sl = slice(64 * u, 64 * u + 64)
        acck[...] = jnp.zeros_like(acck)
        accv[...] = jnp.zeros_like(accv)

        def rows_of(n, carry):
            b = lax.rem(t * (Z // 2) + n, Z)
            if u == 0:
                @pl.when(n == Z // 2)
                def _():
                    dat_copy(p).wait_recv()

                @pl.when(jnp.logical_and(n == Z // 2, p == 0))
                def _():
                    WH.own_load().wait()
                    WH.c_add()
                    WI.own_load().start()
                    WH.x_copy().start()

                @pl.when(jnp.logical_and(n == Z // 2 + 1, p == 0))
                def _():
                    WI.own_load().wait()
                    WI.c_add()
                    WO.own_load().start()
                    WI.x_copy().start()

            rows = pl.ds(pl.multiple_of(b * blk, blk), blk)
            qb, dob = q_v[p, rows, sl], do_v[p, rows, sl]
            kk, vv = k_v[p, :, sl], v_v[p, :, sl]
            s = dot_t(qb, kk) + m_v[u, b].reshape(blk, seq).astype(F32) + bias[...]
            pr = jnp.exp(s - lse_v[p, rows, u:u + 1])
            dp = dot_t(dob, vv)
            tt = pr * dp
            delta = jnp.sum(tt, axis=-1, keepdims=True)
            dsb = (tt - pr * delta).astype(BF)
            p_v[slot, b] = dsb.reshape(shape4)
            dq_v[p, rows, sl] = (dot(dsb, kk) * 0.125).astype(BF)
            acck[...] += dot_0(dsb, qb)
            accv[...] += dot_0(pr.astype(BF), dob)
            return carry

        lax.fori_loop(0, Z, rows_of, 0, unroll=2)
        dk_v[p, :, sl] = acck[...].astype(BF)
        dv_v[p, :, sl] = accv[...].astype(BF)

    def after_0():
        M(0, 0).c_add()
        WO.own_load().wait()
        WO.c_add()
        WO.x_copy().start()
        M(0).y_copy().start()

    def after_1():
        M(1, 1).c_add()
        M(1).z_start()

    def after_2():
        M(2, 0).c_add()
        M(2).y_copy().start()
        M(1).relay()
        M(0).y_add()
        M(0).z_start()

    def after_3():
        M(3, 1).c_add()
        M(3).y_copy().start()
        WH.x_add()
        WH.y_copy().start()
        M(0).relay()

    def after_4():
        M(4, 0).c_add()
        M(4).y_copy().start()
        M(2).y_add()
        M(2).z_start()
        M(1).early_z_end()

    def after_5():
        M(5, 1).c_add()
        M(5).y_copy().start()
        M(2).relay()
        M(3).y_add()
        M(3).z_start()

    after = (after_0, after_1, after_2, after_3, after_4, after_5)

    def pair_step(p, carry):
        dat_local(p).wait()
        for u in range(2):
            h = 2 * p + u
            m_load(h, u).wait()
            if u == 0:
                m_load(h + 1, 1).start()
            else:
                @pl.when(p < pairs - 1)
                def _():
                    m_load(h + 1, 0).start()

            @pl.when(p > 0)
            def _():
                M(h - 2, u).c_copy().wait_send()

            attend(p, u, u)
            M(h, u).c_copy().start()
            for n in range(pairs):
                pl.when(p == n)(after[2 * n + u])
        return carry

    lax.fori_loop(0, pairs, pair_step, 0)
    for cp in loads[4:]:
        cp.wait()

    step = half // 2

    def d_cat(ref, rows):
        return jnp.concatenate([ref[p, rows, :] for p in range(pairs)], axis=1)

    def weight(j):
        return w_v[:, :, :, j].reshape(width, pairs * 128)

    def terms(rows):
        acc = dot_t(d_cat(dq_v, rows), weight(0))
        acc = acc + dot_t(d_cat(dk_v, rows), weight(1))
        return acc + dot_t(d_cat(dv_v, rows), weight(2))

    def theirs(r, carry):
        at = pl.ds(pl.multiple_of(r * step, step), step)
        rows = pl.ds(pl.multiple_of((1 - t) * half + r * step, step), step)
        sx_v[at, :] = terms(rows).astype(BF)
        return carry

    lax.fori_loop(0, 2, theirs, 0)
    x_copy().start()
    M(3).relay()
    WI.x_add()
    WI.z_start()
    M(0).z_end()
    WO.x_add()
    WO.y_copy().start()

    for j, ref in enumerate((dq_v, dk_v, dv_v)):
        g = dot_0(x_v[...], d_cat(ref, slice(None)))
        p_q[:, :, :, j] = g.astype(BF).reshape(p_q.shape[:3] + p_q.shape[4:])
    Q.c_copy().start()
    WI.relay()
    base = small_h.shape[0]
    for n, ref in enumerate((dq_v, dv_v)):
        for p in range(pairs):
            at = base + n * pairs + p
            s_v[at:at + 1, :] = jnp.sum(ref[p].astype(F32), axis=0, keepdims=True)
    for at in range(base + 2 * pairs, s_v.shape[0]):
        s_v[at:at + 1, :] = jnp.zeros((1, 128), F32)
    s_c().start()
    Q.c_add()
    Q.y_copy().start()

    s_c().wait_recv()
    sc_v[...] = sc_v[...] + s_v[...]
    s_y().start()
    WH.y_add()
    WH.z_start()
    M(2).z_end()
    M(4).y_add()
    M(4).z_start()
    WH.relay()
    WI.early_z_end()
    M(3).z_end()
    M(4).relay()
    M(5).y_add()
    M(5).z_start()

    def mine(r, carry):
        at = pl.ds(pl.multiple_of(r * step, step), step)
        rows = pl.ds(pl.multiple_of(t * half + r * step, step), step)
        dx_v[at, :] = terms(rows) + dz_v[at, :]
        return carry

    lax.fori_loop(0, 2, mine, 0)
    s_y().wait_recv()
    sy_v[...] = sy_v[...] + sc_v[...]
    sz_v[z] = sy_v[...]
    for d in zs:
        s_z(d).start()
    Q.y_add()
    Q.z_start()
    WH.z_end()
    M(5).relay()
    WO.y_add()
    WO.z_start()
    Q.relay()
    M(4).z_end()
    x_copy().wait_recv()
    dx_v[...] = dx_v[...] + lx_x[...].astype(F32)
    dx_save = pltpu.make_async_copy(dx_v, dx_o, loc.at[23])
    dx_save.start()
    WO.relay()
    for d in zs:
        s_z_in(d).wait_recv()
    s_c().wait_send()
    total = sz_v[0]
    for i in range(1, Z):
        total = total + sz_v[i]
    s_v[...] = total
    s_x().start()
    M(5).z_end()
    M(1).early_y_end()
    WI.early_y_end()
    Q.z_end()
    WO.z_end()
    s_x().wait_recv()
    low = sx2_v[...] + s_v[...]
    row = lax.broadcasted_iota(jnp.int32, low.shape, 0)
    s_y().wait_send()
    sc_v[...] = jnp.where(row < base, low, s_v[...])
    s_save = pltpu.make_async_copy(sc_v, small_o, loc.at[25])
    s_save.start()

    for p in range(pairs):
        dat_copy(p).wait_send()
    for w in (WH, WI, WO):
        w.finish()
        w.saved().wait()
    for h in range(heads):
        M(h).finish(h < heads - 2)
        gm_save(h).wait()
    Q.finish()
    for d in zs:
        s_z(d).wait_send()
    x_copy().wait_send()
    s_x().wait_send()
    dx_save.wait()
    pltpu.make_async_copy(fin_q, gqkv_o, loc.at[24]).wait()
    s_save.wait()


def backward(deep, dat, q, k, v, mask, lse, x, qkv, g_hid, g_in, g_out, dz1, sg, small, bias):
    pairs, seq, _ = q.shape
    half, width = dz1.shape
    heads, Z, Y, C, blk, _ = mask.shape
    r, n2 = g_in.shape[3], g_in.shape[4]
    n2o = g_out.shape[4]
    n, no = n2 // 2, n2o // 2
    base = small.shape[0]
    rows_s = base + 8
    sd = jax.ShapeDtypeStruct
    dma = pltpu.SemaphoreType.DMA
    vm = pltpu.VMEM
    out_shape = (
        sd((half, width), F32), sd(qkv.shape[3:], F32), sd((r, n), F32), sd((r, n), F32), sd((r, no), F32),
        sd((heads, blk, seq), F32), sd((rows_s, 128), F32),
    )
    pair = vm((pairs, seq, 128), BF)

    def chain(m, early):
        last = (Y, r, m) if early else (r, m)
        return [vm((Z, Y, r, 2 * m), BF), vm((Z, Y, r, m), BF), vm((r, m) if early else (Z, r, m), BF), vm((2,) + last, BF), vm((2,) + last, BF)]

    three, rq, nq = qkv.shape[3:]
    return pl.pallas_call(
        functools.partial(bwd_kernel, deep),
        out_shape=out_shape,
        in_specs=[ANY] * 14 + [VM],
        out_specs=[ANY] * len(out_shape),
        scratch_shapes=[
            pair, pair, pair, pair, vm((pairs, seq, 128), F32), vm((2, Z, Y, C, blk, seq), BF), vm((2, Z, Y, C, blk, seq), BF),
            pair, pair, pair, vm((seq, 64), F32), vm((seq, 64), F32),
            vm((heads, Z, Y, blk, seq), BF), vm((heads, Z, blk, seq), BF), vm((heads, 2, blk, seq), BF), vm((heads, 2, blk, seq), BF),
            vm((2, Y, blk, seq), BF), vm((2, Y, blk, seq), BF), vm((heads, blk, seq), F32),
            vm((Z, Y, r, n2), BF), *chain(n, False), *chain(n, True), *chain(no, False), vm((r, n), F32), vm((r, n), F32), vm((r, no), F32),
            vm((Z, Y, C, three, rq, nq), BF), vm((Z, Y, three, rq, nq), BF), vm((Z, three, rq, nq), BF),
            vm((2, three, rq, nq), BF), vm((2, three, rq, nq), BF), vm((three, rq, nq), F32),
            vm((seq, width), BF), vm((Z, Y, C, three, rq, nq), BF), vm((half, width), BF), vm((half, width), BF), vm((half, width), F32), vm((half, width), F32),
            vm((rows_s, 128), F32), vm((rows_s, 128), F32), vm((rows_s, 128), F32), vm((Z, rows_s, 128), F32), vm((rows_s, 128), F32),
            dma((26,)), dma((2,)), dma((pairs,)), dma((pairs,)),
            dma((6,)), dma((3, 8)), dma((3, 7)), dma((heads, 8)), dma((heads, 7)), dma((8,)), dma((7,)), dma, dma,
            dma((3,)), dma((3,)), dma((Z - 1,)), dma((Z - 1,)),
        ],
        compiler_params=pltpu.CompilerParams(collective_id=2, has_side_effects=True, vmem_limit_bytes=62 << 20),
        name="backward_attention",
    )(dat, q, k, v, mask, lse, x, qkv, g_hid, g_in, g_out, dz1, sg, small, bias)


NEG = -1e30
EPS = 1e-12


def layer_norm(value_rows, scale_vec, shift_vec):
    centre = value_rows - jnp.mean(value_rows, axis=-1, keepdims=True)
    spread = jnp.mean(centre * centre, axis=-1, keepdims=True)
    return centre * lax.rsqrt(spread + EPS) * scale_vec + shift_vec


def gelu_exact(value_rows):
    return jax.nn.gelu(value_rows, approximate=False)


def matmul(left, right):
    return jnp.dot(left, right, preferred_element_type=jnp.float32)


def times_transposed(left, right):
    return lax.dot_general(
        left, right, (((1,), (1,)), ((), ())), preferred_element_type=jnp.float32
    )


def over_rows(left, right):
    return lax.dot_general(
        left, right, (((0,), (0,)), ((), ())), preferred_element_type=jnp.float32
    )


def plain_body(
    inputs,
    lengths,
    w_qkv,
    b_qv,
    w_out,
    b_out,
    ln1_gain,
    ln1_bias,
    w_in,
    b_in,
    w_hid,
    b_hid,
    ln2_gain,
    ln2_bias,
    mask_logits,
    noise,
    cotangent,
):
    seq_count, half_rows, width = inputs.shape
    slot_len = half_rows * lax.axis_size("tensor")
    tensor_rank = lax.axis_index("tensor")
    head_count = mask_logits.shape[0]
    head_dim = w_qkv.shape[2] // head_count
    scale = head_dim ** (-0.5)
    token_count = seq_count * slot_len
    mixed_logits = mask_logits + noise
    local_mask = jax.nn.log_sigmoid(mixed_logits).astype(jnp.bfloat16)
    full_qkv, full_out, full_in, full_hid, full_mask = (
        lax.all_gather(w_qkv, "dp", axis=1, tiled=True),
        lax.all_gather(w_out, "dp", axis=1, tiled=True),
        lax.all_gather(w_in, "dp", axis=0, tiled=True),
        lax.all_gather(w_hid, "dp", axis=1, tiled=True),
        lax.all_gather(local_mask, "dp", axis=1, tiled=True),
    )
    key_valid = jnp.arange(slot_len, dtype=jnp.int32)[None, :] < lengths[:, None]
    own_rows = tensor_rank * half_rows + jnp.arange(half_rows, dtype=jnp.int32)
    row_valid = (own_rows[None, :] < lengths[:, None]).astype(jnp.float32)
    gathered = lax.all_gather(inputs, "tensor", axis=1, tiled=True)
    flat_rows = gathered.reshape(token_count, width)
    query_rows = (matmul(flat_rows, full_qkv[0]) + b_qv[0]).astype(jnp.bfloat16)
    key_rows = matmul(flat_rows, full_qkv[1]).astype(jnp.bfloat16)
    value_rows = (matmul(flat_rows, full_qkv[2]) + b_qv[1]).astype(jnp.bfloat16)

    def split_heads(matrix):
        return matrix.reshape(seq_count, slot_len, head_count, head_dim).transpose(0, 2, 1, 3)

    def join_heads(stacked):
        return stacked.transpose(0, 2, 1, 3).reshape(token_count, head_count * head_dim)

    def masked_scores(query_h, keys_h, mask_h, valid_keys):
        score_matrix = (
            jnp.einsum("qd,kd->qk", query_h, keys_h, preferred_element_type=jnp.float32) * scale
        )
        score_matrix = score_matrix + mask_h.astype(jnp.float32)
        return jnp.where(valid_keys[None, :], score_matrix, NEG)

    def attend_sequence(operands):
        query_s, keys_s, values_s, valid_keys = operands

        def attend_head(head_ops):
            query_h, keys_h, values_h, mask_h = head_ops
            score_matrix = masked_scores(query_h, keys_h, mask_h, valid_keys)
            top_score = jnp.max(score_matrix, axis=-1, keepdims=True)
            expo = jnp.exp(score_matrix - top_score)
            row_total = jnp.sum(expo, axis=-1, keepdims=True)
            attention_probabilities = (expo / row_total).astype(jnp.bfloat16)
            result = jnp.einsum(
                "qk,kd->qd", attention_probabilities, values_h, preferred_element_type=jnp.float32
            )
            return (result.astype(jnp.bfloat16), (top_score + jnp.log(row_total))[:, 0])

        return lax.map(attend_head, (query_s, keys_s, values_s, full_mask))

    head_out, log_total = lax.map(
        attend_sequence,
        (split_heads(query_rows), split_heads(key_rows), split_heads(value_rows), key_valid),
    )
    attn = join_heads(head_out)
    attn_terms = matmul(attn, full_out).reshape(seq_count, slot_len, width)
    attn_part = lax.psum_scatter(attn_terms, "tensor", scatter_dimension=1, tiled=True)
    first_sum = inputs.astype(jnp.float32) + attn_part + b_out
    hidden_one = layer_norm(first_sum, ln1_gain, ln1_bias)
    hidden_rows = lax.all_gather(
        hidden_one.astype(jnp.bfloat16), "tensor", axis=1, tiled=True
    ).reshape(token_count, width)
    pre_act = matmul(hidden_rows, full_in) + b_in
    activated = gelu_exact(pre_act).astype(jnp.bfloat16)
    ffn_terms = matmul(activated, full_hid).reshape(seq_count, slot_len, width)
    ffn_part = lax.psum_scatter(ffn_terms, "tensor", scatter_dimension=1, tiled=True)
    second_sum = hidden_one + ffn_part + b_hid
    outputs = layer_norm(second_sum, ln2_gain, ln2_bias).astype(jnp.bfloat16)
    back_qkv, back_out, back_in, back_hid, back_mask = (
        lax.all_gather(w_qkv, "dp", axis=1, tiled=True),
        lax.all_gather(w_out, "dp", axis=1, tiled=True),
        lax.all_gather(w_in, "dp", axis=0, tiled=True),
        lax.all_gather(w_hid, "dp", axis=1, tiled=True),
        lax.all_gather(local_mask, "dp", axis=1, tiled=True),
    )
    grad_output = cotangent * row_valid[:, :, None]
    _, pull_second = jax.vjp(layer_norm, second_sum, ln2_gain, ln2_bias)
    grad_second, ln2_gain_part, ln2_bias_part = pull_second(grad_output)
    b_hid_part = jnp.sum(grad_second, axis=(0, 1))
    second_rows = lax.all_gather(
        grad_second.astype(jnp.bfloat16), "tensor", axis=1, tiled=True
    ).reshape(token_count, width)
    w_hid_grad = over_rows(activated, second_rows)
    grad_act = times_transposed(second_rows, back_hid)
    _, pull_gelu = jax.vjp(gelu_exact, pre_act)
    grad_pre = pull_gelu(grad_act)[0].astype(jnp.bfloat16)
    b_in_part = jnp.sum(grad_pre.astype(jnp.float32), axis=0)
    w_in_grad = over_rows(hidden_rows, grad_pre)
    hidden_terms = times_transposed(grad_pre, back_in).reshape(seq_count, slot_len, width)
    grad_hidden = grad_second + lax.psum_scatter(
        hidden_terms, "tensor", scatter_dimension=1, tiled=True
    )
    _, pull_first = jax.vjp(layer_norm, first_sum, ln1_gain, ln1_bias)
    grad_first, ln1_gain_part, ln1_bias_part = pull_first(grad_hidden)
    b_out_part = jnp.sum(grad_first, axis=(0, 1))
    first_rows = lax.all_gather(
        grad_first.astype(jnp.bfloat16), "tensor", axis=1, tiled=True
    ).reshape(token_count, width)
    w_out_grad = over_rows(attn, first_rows)
    grad_attn = times_transposed(first_rows, back_out).astype(jnp.bfloat16)

    def sequence_back(mask_acc, operands):
        query_s, keys_s, values_s, grad_s, total_s, valid_keys = operands

        def head_back(head_ops):
            query_h, keys_h, values_h, mask_h, grad_h, total_h = head_ops
            score_matrix = masked_scores(query_h, keys_h, mask_h, valid_keys)
            attention_probabilities = jnp.exp(score_matrix - total_h[:, None])
            grad_probs = jnp.einsum(
                "qd,kd->qk", grad_h, values_h, preferred_element_type=jnp.float32
            )
            centre = jnp.sum(attention_probabilities * grad_probs, axis=-1, keepdims=True)
            grad_scores = (attention_probabilities * (grad_probs - centre)).astype(jnp.bfloat16)
            grad_q = (
                jnp.einsum("qk,kd->qd", grad_scores, keys_h, preferred_element_type=jnp.float32)
                * scale
            ).astype(jnp.bfloat16)
            grad_k = (
                jnp.einsum("qk,qd->kd", grad_scores, query_h, preferred_element_type=jnp.float32)
                * scale
            ).astype(jnp.bfloat16)
            grad_v = jnp.einsum(
                "qk,qd->kd",
                attention_probabilities.astype(jnp.bfloat16),
                grad_h,
                preferred_element_type=jnp.float32,
            ).astype(jnp.bfloat16)
            return (grad_q, grad_k, grad_v, grad_scores)

        grad_q, grad_k, grad_v, grad_sc = lax.map(
            head_back, (query_s, keys_s, values_s, back_mask, grad_s, total_s)
        )
        return (mask_acc + grad_sc.astype(jnp.float32), (grad_q, grad_k, grad_v))

    mask_zero = jnp.zeros(back_mask.shape, jnp.float32)
    mask_grad, (heads_q, heads_k, heads_v) = lax.scan(
        sequence_back,
        mask_zero,
        (
            split_heads(query_rows),
            split_heads(key_rows),
            split_heads(value_rows),
            split_heads(grad_attn),
            log_total,
            key_valid,
        ),
    )
    query_grad = join_heads(heads_q)
    keys_grad = join_heads(heads_k)
    values_grad = join_heads(heads_v)
    b_qv_part = jnp.stack(
        [
            jnp.sum(query_grad.astype(jnp.float32), axis=0),
            jnp.sum(values_grad.astype(jnp.float32), axis=0),
        ]
    )
    w_qkv_grad = jnp.stack(
        [
            over_rows(flat_rows, query_grad),
            over_rows(flat_rows, keys_grad),
            over_rows(flat_rows, values_grad),
        ]
    )
    input_terms = (
        times_transposed(query_grad, back_qkv[0])
        + times_transposed(keys_grad, back_qkv[1])
        + times_transposed(values_grad, back_qkv[2])
    ).reshape(seq_count, slot_len, width)
    input_grad = grad_first + lax.psum_scatter(
        input_terms.astype(jnp.bfloat16), "tensor", scatter_dimension=1, tiled=True
    ).astype(jnp.float32)
    qkv_total, out_total, in_total, hid_total, mask_total = (
        lax.psum_scatter(w_qkv_grad, "dp", scatter_dimension=1, tiled=True),
        lax.psum_scatter(w_out_grad, "dp", scatter_dimension=1, tiled=True),
        lax.psum_scatter(w_in_grad, "dp", scatter_dimension=0, tiled=True),
        lax.psum_scatter(w_hid_grad, "dp", scatter_dimension=1, tiled=True),
        lax.psum_scatter(mask_grad, "dp", scatter_dimension=1, tiled=True),
    )
    mask_logit_grad = mask_total * jax.nn.sigmoid(-mixed_logits)
    ln1_gain_total, ln1_bias_total, ln2_gain_total, ln2_bias_total, b_out_total, b_hid_total = (
        lax.psum(
            (ln1_gain_part, ln1_bias_part, ln2_gain_part, ln2_bias_part, b_out_part, b_hid_part),
            ("dp", "tensor"),
        )
    )
    b_qv_total, b_in_total = lax.psum((b_qv_part, b_in_part), "dp")
    return (
        outputs,
        input_grad,
        qkv_total,
        b_qv_total,
        out_total,
        b_out_total,
        ln1_gain_total,
        ln1_bias_total,
        in_total,
        b_in_total,
        hid_total,
        b_hid_total,
        ln2_gain_total,
        ln2_bias_total,
        mask_logit_grad,
    )


def last_kernel(place, total, *refs):
    n = (len(refs) - 10) // 3
    ins, rest = refs[:n], refs[n:]
    (bqv_o, bin_o), vecs, outs = rest[:2], rest[2:8], rest[8:8 + n]
    held, tot_v, sems = rest[8 + n:8 + 2 * n], rest[8 + 2 * n], rest[9 + 2 * n]
    first = pltpu.make_async_copy(total, tot_v, sems.at[n])
    first.start()
    loads = [pltpu.make_async_copy(a, b, sems.at[i]) for i, (a, b) in enumerate(zip(ins, held))]
    saves = [pltpu.make_async_copy(a, b, sems.at[i]) for i, (a, b) in enumerate(zip(held, outs))]
    for cp in loads:
        cp.start()
    for a, b in zip(loads, saves):
        a.wait()
        b.start()
    first.wait()
    t = place[0]
    per = vecs[0].shape[0] // 128
    for k, ref in enumerate(vecs):
        for i in range(per):
            ref[pl.ds(i * 128, 128)] = tot_v[k * per + i, :]
    m = bin_o.shape[0] // 128
    for i in range(m):
        bin_o[pl.ds(i * 128, 128)] = tot_v[6 * per + t * m + i, :]
    base = total.shape[0] - 8
    nq = bqv_o.shape[1] // 128
    for j in range(2):
        for i in range(nq):
            bqv_o[j:j + 1, i * 128:(i + 1) * 128] = tot_v[base + j * nq + i:base + j * nq + i + 1, :]
    for cp in saves:
        cp.wait()


def last(t, total, arrays, width, n_bin, bqv_shape):
    sd, vm = jax.ShapeDtypeStruct, pltpu.VMEM
    n = len(arrays)
    return pl.pallas_call(
        last_kernel,
        out_shape=(sd(bqv_shape, F32), sd((n_bin,), F32)) + (sd((width,), F32),) * 6 + tuple(sd(a.shape, a.dtype) for a in arrays),
        in_specs=[pl.BlockSpec(memory_space=pltpu.SMEM)] + [ANY] * (n + 1),
        out_specs=[VM] * 8 + [ANY] * n,
        scratch_shapes=[vm(a.shape, a.dtype) for a in arrays] + [vm(total.shape, F32), pltpu.SemaphoreType.DMA((n + 1,))],
        compiler_params=pltpu.CompilerParams(vmem_limit_bytes=60 << 20),
        name="hand_over",
    )(t, total, *arrays)


def body(
    inputs, lengths, w_qkv, b_qv, w_out, b_out, ln1_gain, ln1_bias, w_in, b_in, w_hid, b_hid,
    ln2_gain, ln2_bias, mask_logits, noise, cotangent,
):
    deep = lax.axis_size("dp")
    x = inputs[0]
    half, width = x.shape
    seq = 2 * half
    bias = jnp.where(jnp.arange(seq, dtype=jnp.int32) < lengths[0], 0.0, NEG).astype(F32).reshape(1, seq)
    vectors = (b_out, b_hid, ln1_gain, ln1_bias, ln2_gain, ln2_bias)
    q, k, v, lse, x_all, mask_all, qkv_all, gate, outputs, dz1, g_hid, g_in, g_out, dattn, small = forward(
        deep, x, mask_logits, noise, w_qkv, w_out.T, w_in, w_hid.T, b_in, cotangent[0], b_qv, lengths, vectors)
    place = (deep // 4, 2, 2, w_in.shape[0])
    dx, gqkv, ghid, gin, gout, gmask, total = backward(
        deep, dattn, q, k, v, mask_all, lse, x_all, qkv_all,
        g_hid.reshape(place + (-1,)), g_in.reshape(place + (-1,)), g_out.reshape(place + (-1,)), dz1, gate.reshape(mask_logits.shape), small, bias)
    t = lax.axis_index("tensor").astype(jnp.int32).reshape(1)
    g_bqv, g_bin, v0, v1, v2, v3, v4, v5, outputs, dx, gqkv, gout, gin, ghid, gmask = last(
        t, total, (outputs, dx, gqkv, gout, gin, ghid, gmask), width, b_in.shape[0], b_qv.shape)
    return (outputs[None], dx[None], gqkv, g_bqv, gout.T, v4, v0, v1, gin, g_bin, ghid.T, v5, v2, v3, gmask)


def solution(mesh):
    placed = (
        P("dp", "tensor", None),
        P("dp"),
        P(None, "dp", "tensor"),
        P(None, "tensor"),
        P("tensor", "dp"),
        P(),
        P(),
        P(),
        P("dp", "tensor"),
        P("tensor"),
        P("tensor", "dp"),
        P(),
        P(),
        P(),
        P("tensor", "dp", None),
        P("tensor", "dp", None),
        P("dp", "tensor", None),
    )

    def run(*args):
        w_rows, m_rows = args[8].shape[0], args[14].shape[1]
        tiled = w_rows % 16 == 0 and m_rows % 16 == 0 and args[0].shape[0] == 1 and mesh.shape["dp"] == 16
        return (body if tiled else plain_body)(*args)

    return jax.shard_map(
        run,
        mesh=mesh,
        in_specs=placed,
        out_specs=(
            P("dp", "tensor", None),
            P("dp", "tensor", None),
            P(None, "dp", "tensor"),
            P(None, "tensor"),
            P("tensor", "dp"),
            P(),
            P(),
            P(),
            P("dp", "tensor"),
            P("tensor"),
            P("tensor", "dp"),
            P(),
            P(),
            P(),
            P("tensor", "dp", None),
        ),
        check_vma=False,
    )
```
